128 devices in a mesh: shard: 16 (over z, x), tensor: 8 (over y, core).
Axes of the slice: x: 4, y: 4, z: 4, core: 2. Of those that a mesh axis runs over, the one named last changes fastest.
Arguments:
- gradient: bfloat16 [768, 3072], P('shard', 'tensor'), may hold values from -12 to 12
- moment_one: float32 [768, 3072], P('shard', 'tensor'), may hold values from -6 to 6
- moment_two: float32 [768, 3072], P('shard', 'tensor'), may hold values from 0.5 to 8
- stat_left: float32 [768, 768], P('shard'), may hold values from -1 to 3, as said below
- stat_right: float32 [3072, 3072], P('shard', 'tensor'), may hold values from -1 to 3, as said below
- basis_left: float32 [768, 768], P('shard'), may hold values from -3 to 25, as said below
- basis_right: float32 [3072, 3072], P('shard', 'tensor'), may hold values from -3 to 47, as said below
Outputs:
- update: bfloat16 [768, 3072], P('shard', 'tensor')
- new_moment_one: float32 [768, 3072], P('shard', 'tensor')
- new_moment_two: float32 [768, 3072], P('shard', 'tensor')
- new_stat_left: float32 [768, 768], P('shard')
- new_stat_right: float32 [3072, 3072], P('shard', 'tensor')
- new_basis_left: float32 [768, 768], P('shard')
- new_basis_right: float32 [3072, 3072], P('shard', 'tensor')
The draws below stay inside these ranges and needn't reach their ends.
Inputs may be any that keep to these rules, and one draw needn't show every extreme that they name: `stat_left`: symmetric and positive definite. `stat_right`: symmetric and positive definite. `basis_left`: full rank. `basis_right`: full rank.
All inputs are finite; a program needn't handle non-finite values.
Results may differ from the reference program's by a relative error of at most 0.011.
Values may be sent and summed in bfloat16 or wider, within the bound.
A program may use at most 64 MiB of HBM per device.

```python
import math
import jax
import jax.numpy as jnp
from jax import lax

D = 768
FF = 3072
NS_STEPS = 2


def statistic_matrix(key, matrix_order):
    level_key, noise_key = jax.random.split(key)
    levels = jnp.exp(jax.random.uniform(level_key, (matrix_order,), jnp.float32, math.log(0.25), math.log(2.0)))
    noise_field = jnp.clip(jax.random.normal(noise_key, (matrix_order, matrix_order), jnp.float32), -4.0, 4.0)
    scaled = noise_field * (0.1 / math.sqrt(matrix_order))
    identity = jnp.eye(matrix_order, dtype=jnp.float32)
    return (scaled + scaled.T) * 0.70710678 + identity * levels[None, :]


def basis_matrix(key, matrix_order):
    noise_field = jnp.clip(jax.random.normal(key, (matrix_order, matrix_order), jnp.float32), -4.0, 4.0)
    identity = jnp.eye(matrix_order, dtype=jnp.float32)
    return identity * (0.8 * math.sqrt(matrix_order)) + 0.6 * noise_field


def draw_stat_left(key, part):
    return statistic_matrix(jax.random.fold_in(key, 11), D)


def draw_stat_right(key, part):
    return statistic_matrix(jax.random.fold_in(key, 12), FF)


def draw_basis_left(key, part):
    return basis_matrix(jax.random.fold_in(key, 13), D)


def draw_basis_right(key, part):
    return basis_matrix(jax.random.fold_in(key, 14), FF)


def raised(array, own_key, source, target, blocks, factor):
    owner, partner = [(jnp.arange(array.shape[position]) // (array.shape[position] // blocks)).reshape([-1 if axis == position else 1 for axis in range(array.ndim)]) for position in (source, target)]
    chosen = jax.random.permutation(own_key, blocks)[partner]
    strong = (owner == chosen) | (owner == (partner + blocks // 2) % blocks)
    return jnp.where(strong, factor * array, array)


def level_of(stream_key, shape, cuts, smallest, top_value):
    loudness, own = 1.0, jax.random.fold_in(stream_key, 6)
    for dim, parts in cuts:
        draws = jnp.exp(jax.random.uniform(jax.random.fold_in(own, dim), (parts,), jnp.float32, smallest / len(cuts), top_value / len(cuts)))
        loudness = loudness * jnp.repeat(draws, shape[dim] // parts).reshape([-1 if axis == dim else 1 for axis in range(len(shape))])
    return loudness


def noise(own_key, shape, scale, most, pieces=(), kind=jnp.bfloat16):
    result = scale * jax.random.normal(own_key, shape, jnp.float32)
    if pieces:
        result = result * level_of(own_key, shape, pieces, -0.22, 0.18)
    return jnp.clip(result, -most, most).astype(kind)


def gaussian_with(own_key, extent, width, most, cuts, heavy, held_as=jnp.bfloat16):
    entries = width * jax.random.normal(own_key, extent, jnp.float32)
    if cuts:
        entries = entries * level_of(own_key, extent, cuts, -0.22, 0.18)
    return jnp.clip(raised(entries, jax.random.fold_in(own_key, 3), *heavy), -most, most).astype(held_as)


def setup_inputs(seed: int = 0) -> dict:
    keys = jax.random.split(jax.random.key(seed), 8)
    gradient = gaussian_with(keys[0], (D, FF), 2.0, 12.0, ((0, 16), (1, 8)), (0, 1, 16, 2.0))
    moment_one = noise(keys[1], (D, FF), 1.0, 6.0, ((0, 16), (1, 8)), jnp.float32)
    moment_two = jnp.clip(jnp.exp(math.log(8.0) - 2.7725887 * jax.random.uniform(keys[2], (D, FF), jnp.float32) ** level_of(keys[2], (D, FF), ((0, 16), (1, 8)), -0.2, 0.2)), 0.5, 8.0)
    stat_left = draw_stat_left(jax.random.fold_in(keys[7], 71), 0)
    stat_right = draw_stat_right(jax.random.fold_in(keys[7], 71), 0)
    basis_left = draw_basis_left(jax.random.fold_in(keys[7], 71), 0)
    basis_right = draw_basis_right(jax.random.fold_in(keys[7], 71), 0)
    return dict(gradient=gradient, moment_one=moment_one, moment_two=moment_two, stat_left=stat_left, stat_right=stat_right, basis_left=basis_left, basis_right=basis_right)


beta_one = 0.95
beta_two = 0.95
beta_stat = 0.95
correction = 1.0 - 0.95 ** 10
adam_eps = 1e-08
highest = lax.Precision.HIGHEST

def blend_stat(previous, product, divisor):
    return beta_stat * previous + (1.0 - beta_stat) * (product / divisor)

def adam_moments(rotated, moment_one, moment_two):
    first_moment = beta_one * moment_one + (1.0 - beta_one) * rotated
    second_moment = beta_two * moment_two + (1.0 - beta_two) * (rotated * rotated)
    direction = (first_moment / correction / (jnp.sqrt(second_moment / correction) + adam_eps)).astype(jnp.bfloat16)
    return (first_moment, second_moment, direction)

def reference(gradient, moment_one, moment_two, stat_left, stat_right, basis_left, basis_right):
    left_q = basis_left / math.sqrt(D)
    right_q = basis_right / math.sqrt(FF)
    left_qb = left_q.astype(jnp.bfloat16)
    right_qb = right_q.astype(jnp.bfloat16)
    new_stat_left = blend_stat(stat_left, jnp.dot(gradient, gradient.T, preferred_element_type=jnp.float32), FF)
    new_stat_right = blend_stat(stat_right, jnp.dot(gradient.T, gradient, preferred_element_type=jnp.float32), D)
    half_rotated = jnp.dot(left_qb.T, gradient, preferred_element_type=jnp.float32).astype(jnp.bfloat16)
    rotated = jnp.dot(half_rotated, right_qb, preferred_element_type=jnp.float32)
    new_moment_one, new_moment_two, direction = adam_moments(rotated, moment_one, moment_two)
    back_half = jnp.dot(left_qb, direction, preferred_element_type=jnp.float32).astype(jnp.bfloat16)
    update = jnp.dot(back_half, right_qb.T, preferred_element_type=jnp.float32).astype(jnp.bfloat16)
    power_left = jnp.dot(new_stat_left, left_q, precision=highest, preferred_element_type=jnp.float32)
    iterate_left = power_left * (math.sqrt(D) / (4.0 * jnp.sqrt(jnp.sum(power_left * power_left))))
    for iteration in range(NS_STEPS):
        gram_left = jnp.dot(iterate_left.T, iterate_left, precision=highest, preferred_element_type=jnp.float32)
        iterate_left = 1.5 * iterate_left - 0.5 * jnp.dot(iterate_left, gram_left, precision=highest, preferred_element_type=jnp.float32)
    power_right = jnp.dot(new_stat_right, right_q, precision=highest, preferred_element_type=jnp.float32)
    iterate_right = power_right * (math.sqrt(FF) / (4.0 * jnp.sqrt(jnp.sum(power_right * power_right))))
    identity = jnp.eye(FF, dtype=jnp.float32)
    for iteration in range(NS_STEPS):
        rounded_iterate = iterate_right.astype(jnp.bfloat16)
        gram_right = jnp.dot(rounded_iterate.T, rounded_iterate, preferred_element_type=jnp.float32)
        mixing = (1.5 * identity - 0.5 * gram_right).astype(jnp.bfloat16)
        iterate_right = jnp.dot(rounded_iterate, mixing, preferred_element_type=jnp.float32)
    return (update, new_moment_one, new_moment_two, new_stat_left, new_stat_right, iterate_left * math.sqrt(D), iterate_right * math.sqrt(FF))
```

```python
import functools
import math

import jax
import jax.numpy as jnp
from jax import lax
from jax.experimental import pallas as pl
from jax.experimental.pallas import tpu as pltpu
from jax.sharding import PartitionSpec as P

D = 768
FF = 3072
BF = jnp.bfloat16
F32 = jnp.float32
MESH = pl.DeviceIdType.MESH

beta = 0.95
correction = 1.0 - 0.95**10
adam_eps = 1e-08


class Move:
    def __init__(self, copy, landing):
        self.copy, self.landing = copy, landing

    def recv(self):
        self.landing.wait_recv()


class Net:
    def __init__(self, send_sem, recv_sem):
        self.send_sem, self.recv_sem = send_sem, recv_sem
        self.count = 0
        self.sent = []
        s, t = lax.axis_index("shard"), lax.axis_index("tensor")
        self.s, self.t = s, t
        self.z, self.x = s // 4, s % 4
        self.y, self.c = t // 2, t % 2

    def nbr(self, d):
        s, t = self.s, self.t
        z, x, y, c = self.z, self.x, self.y, self.c
        if d == "c":
            return (s, y * 2 + 1 - c)
        step = 1 if d[0] == "+" else 3
        if d[1] == "x":
            return (z * 4 + (x + step) % 4, t)
        if d[1] == "z":
            return (((z + step) % 4) * 4 + x, t)
        return (s, ((y + step) % 4) * 2 + c)

    def barrier(self, dirs):
        sem = pltpu.get_barrier_semaphore()
        for d in dirs:
            pl.semaphore_signal(sem, inc=1, device_id=self.nbr(d), device_id_type=MESH)
        pl.semaphore_wait(sem, len(dirs))

    def send(self, src, dst, landing, d):
        k = self.count
        self.count += 1
        mk = lambda a, b: pltpu.make_async_remote_copy(
            src_ref=a,
            dst_ref=b,
            send_sem=self.send_sem.at[k],
            recv_sem=self.recv_sem.at[k],
            device_id=self.nbr(d),
            device_id_type=MESH,
        )
        copy = mk(src, dst)
        copy.start()
        self.sent.append(copy)
        return Move(copy, mk(landing, landing))

    def drain(self):
        for copy in self.sent:
            copy.wait_send()
        self.sent = []


def cuts(rows):
    if rows % 64 == 0:
        q = rows // 4
        return ((0, q, 2 * q), (2 * q, 3 * q, 4 * q))
    if rows == 48:
        return ((0, 16, 32), (32, 48, 48))
    return ((0, rows, rows), None)


class ShardGather:
    def __init__(self, net, src, buf):
        self.net, self.src, self.buf = net, src, buf
        self.flows = [(i, f) for i, f in enumerate(cuts(src.shape[0])) if f is not None]
        self.m = {}

    def view(self, blk, lo, hi):
        n = self.net
        return self.buf.at[(n.z + blk[0]) % 4, (n.x + blk[1]) % 4, pl.ds(lo, hi - lo), :]

    def axes(self, i):
        return ("x", "z") if i == 0 else ("z", "x")

    def rel(self, i, first, second):
        return (second, first) if i == 0 else (first, second)

    def go(self, i, stage, sgn, first, second, lo, hi, key, own=False):
        if hi == lo:
            return
        axis = self.axes(i)[stage]
        d = ("+" if sgn > 0 else "-") + axis
        blk = self.rel(i, first, second)
        lf, ls = (first - sgn, second) if stage == 0 else (first, second - sgn)
        src = self.src.at[pl.ds(lo, hi - lo), :] if own else self.view(blk, lo, hi)
        self.m[key] = self.net.send(src, self.view(blk, lo, hi), self.view(self.rel(i, lf, ls), lo, hi), d)

    def wait(self, *key):
        if key in self.m:
            self.m[key].recv()

    def start(self):
        n = self.net
        for i, (lo, mid, hi) in self.flows:
            for sgn in (1, -1):
                self.go(i, 0, sgn, 0, 0, lo, hi, (i, "a", sgn), own=True)
        for i, (lo, mid, hi) in self.flows:
            for sgn in (1, -1):
                self.go(i, 1, sgn, 0, 0, lo, hi, (i, "b", 0, sgn), own=True)

    def local(self, sem):
        n = self.net
        self.mine = pltpu.make_async_copy(self.src, self.buf.at[n.z, n.x], sem)
        self.mine.start()

    def second(self, i, first, lo, hi):
        for sgn in (1, -1):
            self.go(i, 1, sgn, first, 0, lo, hi, (i, "b", first, sgn))

    def relay(self, i, first, lo, mid, hi):
        for sgn in (1, -1):
            self.wait(i, "b", first, sgn)
            a, b = (lo, mid) if sgn > 0 else (mid, hi)
            self.go(i, 1, sgn, first, -sgn, a, b, (i, "bb", first, sgn))

    def step1(self):
        for i, (lo, mid, hi) in self.flows:
            for sgn in (1, -1):
                self.wait(i, "a", sgn)
                a, b = (lo, mid) if sgn > 0 else (mid, hi)
                self.go(i, 0, sgn, -sgn, 0, a, b, (i, "aa", sgn))
                self.second(i, -sgn, lo, hi)

    def step2(self):
        for i, (lo, mid, hi) in self.flows:
            self.relay(i, 0, lo, mid, hi)
        for i, (lo, mid, hi) in self.flows:
            self.wait(i, "aa", 1)
            self.wait(i, "aa", -1)
            self.second(i, 2, lo, hi)

    def step3(self):
        for i, (lo, mid, hi) in self.flows:
            for first in (1, -1, 2):
                self.relay(i, first, lo, mid, hi)

    def finish(self):
        for i, _ in self.flows:
            for first in (0, 1, -1, 2):
                for sgn in (1, -1):
                    self.wait(i, "bb", first, sgn)
        self.mine.wait()


class TensorGather:
    def __init__(self, net, src, buf):
        self.net, self.src, self.buf = net, src, buf
        rows = src.shape[0]
        self.cut = (0, rows // 32 * 16, rows)

    def view(self, dy, other, lo, hi):
        n = self.net
        return self.buf.at[(n.y + dy) % 4, (1 - n.c) if other else n.c, pl.ds(lo, hi - lo), :]

    def start(self):
        n = self.net
        hi = self.cut[2]
        self.a = {
            sgn: n.send(self.src, self.view(0, 0, 0, hi), self.view(-sgn, 0, 0, hi), "+y" if sgn > 0 else "-y")
            for sgn in (1, -1)
        }
        self.sib = [n.send(self.src, self.view(0, 0, 0, hi), self.view(0, 1, 0, hi), "c")]

    def local(self, sem):
        n = self.net
        self.mine = pltpu.make_async_copy(self.src, self.buf.at[n.y, n.c], sem)
        self.mine.start()

    def pair(self, dy):
        n, hi = self.net, self.cut[2]
        self.sib.append(n.send(self.view(dy, 0, 0, hi), self.view(dy, 0, 0, hi), self.view(dy, 1, 0, hi), "c"))

    def step1(self):
        n = self.net
        lo, mid, hi = self.cut
        self.aa = []
        for sgn in (1, -1):
            self.a[sgn].recv()
            a, b = (lo, mid) if sgn > 0 else (mid, hi)
            self.aa.append(
                n.send(self.view(-sgn, 0, a, b), self.view(-sgn, 0, a, b), self.view(2, 0, a, b), "+y" if sgn > 0 else "-y")
            )
            self.pair(-sgn)

    def step2(self):
        for m in self.aa:
            m.recv()
        self.pair(2)

    def finish(self):
        for m in self.sib:
            m.recv()
        self.mine.wait()


def run_kernel(body, name, ident, outs, args, scratch, sems):
    def kernel(*refs):
        nin, nout = len(args), len(outs)
        body(refs[:nin], refs[nin : nin + nout], refs[nin + nout :])

    kernel.__name__ = name
    vm = pl.BlockSpec(memory_space=pltpu.VMEM)
    return pl.pallas_call(
        kernel,
        out_shape=[jax.ShapeDtypeStruct(shape, dtype) for shape, dtype in outs],
        in_specs=[vm] * len(args),
        out_specs=[vm] * len(outs),
        scratch_shapes=list(scratch)
        + [
            pltpu.SemaphoreType.DMA((sems,)),
            pltpu.SemaphoreType.DMA((sems,)),
            pltpu.SemaphoreType.DMA((8,)),
        ],
        compiler_params=pltpu.CompilerParams(
            collective_id=ident, has_side_effects=True, vmem_limit_bytes=48 * 2**20
        ),
        name=name,
    )(*args)


PLANE = ("+x", "-x", "+z", "-z")
LINE = ("+y", "-y", "c")


def run_gathers(gathers, lsem):
    for g in gathers:
        g.start()
    for k, g in enumerate(gathers):
        g.local(lsem.at[k])
    for g in gathers:
        g.step1()
    for g in gathers:
        g.step2()
    for g in gathers:
        if isinstance(g, ShardGather):
            g.step3()
    for g in gathers:
        g.finish()


def gather_kernel(name, ident, shard_args, tensor_args):
    args = list(shard_args) + list(tensor_args)
    ns = len(shard_args)
    outs = [((4, 4) + a.shape, a.dtype) for a in shard_args] + [((4, 2) + a.shape, a.dtype) for a in tensor_args]
    dirs = (PLANE if shard_args else ()) + (LINE if tensor_args else ())

    def body(ins, out, rest):
        net = Net(rest[-3], rest[-2])
        net.barrier(dirs)
        gs = [TensorGather(net, ins[k], out[k]) for k in range(ns, len(args))]
        gs += [ShardGather(net, ins[k], out[k]) for k in range(ns)]
        run_gathers(gs, rest[-1])
        net.drain()

    return run_kernel(body, name, ident, outs, args, [], 40 * ns + 8 * len(tensor_args))


def broadcast_line(net, src, dst, lsem):
    rows = src.shape[0]
    half = rows // 2
    k = net.count
    net.count += 5
    dy = (net.y - net.z + 4) % 4
    main = net.c == net.x // 2

    def mk(j, a, lo, hi, d):
        return pltpu.make_async_remote_copy(
            src_ref=a.at[pl.ds(lo, hi - lo), :],
            dst_ref=dst.at[pl.ds(lo, hi - lo), :],
            send_sem=net.send_sem.at[k + j],
            recv_sem=net.recv_sem.at[k + j],
            device_id=net.nbr(d),
            device_id_type=MESH,
        )

    @pl.when(main)
    def _():
        @pl.when(dy == 0)
        def _():
            plus, minus, sib = mk(0, src, 0, rows, "+y"), mk(1, src, 0, rows, "-y"), mk(4, src, 0, rows, "c")
            plus.start()
            minus.start()
            sib.start()
            mine = pltpu.make_async_copy(src, dst, lsem)
            mine.start()
            mine.wait()
            plus.wait_send()
            minus.wait_send()
            sib.wait_send()

        @pl.when(dy == 1)
        def _():
            mk(0, dst, 0, rows, "+y").wait_recv()
            on, sib = mk(2, dst, 0, half, "+y"), mk(4, dst, 0, rows, "c")
            on.start()
            sib.start()
            on.wait_send()
            sib.wait_send()

        @pl.when(dy == 3)
        def _():
            mk(1, dst, 0, rows, "-y").wait_recv()
            on, sib = mk(3, dst, half, rows, "-y"), mk(4, dst, 0, rows, "c")
            on.start()
            sib.start()
            on.wait_send()
            sib.wait_send()

        @pl.when(dy == 2)
        def _():
            mk(2, dst, 0, half, "+y").wait_recv()
            mk(3, dst, half, rows, "-y").wait_recv()
            sib = mk(4, dst, 0, rows, "c")
            sib.start()
            sib.wait_send()

    @pl.when(jnp.logical_not(main))
    def _():
        mk(4, dst, 0, rows, "c").wait_recv()


def line_kernel(name, ident, own, tensor_args):
    args = [own] + list(tensor_args)
    outs = [(own.shape, own.dtype)] + [((4, 2) + a.shape, a.dtype) for a in tensor_args]

    def body(ins, out, rest):
        net = Net(rest[-3], rest[-2])
        net.barrier(LINE)
        gs = [TensorGather(net, ins[k], out[k]) for k in range(1, len(args))]
        for g in gs:
            g.start()
        for j, g in enumerate(gs):
            g.local(rest[-1].at[j + 1])
        for g in gs:
            g.step1()
        broadcast_line(net, ins[0], out[0], rest[-1].at[0])
        for g in gs:
            g.step2()
        for g in gs:
            g.finish()
        net.drain()

    return run_kernel(body, name, ident, outs, args, [], 5 + 8 * len(tensor_args))


def add_into(a, b):
    a[...] = (a[...].astype(F32) + b[...].astype(F32)).astype(a.dtype)


class RingScatter:
    def __init__(self, net, axis, pick, half, first, second):
        self.net, self.axis, self.pick, self.half = net, axis, pick, half
        self.first, self.second = first, second

    def start(self):
        n = self.net
        self.one = [
            n.send(self.half(self.pick(2), h), self.first[h], self.first[h], ("+", "-")[h] + self.axis) for h in (0, 1)
        ]

    def middle(self):
        n = self.net
        self.two = []
        for h, rel in ((0, 1), (1, -1)):
            self.one[h].recv()
            add_into(self.half(self.pick(rel), h), self.first[h])
            self.two.append(n.send(self.pick(rel), self.second[h], self.second[h], ("+", "-")[h] + self.axis))

    def total(self):
        for m in self.two:
            m.recv()
        own = self.pick(0)
        return own[...].astype(F32) + self.second[0][...].astype(F32) + self.second[1][...].astype(F32)


def plane_scatter(net, part, out, rest):
    z, x = net.z, net.x
    rows, cols = part.shape[2], part.shape[3]
    h = rows // 2
    f1, f2, q, g1, g2 = rest[:5]
    zx = (z, x)
    stages = []
    for i in (0, 1):
        lo = i * h

        def pick(rel, i=i, lo=lo):
            if i == 0:
                return part.at[(z + rel) % 4, :, pl.ds(lo, h), :]
            return part.at[:, (x + rel) % 4, pl.ds(lo, h), :]

        def half(view, k):
            return view.at[pl.ds(2 * k, 2)]

        stages.append(
            RingScatter(net, "zx"[i], pick, half, [f1.at[i, 0], f1.at[i, 1]], [f2.at[i, 0], f2.at[i, 1]])
        )
    for r in stages:
        r.start()
    for r in stages:
        r.middle()
    later = []
    for i, r in enumerate(stages):
        q[i] = r.total().astype(q.dtype)

        def pick(rel, i=i):
            return q.at[i, (zx[1 - i] + rel) % 4]

        def half(view, k):
            return view.at[pl.ds(k * (h // 2), h // 2), :]

        later.append(
            RingScatter(net, "xz"[i], pick, half, [g1.at[i, 0], g1.at[i, 1]], [g2.at[i, 0], g2.at[i, 1]])
        )
        later[-1].start()
    for r in later:
        r.middle()
    for i, r in enumerate(later):
        out[pl.ds(i * h, h), :] = r.total()


def scatter_kernel(name, ident, part, tiles):
    rows, cols = part.shape[2:]
    h = rows // 2
    args = [part] + list(tiles)
    outs = [((rows, cols), F32)] + [((4, 4) + a.shape, a.dtype) for a in tiles]
    scratch = [
        pltpu.VMEM((2, 2, 2, h, cols), BF),
        pltpu.VMEM((2, 2, 4, h, cols), BF),
        pltpu.VMEM((2, 4, h, cols), BF),
        pltpu.VMEM((2, 2, h // 2, cols), BF),
        pltpu.VMEM((2, 2, h, cols), BF),
    ]

    def body(ins, out, rest):
        net = Net(rest[-3], rest[-2])
        net.barrier(PLANE)
        gs = [ShardGather(net, ins[k], out[k]) for k in range(1, len(args))]
        for g in gs:
            g.start()
        for j, g in enumerate(gs):
            g.local(rest[-1].at[j])
        plane_scatter(net, ins[0], out[0], rest)
        for g in gs:
            g.step1()
        for g in gs:
            g.step2()
        for g in gs:
            g.step3()
        for g in gs:
            g.finish()
        net.drain()

    return run_kernel(body, name, ident, outs, args, scratch, 16 + 20 * len(tiles))


def line_scatter(net, part, out, rest):
    y, c = net.y, net.c
    g0, q, g1, g2 = rest[:4]
    rows = part.shape[2]
    m = net.send(part.at[1 - c], g0, g0, "c")
    m.recv()
    q[...] = (part[c].astype(F32) + g0[...].astype(F32)).astype(q.dtype)
    cut = rows // 32 * 16

    def pick(rel):
        return q.at[(y + rel) % 4]

    def half(view, k):
        return view.at[pl.ds(0, cut), :] if k == 0 else view.at[pl.ds(cut, rows - cut), :]

    ring = RingScatter(net, "y", pick, half, [g1.at[pl.ds(0, cut)], g1.at[pl.ds(cut, rows - cut)]], [g2.at[0], g2.at[1]])
    ring.start()
    yield
    ring.middle()
    yield
    out[...] = ring.total().astype(out.dtype)


def power_kernel(name, ident, part, block):
    rows, cols = part.shape[2:]
    outs = [((rows, cols), BF), ((4, 2) + block.shape, block.dtype)]
    scratch = [
        pltpu.VMEM((4, rows, cols), BF),
        pltpu.VMEM((4, rows, cols), BF),
        pltpu.VMEM((rows, cols), BF),
        pltpu.VMEM((2, rows, cols), BF),
    ]

    def body(ins, out, rest):
        net = Net(rest[-3], rest[-2])
        net.barrier(LINE)
        g = TensorGather(net, ins[1], out[1])
        g.start()
        g.local(rest[-1].at[0])
        steps = line_scatter(net, ins[0], out[0], rest)
        next(steps)
        g.step1()
        next(steps)
        g.step2()
        for _ in steps:
            pass
        g.finish()
        net.drain()

    return run_kernel(body, name, ident, outs, [part, block], scratch, 16)


def dot(a, b):
    return jnp.dot(a, b, preferred_element_type=F32)


def rows_dot(blocks, cols):
    wide = blocks.reshape(8, blocks.shape[2], blocks.shape[3]).transpose(1, 0, 2).reshape(blocks.shape[2], -1)
    return dot(wide, cols)


def gram_terms(blocks, own):
    b = blocks.reshape(8, blocks.shape[2], blocks.shape[3])
    out = jnp.einsum("tri,rj->tij", b, own, preferred_element_type=F32)
    return out.astype(BF).reshape(4, 4, FF // 16, own.shape[1])


def local(gradient, moment_one, moment_two, stat_left, stat_right, basis_left, basis_right):
    s = lax.axis_index("shard")
    rows_left = gradient.shape[0]
    left_q = (basis_left / math.sqrt(D)).astype(BF)
    right_q = (basis_right / math.sqrt(FF)).astype(BF)
    grad_cols, left_all, right_cols = gather_kernel("gather_in", 0, [gradient, left_q, right_q], [])
    grad_cols = grad_cols.reshape(D, -1)
    left_all = left_all.reshape(D, D)
    right_cols = right_cols.reshape(FF, -1)
    width = FF // 16
    give = jnp.where(s % 2 == 0, grad_cols[:, :width], grad_cols[:, width:])
    own_cols = lax.dynamic_slice_in_dim(left_all, s * rows_left, rows_left, 1)
    half = dot(own_cols.T, grad_cols).astype(BF)
    left_terms = dot(gradient, grad_cols.T).astype(BF)
    grad_rows, half_rows, left_parts = line_kernel("line_in", 1, give, [half, left_terms])
    new_stat_right = beta * stat_right + (1.0 - beta) * (dot(grad_rows.T, grad_cols) / D)
    gram_rows = jnp.sum(left_parts.reshape(8, rows_left, D).astype(F32), axis=0)
    new_stat_left = beta * stat_left + (1.0 - beta) * (gram_rows / FF)
    rotated = rows_dot(half_rows, right_cols)
    new_moment_one = beta * moment_one + (1.0 - beta) * rotated
    new_moment_two = beta * moment_two + (1.0 - beta) * (rotated * rotated)
    direction = (
        new_moment_one / correction / (jnp.sqrt(new_moment_two / correction) + adam_eps)
    ).astype(BF)
    power_left = dot(new_stat_left.astype(BF), left_all).astype(BF)
    dir_cols, power_left_all, stat_rows = gather_kernel(
        "gather_mid", 2, [direction, power_left], [new_stat_right.astype(BF)]
    )
    back_half = dot(left_q, dir_cols.reshape(D, -1)).astype(BF)
    back_terms = dot(back_half, right_cols.T).astype(BF)
    back_terms = back_terms.reshape(rows_left, 4, 2, -1).transpose(2, 1, 0, 3)
    power = rows_dot(stat_rows, right_cols)
    power_b = power.astype(BF)
    update, power_rows = power_kernel("line_mid", 3, back_terms, power_b)

    terms = gram_terms(power_rows, power_b)
    squares = jnp.sum(jnp.square(power_rows.astype(F32)))
    gram, tiles = scatter_kernel("scatter_one", 4, terms, [jnp.broadcast_to(squares, (8, 128))])
    total = jnp.sum(tiles[:, :, 0, 0])
    scale = math.sqrt(FF) / (4.0 * jnp.sqrt(total))
    gram_b = (gram * (scale * scale)).astype(BF)
    (gram_cols,) = gather_kernel("gather_one", 5, [gram_b], [])
    iterate = scale * (1.5 * power - 0.5 * rows_dot(power_rows, gram_cols.reshape(FF, -1)))
    iterate_b = iterate.astype(BF)
    (iterate_rows,) = gather_kernel("line_two", 6, [], [iterate_b])
    (gram,) = scatter_kernel("scatter_two", 7, gram_terms(iterate_rows, iterate_b), [])
    (gram_cols,) = gather_kernel("gather_two", 8, [gram.astype(BF)], [])
    iterate = 1.5 * iterate - 0.5 * rows_dot(iterate_rows, gram_cols.reshape(FF, -1))

    whole = power_left_all.reshape(D, D).astype(F32)
    whole = whole * (math.sqrt(D) / (4.0 * jnp.sqrt(jnp.sum(whole * whole))))
    wb = whole.astype(BF)
    gl = dot(wb.T, wb).astype(BF)
    whole = 1.5 * whole - 0.5 * dot(wb, gl)
    wb = whole.astype(BF)
    gl = dot(wb.T, wb).astype(BF)
    own = lax.dynamic_slice_in_dim(whole, s * rows_left, rows_left, 0)
    left = 1.5 * own - 0.5 * dot(own.astype(BF), gl)
    return (
        update,
        new_moment_one,
        new_moment_two,
        new_stat_left,
        new_stat_right,
        left * math.sqrt(D),
        iterate * math.sqrt(FF),
    )


def solution(mesh):
    both, row = P("shard", "tensor"), P("shard", None)
    return jax.shard_map(
        local,
        mesh=mesh,
        in_specs=(both, both, both, row, both, row, both),
        out_specs=(both, both, both, row, both, row, both),
        check_vma=False,
    )
```

```python
import functools
import math

import jax
import jax.numpy as jnp
from jax import lax
from jax.experimental import pallas as pl
from jax.experimental.pallas import tpu as pltpu
from jax.sharding import PartitionSpec as P

D = 768
FF = 3072
BF = jnp.bfloat16
F32 = jnp.float32
MESH = pl.DeviceIdType.MESH

beta = 0.95
correction = 1.0 - 0.95**10
adam_eps = 1e-08


class Move:
    def __init__(self, copy, landing):
        self.copy, self.landing = copy, landing

    def recv(self):
        self.landing.wait_recv()


class Net:
    def __init__(self, send_sem, recv_sem):
        self.send_sem, self.recv_sem = send_sem, recv_sem
        self.count = 0
        self.sent = []
        s, t = lax.axis_index("shard"), lax.axis_index("tensor")
        self.s, self.t = s, t
        self.z, self.x = s // 4, s % 4
        self.y, self.c = t // 2, t % 2

    def nbr(self, d):
        s, t = self.s, self.t
        z, x, y, c = self.z, self.x, self.y, self.c
        if d == "c":
            return (s, y * 2 + 1 - c)
        step = 1 if d[0] == "+" else 3
        if d[1] == "x":
            return (z * 4 + (x + step) % 4, t)
        if d[1] == "z":
            return (((z + step) % 4) * 4 + x, t)
        return (s, ((y + step) % 4) * 2 + c)

    def barrier(self, dirs):
        sem = pltpu.get_barrier_semaphore()
        for d in dirs:
            pl.semaphore_signal(sem, inc=1, device_id=self.nbr(d), device_id_type=MESH)
        pl.semaphore_wait(sem, len(dirs))

    def send(self, src, dst, landing, d):
        k = self.count
        self.count += 1
        mk = lambda a, b: pltpu.make_async_remote_copy(
            src_ref=a,
            dst_ref=b,
            send_sem=self.send_sem.at[k],
            recv_sem=self.recv_sem.at[k],
            device_id=self.nbr(d),
            device_id_type=MESH,
        )
        copy = mk(src, dst)
        copy.start()
        self.sent.append(copy)
        return Move(copy, mk(landing, landing))

    def drain(self):
        for copy in self.sent:
            copy.wait_send()
        self.sent = []


def cuts(rows):
    if rows % 64 == 0:
        q = rows // 4
        return ((0, q, 2 * q), (2 * q, 3 * q, 4 * q))
    if rows == 48:
        return ((0, 16, 32), (32, 48, 48))
    return ((0, rows, rows), None)


class ShardGather:
    def __init__(self, net, src, buf):
        self.net, self.src, self.buf = net, src, buf
        self.flows = [(i, f) for i, f in enumerate(cuts(src.shape[0])) if f is not None]
        self.m = {}

    def view(self, blk, lo, hi):
        n, rows = self.net, self.src.shape[0]
        slot = (n.z + blk[0]) % 4 * 4 + (n.x + blk[1]) % 4
        return self.buf.at[pl.ds(pl.multiple_of(slot * rows + lo, 8), hi - lo), :]

    def axes(self, i):
        return ("x", "z") if i == 0 else ("z", "x")

    def rel(self, i, first, second):
        return (second, first) if i == 0 else (first, second)

    def go(self, i, stage, sgn, first, second, lo, hi, key, own=False):
        if hi == lo:
            return
        axis = self.axes(i)[stage]
        d = ("+" if sgn > 0 else "-") + axis
        blk = self.rel(i, first, second)
        lf, ls = (first - sgn, second) if stage == 0 else (first, second - sgn)
        src = self.src.at[pl.ds(lo, hi - lo), :] if own else self.view(blk, lo, hi)
        self.m[key] = self.net.send(src, self.view(blk, lo, hi), self.view(self.rel(i, lf, ls), lo, hi), d)

    def wait(self, *key):
        if key in self.m:
            self.m[key].recv()

    def start(self):
        n = self.net
        for i, (lo, mid, hi) in self.flows:
            for sgn in (1, -1):
                self.go(i, 0, sgn, 0, 0, lo, hi, (i, "a", sgn), own=True)
        for i, (lo, mid, hi) in self.flows:
            for sgn in (1, -1):
                self.go(i, 1, sgn, 0, 0, lo, hi, (i, "b", 0, sgn), own=True)

    def local(self, sem):
        n = self.net
        self.mine = pltpu.make_async_copy(self.src, self.view((0, 0), 0, self.src.shape[0]), sem)
        self.mine.start()

    def second(self, i, first, lo, hi):
        for sgn in (1, -1):
            self.go(i, 1, sgn, first, 0, lo, hi, (i, "b", first, sgn))

    def relay(self, i, first, lo, mid, hi):
        for sgn in (1, -1):
            self.wait(i, "b", first, sgn)
            a, b = (lo, mid) if sgn > 0 else (mid, hi)
            self.go(i, 1, sgn, first, -sgn, a, b, (i, "bb", first, sgn))

    def step1(self):
        for i, (lo, mid, hi) in self.flows:
            for sgn in (1, -1):
                self.wait(i, "a", sgn)
                a, b = (lo, mid) if sgn > 0 else (mid, hi)
                self.go(i, 0, sgn, -sgn, 0, a, b, (i, "aa", sgn))
                self.second(i, -sgn, lo, hi)

    def step2(self):
        for i, (lo, mid, hi) in self.flows:
            self.relay(i, 0, lo, mid, hi)
        for i, (lo, mid, hi) in self.flows:
            self.wait(i, "aa", 1)
            self.wait(i, "aa", -1)
            self.second(i, 2, lo, hi)

    def step3(self):
        for i, (lo, mid, hi) in self.flows:
            for first in (1, -1, 2):
                self.relay(i, first, lo, mid, hi)

    def finish(self):
        for i, _ in self.flows:
            for first in (0, 1, -1, 2):
                for sgn in (1, -1):
                    self.wait(i, "bb", first, sgn)
        self.mine.wait()


class TensorGather:
    def __init__(self, net, src, buf):
        self.net, self.src, self.buf = net, src, buf
        rows = src.shape[0]
        self.cut = (0, rows // 32 * 16, rows)

    def view(self, dy, other, lo, hi):
        n, rows = self.net, self.src.shape[0]
        slot = (n.y + dy) % 4 * 2 + ((1 - n.c) if other else n.c)
        return self.buf.at[pl.ds(pl.multiple_of(slot * rows + lo, 16), hi - lo), :]

    def start(self):
        n = self.net
        hi = self.cut[2]
        self.a = {
            sgn: n.send(self.src, self.view(0, 0, 0, hi), self.view(-sgn, 0, 0, hi), "+y" if sgn > 0 else "-y")
            for sgn in (1, -1)
        }
        self.sib = [n.send(self.src, self.view(0, 0, 0, hi), self.view(0, 1, 0, hi), "c")]

    def local(self, sem):
        n = self.net
        self.mine = pltpu.make_async_copy(self.src, self.view(0, 0, 0, self.src.shape[0]), sem)
        self.mine.start()

    def pair(self, dy):
        n, hi = self.net, self.cut[2]
        self.sib.append(n.send(self.view(dy, 0, 0, hi), self.view(dy, 0, 0, hi), self.view(dy, 1, 0, hi), "c"))

    def step1(self):
        n = self.net
        lo, mid, hi = self.cut
        self.aa = []
        for sgn in (1, -1):
            self.a[sgn].recv()
            a, b = (lo, mid) if sgn > 0 else (mid, hi)
            self.aa.append(
                n.send(self.view(-sgn, 0, a, b), self.view(-sgn, 0, a, b), self.view(2, 0, a, b), "+y" if sgn > 0 else "-y")
            )
            self.pair(-sgn)

    def step2(self):
        for m in self.aa:
            m.recv()
        self.pair(2)

    def finish(self):
        for m in self.sib:
            m.recv()
        self.mine.wait()


def add_into(a, b):
    a[...] = (a[...].astype(F32) + b[...].astype(F32)).astype(a.dtype)


class RingScatter:
    def __init__(self, net, axis, pick, half, first, second):
        self.net, self.axis, self.pick, self.half = net, axis, pick, half
        self.first, self.second = first, second

    def start(self):
        n = self.net
        self.one = [
            n.send(self.half(self.pick(2), h), self.first[h], self.first[h], ("+", "-")[h] + self.axis) for h in (0, 1)
        ]

    def middle(self):
        n = self.net
        self.two = []
        for h, rel in ((0, 1), (1, -1)):
            self.one[h].recv()
            add_into(self.half(self.pick(rel), h), self.first[h])
            self.two.append(n.send(self.pick(rel), self.second[h], self.second[h], ("+", "-")[h] + self.axis))

    def total(self):
        for m in self.two:
            m.recv()
        own = self.pick(0)
        return own[...].astype(F32) + self.second[0][...].astype(F32) + self.second[1][...].astype(F32)


class LineBroadcast:
    def __init__(self, net, src, dst, lsem):
        self.net, self.src, self.dst, self.lsem = net, src, dst, lsem
        self.k = net.count
        net.count += 5
        self.dy = (net.y - net.z + 4) % 4
        self.main = net.c == net.x // 2
        self.rows = src.shape[0]

    def msg(self, j, a, lo, hi, d):
        n = self.net
        return pltpu.make_async_remote_copy(
            src_ref=a.at[pl.ds(lo, hi - lo), :],
            dst_ref=self.dst.at[pl.ds(lo, hi - lo), :],
            send_sem=n.send_sem.at[self.k + j],
            recv_sem=n.recv_sem.at[self.k + j],
            device_id=n.nbr(d),
            device_id_type=MESH,
        )

    def at(self, dy):
        return pl.when(jnp.logical_and(self.main, self.dy == dy))

    def start(self):
        r = self.rows

        @self.at(0)
        def _():
            self.msg(0, self.src, 0, r, "+y").start()
            self.msg(1, self.src, 0, r, "-y").start()
            self.msg(4, self.src, 0, r, "c").start()
            pltpu.make_async_copy(self.src, self.dst, self.lsem).start()

    def middle(self):
        r, h = self.rows, self.rows // 2

        @self.at(1)
        def _():
            self.msg(0, self.dst, 0, r, "+y").wait_recv()
            self.msg(2, self.dst, 0, h, "+y").start()
            self.msg(4, self.dst, 0, r, "c").start()

        @self.at(3)
        def _():
            self.msg(1, self.dst, 0, r, "-y").wait_recv()
            self.msg(3, self.dst, h, r, "-y").start()
            self.msg(4, self.dst, 0, r, "c").start()

    def finish(self):
        r, h = self.rows, self.rows // 2

        @self.at(2)
        def _():
            self.msg(2, self.dst, 0, h, "+y").wait_recv()
            self.msg(3, self.dst, h, r, "-y").wait_recv()
            self.msg(4, self.dst, 0, r, "c").start()

        @pl.when(jnp.logical_not(self.main))
        def _():
            self.msg(4, self.dst, 0, r, "c").wait_recv()

        @self.at(0)
        def _():
            pltpu.make_async_copy(self.src, self.dst, self.lsem).wait()
            self.msg(0, self.src, 0, r, "+y").wait_send()
            self.msg(1, self.src, 0, r, "-y").wait_send()

        @self.at(1)
        def _():
            self.msg(2, self.dst, 0, h, "+y").wait_send()

        @self.at(3)
        def _():
            self.msg(3, self.dst, h, r, "-y").wait_send()

        @pl.when(self.main)
        def _():
            self.msg(4, self.dst, 0, r, "c").wait_send()


def plane_scatter(net, part, out, f1, f2, q, g1, g2):
    z, x = net.z, net.x
    h = part.shape[2] // 2
    zx = (z, x)
    stages = []
    for i in (0, 1):
        lo = i * h

        def pick(rel, i=i, lo=lo):
            if i == 0:
                return part.at[(z + rel) % 4, :, pl.ds(lo, h), :]
            return part.at[:, (x + rel) % 4, pl.ds(lo, h), :]

        def half(view, k):
            return view.at[pl.ds(2 * k, 2)]

        stages.append(RingScatter(net, "zx"[i], pick, half, [f1.at[i, 0], f1.at[i, 1]], [f2.at[i, 0], f2.at[i, 1]]))
    for r in stages:
        r.start()
    yield
    for r in stages:
        r.middle()
    yield
    later = []
    for i, r in enumerate(stages):
        q[i] = r.total().astype(q.dtype)

        def pick(rel, i=i):
            return q.at[i, (zx[1 - i] + rel) % 4]

        def half(view, k):
            return view.at[pl.ds(k * (h // 2), h // 2), :]

        later.append(RingScatter(net, "xz"[i], pick, half, [g1.at[i, 0], g1.at[i, 1]], [g2.at[i, 0], g2.at[i, 1]]))
        later[-1].start()
    yield
    for r in later:
        r.middle()
    yield
    for i, r in enumerate(later):
        out[pl.ds(i * h, h), :] = r.total()


def line_scatter(net, part, out, g0, q, g1, g2):
    y, c = net.y, net.c
    rows = part.shape[2]
    m = net.send(part.at[1 - c], g0, g0, "c")
    yield
    m.recv()
    q[...] = (part[c].astype(F32) + g0[...].astype(F32)).astype(q.dtype)
    cut = rows // 32 * 16

    def pick(rel):
        return q.at[(y + rel) % 4]

    def half(view, k):
        return view.at[pl.ds(0, cut), :] if k == 0 else view.at[pl.ds(cut, rows - cut), :]

    ring = RingScatter(net, "y", pick, half, [g1.at[pl.ds(0, cut)], g1.at[pl.ds(cut, rows - cut)]], [g2.at[0], g2.at[1]])
    ring.start()
    yield
    ring.middle()
    yield
    out[...] = ring.total().astype(out.dtype)


def dot(a, b):
    return jnp.dot(a, b, preferred_element_type=F32)


def dot_tn(a, b):
    return lax.dot_general(a, b, (((0,), (0,)), ((), ())), preferred_element_type=F32)


def dot_nt(a, b):
    return lax.dot_general(a, b, (((1,), (1,)), ((), ())), preferred_element_type=F32)


def rows_dot(blocks, cols, acc):
    rows, width = acc.shape[0], blocks.shape[1]
    acc[...] = jnp.zeros_like(acc)

    def step(j, carry):
        a = blocks[pl.ds(pl.multiple_of(j * rows, 16), rows), :]
        acc[...] += dot(a, cols[pl.ds(pl.multiple_of(j * width, 16), width), :])
        return carry

    lax.fori_loop(0, 8, step, 0)


SEMS = 430
ROWS, COLS, LROWS = FF // 16, FF // 8, D // 16
BUFFERS = dict(
    lq=((LROWS, D), BF),
    rq=((ROWS, COLS), BF),
    gcols=((D, COLS), BF),
    lall=((D, D), BF),
    qcols=((FF, COLS), BF),
    gs_own=((D, ROWS), BF),
    gs=((D, ROWS), BF),
    lterms=((LROWS, D), BF),
    lparts=((8 * LROWS, D), BF),
    half_all=((D, COLS), BF),
    half_rows=((8 * LROWS, COLS), BF),
    s_b=((ROWS, COLS), BF),
    s_rows=((8 * ROWS, COLS), BF),
    p=((ROWS, COLS), F32),
    p_b=((ROWS, COLS), BF),
    p_rows=((8 * ROWS, COLS), BF),
    rot=((LROWS, COLS), F32),
    dir_b=((LROWS, COLS), BF),
    dir_cols=((D, COLS), BF),
    pl_own=((LROWS, D), F32),
    pl_b=((LROWS, D), BF),
    pl_all=((D, D), BF),
    gl=((D, D), BF),
    wl=((D, D), BF),
    tile=((8, 128), F32),
    tiles=((128, 128), F32),
    part=((4, 4, ROWS, COLS), BF),
    f1=((2, 2, 2, ROWS // 2, COLS), BF),
    f2=((2, 2, 4, ROWS // 2, COLS), BF),
    fq=((2, 4, ROWS // 2, COLS), BF),
    fg1=((2, 2, ROWS // 4, COLS), BF),
    fg2=((2, 2, ROWS // 2, COLS), BF),
    a=((ROWS, COLS), F32),
    a_b=((ROWS, COLS), BF),
    a_cols=((FF, COLS), BF),
    a_rows=((8 * ROWS, COLS), BF),
    t=((ROWS, COLS), F32),
    t_b=((ROWS, COLS), BF),
    t_cols=((FF, COLS), BF),
    t_rows=((8 * ROWS, COLS), BF),
    w=((ROWS, COLS), F32),
    w_b=((ROWS, COLS), BF),
    w_cols=((FF, COLS), BF),
    upart=((2, 4, LROWS, COLS), BF),
    u0=((4, LROWS, COLS), BF),
    uq=((4, LROWS, COLS), BF),
    u1=((LROWS, COLS), BF),
    u2=((2, LROWS, COLS), BF),
)
NBR = ("+x", "-x", "+z", "-z", "+y", "-y", "c")


def kernel(*refs):
    grad, m1, m2, stat_l, stat_r, basis_l, basis_r = refs[:7]
    update, new_m1, new_m2, new_sl, new_sr, new_bl, new_br = refs[7:14]
    b = dict(zip(BUFFERS, refs[14 : 14 + len(BUFFERS)]))
    send_sem, recv_sem, lsem = refs[14 + len(BUFFERS) :]
    net = Net(send_sem, recv_sem)
    x, s = net.x, net.s
    own_left = pl.ds(pl.multiple_of(s * LROWS, 16), LROWS)
    locals_used = [0]

    def begin(*gathers):
        for g in gathers:
            g.start()
            g.local(lsem.at[locals_used[0]])
            locals_used[0] += 1

    def shard(src, dst):
        return ShardGather(net, src if not isinstance(src, str) else b[src], b[dst])

    def tensor(src, dst):
        return TensorGather(net, b[src], b[dst])

    b["lq"][...] = (basis_l[...] * (1.0 / math.sqrt(D))).astype(BF)
    b["rq"][...] = (basis_r[...] * (1.0 / math.sqrt(FF))).astype(BF)
    net.barrier(NBR)

    g_grad, g_left, g_right = shard(grad, "gcols"), shard("lq", "lall"), shard("rq", "qcols")
    begin(g_grad, g_left)
    g_grad.step1()
    g_left.step1()
    g_grad.step2()
    g_left.step2()
    g_grad.step3()
    g_grad.finish()
    begin(g_right)
    cast = LineBroadcast(net, b["gs_own"], b["gs"], lsem.at[locals_used[0]])
    locals_used[0] += 1
    pick = lax.broadcasted_iota(jnp.int32, (COLS, ROWS), 0) == lax.broadcasted_iota(
        jnp.int32, (COLS, ROWS), 1
    ) + ROWS * (x % 2)
    gcols = b["gcols"][...]
    b["gs_own"][...] = dot(gcols, jnp.where(pick, 1.0, 0.0).astype(BF)).astype(BF)
    cast.start()
    b["lterms"][...] = dot_nt(grad[...], gcols).astype(BF)
    t_lterms = tensor("lterms", "lparts")
    begin(t_lterms)
    g_left.step3()
    g_right.step1()
    cast.middle()
    g_left.finish()
    b["half_all"][...] = dot_tn(b["lall"][...], gcols).astype(BF)
    g_right.step2()
    cast.finish()

    new_sr[...] = beta * stat_r[...] + ((1.0 - beta) / D) * dot_tn(b["gs"][...], gcols)
    b["s_b"][...] = new_sr[...].astype(BF)
    t_stat = tensor("s_b", "s_rows")
    begin(t_stat)
    t_half = TensorGather(net, b["half_all"].at[own_left, :], b["half_rows"])
    begin(t_half)
    t_lterms.step1()
    g_right.step3()
    t_stat.step1()
    t_half.step1()
    t_lterms.step2()
    t_stat.step2()
    t_half.step2()
    g_right.finish()
    t_stat.finish()
    rows_dot(b["s_rows"], b["qcols"], b["p"])
    b["p_b"][...] = b["p"][...].astype(BF)
    t_power = tensor("p_b", "p_rows")
    begin(t_power)

    t_lterms.finish()
    t_half.finish()
    rows_dot(b["half_rows"], b["qcols"], b["rot"])
    rot = b["rot"][...]
    first = beta * m1[...] + (1.0 - beta) * rot
    second = beta * m2[...] + (1.0 - beta) * (rot * rot)
    new_m1[...] = first
    new_m2[...] = second
    b["dir_b"][...] = ((first / correction) / (jnp.sqrt(second / correction) + adam_eps)).astype(BF)
    g_dir = shard("dir_b", "dir_cols")
    begin(g_dir)
    gram = b["lparts"][pl.ds(0, LROWS), :].astype(F32)
    for j in range(1, 8):
        gram += b["lparts"][pl.ds(j * LROWS, LROWS), :].astype(F32)
    new_sl[...] = beta * stat_l[...] + ((1.0 - beta) / FF) * gram
    b["pl_own"][...] = dot(new_sl[...].astype(BF), b["lall"][...])
    b["pl_b"][...] = b["pl_own"][...].astype(BF)
    g_pl = shard("pl_b", "pl_all")
    begin(g_pl)
    t_power.step1()
    g_dir.step1()
    g_pl.step1()
    t_power.step2()
    t_power.finish()

    def squares(j, total):
        v = b["p_rows"][pl.ds(pl.multiple_of(j * 16, 16), 16), :].astype(F32)
        return total + v * v

    def term(j, carry):
        v = dot_tn(b["p_rows"][pl.ds(pl.multiple_of(j * ROWS, 16), ROWS), :], b["p_b"][...]).astype(BF)
        b["part"][j // 2, pl.ds(j % 2 * 2, 2), :, :] = v.reshape(2, ROWS, COLS)
        return carry

    lax.fori_loop(0, 8, term, 0)
    scatter = plane_scatter(net, b["part"], b["a"], b["f1"], b["f2"], b["fq"], b["fg1"], b["fg2"])
    next(scatter)
    total = lax.fori_loop(0, ROWS // 2, squares, jnp.zeros((16, COLS), F32))
    b["tile"][...] = jnp.broadcast_to(jnp.sum(total, keepdims=True), (8, 128))
    g_tile = shard("tile", "tiles")
    begin(g_tile)
    g_dir.step2()
    g_pl.step2()
    next(scatter)
    g_tile.step1()
    g_dir.step3()
    g_pl.step3()
    next(scatter)
    g_tile.step2()
    next(scatter)
    g_tile.step3()
    for _ in scatter:
        pass
    g_tile.finish()
    norm = jnp.sum(b["tiles"][...], keepdims=True) / 1024.0
    scale = math.sqrt(FF) / (4.0 * jnp.sqrt(norm))
    b["a"][...] = b["a"][...] * (scale * scale)
    b["a_b"][...] = b["a"][...].astype(BF)
    g_a, t_a = shard("a_b", "a_cols"), tensor("a_b", "a_rows")
    begin(g_a, t_a)

    g_dir.finish()
    back = dot(b["lq"][...], b["dir_cols"][...]).astype(BF)

    def back_term(j, carry):
        v = dot_nt(back, b["qcols"][pl.ds(pl.multiple_of(j * COLS, 16), COLS), :])
        b["upart"][j % 2, j // 2] = v.astype(BF)
        return carry

    lax.fori_loop(0, 8, back_term, 0)
    to_update = line_scatter(net, b["upart"], update, b["u0"], b["uq"], b["u1"], b["u2"])
    g_a.step1()
    t_a.step1()
    next(to_update)
    g_a.step2()
    t_a.step2()
    next(to_update)

    g_pl.finish()

    def left_squares(j, total):
        v = b["pl_all"][pl.ds(pl.multiple_of(j * 16, 16), 16), :].astype(F32)
        return total + v * v

    left_total = lax.fori_loop(0, D // 16, left_squares, jnp.zeros((16, D), F32))
    left_scale = math.sqrt(D) / (4.0 * jnp.sqrt(jnp.sum(left_total, keepdims=True)))

    def left_gram(ref, factor):
        def step(j, carry):
            cut = pl.ds(pl.multiple_of(j * 128, 128), 128)
            b["gl"][cut, :] = (dot_tn(ref[:, cut], ref[...]) * factor).astype(BF)
            return carry

        lax.fori_loop(0, D // 128, step, 0)

    g_a.step3()
    left_gram(b["pl_all"], left_scale * left_scale)
    next(to_update)
    g_a.finish()
    t_a.finish()
    for _ in to_update:
        pass

    rows_dot(b["a_rows"], b["a_cols"], b["t"])
    b["t_b"][...] = b["t"][...].astype(BF)
    g_t, t_t = shard("t_b", "t_cols"), tensor("t_b", "t_rows")
    begin(g_t, t_t)

    def left_step(j, carry):
        cut = pl.ds(pl.multiple_of(j * 128, 128), 128)
        v = b["pl_all"][cut, :]
        b["wl"][cut, :] = (left_scale * (1.5 * v.astype(F32) - 0.5 * dot(v, b["gl"][...]))).astype(BF)
        return carry

    lax.fori_loop(0, D // 128, left_step, 0)
    b["pl_own"][...] = left_scale * (1.5 * b["pl_own"][...] - 0.5 * dot(b["pl_b"][...], b["gl"][...]))
    g_t.step1()
    t_t.step1()
    g_t.step2()
    t_t.step2()
    g_t.step3()
    t_t.finish()

    def blend(j, carry):
        cut = pl.ds(pl.multiple_of(j * ROWS, 16), ROWS)
        v = -0.5625 * b["a_rows"][cut, :].astype(F32) + 0.0625 * b["t_rows"][cut, :].astype(F32)
        b["t_rows"][cut, :] = v.astype(BF)
        return carry

    net.drain()
    lax.fori_loop(0, 8, blend, 0)
    g_t.finish()

    rows_dot(b["t_rows"], b["t_cols"], b["w"])
    b["w_b"][...] = (b["w"][...] - 2.4375 * b["a"][...] + 1.6875 * b["t"][...]).astype(BF)
    g_w = shard("w_b", "w_cols")
    begin(g_w)
    left_gram(b["wl"], 1.0)
    mine = b["pl_own"][...]
    new_bl[...] = math.sqrt(D) * (1.5 * mine - 0.5 * dot(mine.astype(BF), b["gl"][...]))
    g_w.step1()
    g_w.step2()
    g_w.step3()
    g_w.finish()
    rows_dot(b["p_rows"], b["w_cols"], b["w"])
    new_br[...] = (math.sqrt(FF) * scale) * (2.25 * b["p"][...] + b["w"][...])
    net.drain()


def local(gradient, moment_one, moment_two, stat_left, stat_right, basis_left, basis_right):
    args = (gradient, moment_one, moment_two, stat_left, stat_right, basis_left, basis_right)
    outs = (gradient, moment_one, moment_two, stat_left, stat_right, basis_left, basis_right)
    vm = pl.BlockSpec(memory_space=pltpu.VMEM)
    return pl.pallas_call(
        kernel,
        out_shape=[jax.ShapeDtypeStruct(a.shape, a.dtype) for a in outs],
        in_specs=[vm] * 7,
        out_specs=[vm] * 7,
        scratch_shapes=[pltpu.VMEM(shape, dtype) for shape, dtype in BUFFERS.values()]
        + [
            pltpu.SemaphoreType.DMA((SEMS,)),
            pltpu.SemaphoreType.DMA((SEMS,)),
            pltpu.SemaphoreType.DMA((16,)),
        ],
        compiler_params=pltpu.CompilerParams(
            collective_id=0, has_side_effects=True, vmem_limit_bytes=60 * 2**20
        ),
        name="step",
    )(*args)


def solution(mesh):
    both, row = P("shard", "tensor"), P("shard", None)
    return jax.shard_map(
        local,
        mesh=mesh,
        in_specs=(both, both, both, row, both, row, both),
        out_specs=(both, both, both, row, both, row, both),
        check_vma=False,
    )
```

```python
import functools
import math

import jax
import jax.numpy as jnp
from jax import lax
from jax.experimental import pallas as pl
from jax.experimental.pallas import tpu as pltpu
from jax.sharding import PartitionSpec as P

D = 768
FF = 3072
BF = jnp.bfloat16
F32 = jnp.float32
MESH = pl.DeviceIdType.MESH

beta = 0.95
correction = 1.0 - 0.95**10
adam_eps = 1e-08


class Move:
    def __init__(self, copy, landing):
        self.copy, self.landing = copy, landing

    def recv(self):
        self.landing.wait_recv()


class Net:
    def __init__(self, send_sem, recv_sem):
        self.send_sem, self.recv_sem = send_sem, recv_sem
        self.count = 0
        self.sent = []
        s, t = lax.axis_index("shard"), lax.axis_index("tensor")
        self.s, self.t = s, t
        self.z, self.x = s // 4, s % 4
        self.y, self.c = t // 2, t % 2

    def nbr(self, d):
        s, t = self.s, self.t
        z, x, y, c = self.z, self.x, self.y, self.c
        if d == "c":
            return (s, y * 2 + 1 - c)
        step = 1 if d[0] == "+" else 3
        if d[1] == "x":
            return (z * 4 + (x + step) % 4, t)
        if d[1] == "z":
            return (((z + step) % 4) * 4 + x, t)
        return (s, ((y + step) % 4) * 2 + c)

    def barrier(self, dirs):
        sem = pltpu.get_barrier_semaphore()
        for d in dirs:
            pl.semaphore_signal(sem, inc=1, device_id=self.nbr(d), device_id_type=MESH)
        pl.semaphore_wait(sem, len(dirs))

    def send(self, src, dst, landing, d):
        k = self.count
        self.count += 1
        mk = lambda a, b: pltpu.make_async_remote_copy(
            src_ref=a,
            dst_ref=b,
            send_sem=self.send_sem.at[k],
            recv_sem=self.recv_sem.at[k],
            device_id=self.nbr(d),
            device_id_type=MESH,
        )
        copy = mk(src, dst)
        copy.start()
        self.sent.append(copy)
        return Move(copy, mk(landing, landing))

    def drain(self):
        for copy in self.sent:
            copy.wait_send()
        self.sent = []


def cuts(rows):
    if rows % 64 == 0:
        q = rows // 4
        return ((0, q, 2 * q), (2 * q, 3 * q, 4 * q))
    if rows == 48:
        return ((0, 16, 32), (32, 48, 48))
    return ((0, rows, rows), None)


class ShardGather:
    def __init__(self, net, src, buf):
        self.net, self.src, self.buf = net, src, buf
        self.flows = [(i, f) for i, f in enumerate(cuts(src.shape[0])) if f is not None]
        self.m = {}

    def view(self, blk, lo, hi):
        n, rows = self.net, self.src.shape[0]
        slot = (n.z + blk[0]) % 4 * 4 + (n.x + blk[1]) % 4
        return self.buf.at[pl.ds(pl.multiple_of(slot * rows + lo, 8), hi - lo), :]

    def axes(self, i):
        return ("x", "z") if i == 0 else ("z", "x")

    def rel(self, i, first, second):
        return (second, first) if i == 0 else (first, second)

    def go(self, i, stage, sgn, first, second, lo, hi, key, own=False):
        if hi == lo:
            return
        axis = self.axes(i)[stage]
        d = ("+" if sgn > 0 else "-") + axis
        blk = self.rel(i, first, second)
        lf, ls = (first - sgn, second) if stage == 0 else (first, second - sgn)
        src = self.src.at[pl.ds(lo, hi - lo), :] if own else self.view(blk, lo, hi)
        self.m[key] = self.net.send(src, self.view(blk, lo, hi), self.view(self.rel(i, lf, ls), lo, hi), d)

    def wait(self, *key):
        if key in self.m:
            self.m[key].recv()

    def start(self):
        n = self.net
        for i, (lo, mid, hi) in self.flows:
            for sgn in (1, -1):
                self.go(i, 0, sgn, 0, 0, lo, hi, (i, "a", sgn), own=True)
        for i, (lo, mid, hi) in self.flows:
            for sgn in (1, -1):
                self.go(i, 1, sgn, 0, 0, lo, hi, (i, "b", 0, sgn), own=True)

    def local(self, sem):
        n = self.net
        self.mine = pltpu.make_async_copy(self.src, self.view((0, 0), 0, self.src.shape[0]), sem)
        self.mine.start()

    def second(self, i, first, lo, hi):
        for sgn in (1, -1):
            self.go(i, 1, sgn, first, 0, lo, hi, (i, "b", first, sgn))

    def relay(self, i, first, lo, mid, hi):
        for sgn in (1, -1):
            self.wait(i, "b", first, sgn)
            a, b = (lo, mid) if sgn > 0 else (mid, hi)
            self.go(i, 1, sgn, first, -sgn, a, b, (i, "bb", first, sgn))

    def step1(self):
        for i, (lo, mid, hi) in self.flows:
            for sgn in (1, -1):
                self.wait(i, "a", sgn)
                a, b = (lo, mid) if sgn > 0 else (mid, hi)
                self.go(i, 0, sgn, -sgn, 0, a, b, (i, "aa", sgn))
                self.second(i, -sgn, lo, hi)

    def step2(self):
        for i, (lo, mid, hi) in self.flows:
            self.relay(i, 0, lo, mid, hi)
        for i, (lo, mid, hi) in self.flows:
            self.wait(i, "aa", 1)
            self.wait(i, "aa", -1)
            self.second(i, 2, lo, hi)

    def step3(self):
        for i, (lo, mid, hi) in self.flows:
            for first in (1, -1, 2):
                self.relay(i, first, lo, mid, hi)

    def finish(self):
        for i, _ in self.flows:
            for first in (0, 1, -1, 2):
                for sgn in (1, -1):
                    self.wait(i, "bb", first, sgn)
        self.mine.wait()


class TensorGather:
    def __init__(self, net, src, buf, wide=True):
        self.net, self.src, self.buf, self.wide = net, src, buf, wide
        rows = src.shape[0]
        self.cut = (0, rows // 32 * 16, rows)

    def view(self, dy, other, lo, hi):
        n, (rows, cols) = self.net, self.src.shape
        slot = (n.y + dy) % 4 * 2 + ((1 - n.c) if other else n.c)
        if self.wide:
            return self.buf.at[pl.ds(lo, hi - lo), pl.ds(pl.multiple_of(slot * cols, 128), cols)]
        return self.buf.at[pl.ds(pl.multiple_of(slot * rows + lo, 16), hi - lo), :]

    def start(self):
        n = self.net
        lo, mid, hi = self.cut
        own = lambda a, b: self.src.at[pl.ds(a, b - a), :]
        put = lambda a, b, sgn: n.send(
            own(a, b), self.view(0, 0, a, b), self.view(-sgn, 0, a, b), "+y" if sgn > 0 else "-y"
        )
        self.a = {1: put(lo, mid, 1), -1: put(mid, hi, -1)}
        self.rest = {1: put(mid, hi, 1), -1: put(lo, mid, -1)}
        self.sib = [n.send(self.src, self.view(0, 0, lo, hi), self.view(0, 1, lo, hi), "c")]

    def local(self, sem):
        self.mine = pltpu.make_async_copy(self.src, self.view(0, 0, 0, self.src.shape[0]), sem)
        self.mine.start()

    def pair(self, dy, lo, hi):
        n = self.net
        self.sib.append(n.send(self.view(dy, 0, lo, hi), self.view(dy, 0, lo, hi), self.view(dy, 1, lo, hi), "c"))

    def step1(self):
        n = self.net
        lo, mid, hi = self.cut
        self.aa = []
        for sgn in (1, -1):
            self.a[sgn].recv()
            a, b = (lo, mid) if sgn > 0 else (mid, hi)
            v = self.view(-sgn, 0, a, b)
            self.aa.append(n.send(v, v, self.view(2, 0, a, b), "+y" if sgn > 0 else "-y"))

    def step2(self):
        lo, mid, hi = self.cut
        for sgn in (1, -1):
            self.rest[sgn].recv()
            self.pair(-sgn, lo, hi)
        for m, (a, b) in zip(self.aa, ((lo, mid), (mid, hi))):
            m.recv()
            self.pair(2, a, b)

    def finish(self):
        for m in self.sib:
            m.recv()
        self.mine.wait()


def add_into(a, b):
    a[...] = (a[...].astype(F32) + b[...].astype(F32)).astype(a.dtype)


class RingScatter:
    def __init__(self, net, axis, pick, half, first, second):
        self.net, self.axis, self.pick, self.half = net, axis, pick, half
        self.first, self.second = first, second

    def start(self):
        n = self.net
        self.one = [
            n.send(self.half(self.pick(2), h), self.first[h], self.first[h], ("+", "-")[h] + self.axis) for h in (0, 1)
        ]

    def middle(self):
        n = self.net
        self.two = []
        for h, rel in ((0, 1), (1, -1)):
            self.one[h].recv()
            add_into(self.half(self.pick(rel), h), self.first[h])
            self.two.append(n.send(self.pick(rel), self.second[h], self.second[h], ("+", "-")[h] + self.axis))

    def total(self):
        for m in self.two:
            m.recv()
        own = self.pick(0)
        return own[...].astype(F32) + self.second[0][...].astype(F32) + self.second[1][...].astype(F32)


class LineBroadcast:
    def __init__(self, net, src, dst, lsem):
        self.net, self.src, self.dst, self.lsem = net, src, dst, lsem
        self.k = net.count
        net.count += 8
        self.dy = (net.y - net.z + 4) % 4
        self.main = net.c == net.x // 2
        h = src.shape[0] // 2
        lo, hi = pl.ds(0, h), pl.ds(h, h)
        self.kinds = [(lo, "+y"), (hi, "+y"), (hi, "-y"), (lo, "-y"), (lo, "+y"), (hi, "-y"), (lo, "c"), (hi, "c")]

    def msg(self, j, a=None):
        n = self.net
        cut, d = self.kinds[j]
        a = self.dst if a is None else a
        return pltpu.make_async_remote_copy(
            src_ref=a.at[cut, :],
            dst_ref=self.dst.at[cut, :],
            send_sem=n.send_sem.at[self.k + j],
            recv_sem=n.recv_sem.at[self.k + j],
            device_id=n.nbr(d),
            device_id_type=MESH,
        )

    def at(self, dy):
        return pl.when(jnp.logical_and(self.main, self.dy == dy))

    def start(self):
        @self.at(0)
        def _():
            for j in (0, 2, 1, 3, 6, 7):
                self.msg(j, self.src).start()
            pltpu.make_async_copy(self.src, self.dst, self.lsem).start()

    def middle(self):
        for dy, j, onward, half in ((1, 0, 4, 6), (3, 2, 5, 7)):

            @self.at(dy)
            def _(j=j, onward=onward, half=half):
                self.msg(j).wait_recv()
                self.msg(onward).start()
                self.msg(half).start()

    def finish(self):
        for dy, j, half in ((1, 1, 7), (3, 3, 6)):

            @self.at(dy)
            def _(j=j, half=half):
                self.msg(j).wait_recv()
                self.msg(half).start()

        @self.at(2)
        def _():
            for j, half in ((4, 6), (5, 7)):
                self.msg(j).wait_recv()
                self.msg(half).start()

        @pl.when(jnp.logical_not(self.main))
        def _():
            self.msg(6).wait_recv()
            self.msg(7).wait_recv()

        @self.at(0)
        def _():
            pltpu.make_async_copy(self.src, self.dst, self.lsem).wait()

    def drain(self):
        @self.at(0)
        def _():
            for j in range(4):
                self.msg(j, self.src).wait_send()

        for dy, onward in ((1, 4), (3, 5)):

            @self.at(dy)
            def _(onward=onward):
                self.msg(onward).wait_send()

        @pl.when(self.main)
        def _():
            self.msg(6).wait_send()
            self.msg(7).wait_send()


def plane_scatter(net, part, out, f1, f2, q, g1, g2):
    z, x = net.z, net.x
    h = part.shape[2] // 2
    zx = (z, x)
    stages = []
    for i in (0, 1):
        lo = i * h

        def pick(rel, i=i, lo=lo):
            if i == 0:
                return part.at[(z + rel) % 4, :, pl.ds(lo, h), :]
            return part.at[:, (x + rel) % 4, pl.ds(lo, h), :]

        def half(view, k):
            return view.at[pl.ds(2 * k, 2)]

        stages.append(RingScatter(net, "zx"[i], pick, half, [f1.at[i, 0], f1.at[i, 1]], [f2.at[i, 0], f2.at[i, 1]]))
    stages[0].start()
    yield
    stages[1].start()
    yield
    for r in stages:
        r.middle()
    yield
    later = []
    for i, r in enumerate(stages):
        q[i] = r.total().astype(q.dtype)

        def pick(rel, i=i):
            return q.at[i, (zx[1 - i] + rel) % 4]

        def half(view, k):
            return view.at[pl.ds(k * (h // 2), h // 2), :]

        later.append(RingScatter(net, "xz"[i], pick, half, [g1.at[i, 0], g1.at[i, 1]], [g2.at[i, 0], g2.at[i, 1]]))
        later[-1].start()
    yield
    for r in later:
        r.middle()
    yield
    for i, r in enumerate(later):
        out[pl.ds(i * h, h), :] = r.total()


def line_scatter(net, part, out, g0, q, g1, g2):
    y, c = net.y, net.c
    rows = part.shape[2]
    m = net.send(part.at[1 - c], g0, g0, "c")
    yield
    m.recv()
    q[...] = (part[c].astype(F32) + g0[...].astype(F32)).astype(q.dtype)
    cut = rows // 32 * 16

    def pick(rel):
        return q.at[(y + rel) % 4]

    def half(view, k):
        return view.at[pl.ds(0, cut), :] if k == 0 else view.at[pl.ds(cut, rows - cut), :]

    ring = RingScatter(net, "y", pick, half, [g1.at[pl.ds(0, cut)], g1.at[pl.ds(cut, rows - cut)]], [g2.at[0], g2.at[1]])
    ring.start()
    yield
    ring.middle()
    yield
    out[...] = ring.total().astype(out.dtype)


def dot(a, b):
    return jnp.dot(a, b, preferred_element_type=F32)


def dot_tn(a, b):
    return lax.dot_general(a, b, (((0,), (0,)), ((), ())), preferred_element_type=F32)


def dot_nt(a, b):
    return lax.dot_general(a, b, (((1,), (1,)), ((), ())), preferred_element_type=F32)


SEMS = 343
ROWS, COLS, LROWS = FF // 16, FF // 8, D // 16
BUFFERS = dict(
    lq=((LROWS, D), BF),
    rq=((ROWS, COLS), BF),
    gcols=((D, COLS), BF),
    lall=((D, D), BF),
    qcols=((FF, COLS), BF),
    gs_own=((D, ROWS), BF),
    gs=((D, ROWS), BF),
    lterms=((LROWS, D), BF),
    lparts=((8 * LROWS, D), BF),
    half_all=((D, COLS), BF),
    half_rows=((LROWS, FF), BF),
    s_b=((ROWS, COLS), BF),
    s_rows=((ROWS, FF), BF),
    p=((ROWS, COLS), F32),
    p_b=((ROWS, COLS), BF),
    p_rows=((ROWS, FF), BF),
    dir_b=((LROWS, COLS), BF),
    dir_cols=((D, COLS), BF),
    pl_own=((LROWS, D), F32),
    pl_b=((LROWS, D), BF),
    pl_all=((D, D), BF),
    gl=((D, D), BF),
    wl=((D, D), BF),
    tile=((8, 128), F32),
    tiles=((128, 128), F32),
    part=((4, 4, ROWS, COLS), BF),
    f1=((2, 2, 2, ROWS // 2, COLS), BF),
    f2=((2, 2, 4, ROWS // 2, COLS), BF),
    fq=((2, 4, ROWS // 2, COLS), BF),
    fg1=((2, 2, ROWS // 4, COLS), BF),
    fg2=((2, 2, ROWS // 2, COLS), BF),
    a=((ROWS, COLS), F32),
    a_b=((ROWS, COLS), BF),
    a_cols=((FF, COLS), BF),
    y1_b=((ROWS, COLS), BF),
    y1_rows=((ROWS, FF), BF),
    y2_b=((ROWS, COLS), BF),
    y2_rows=((ROWS, FF), BF),
    y3_b=((ROWS, COLS), BF),
    y3_rows=((ROWS, FF), BF),
    upart=((2, 4, LROWS, COLS), BF),
    u0=((4, LROWS, COLS), BF),
    uq=((4, LROWS, COLS), BF),
    u1=((LROWS, COLS), BF),
    u2=((2, LROWS, COLS), BF),
)
NBR = ("+x", "-x", "+z", "-z", "+y", "-y", "c")


def kernel(*refs):
    update, new_m1, new_m2, new_sl, new_sr, new_bl, new_br = refs[7:14]
    b = dict(zip(BUFFERS, refs[14 : 14 + len(BUFFERS)]))
    send_sem, recv_sem, lsem = refs[14 + len(BUFFERS) : 17 + len(BUFFERS)]
    inputs = refs[17 + len(BUFFERS) :]
    grad, m1, m2, stat_l, stat_r, basis_l, basis_r = inputs
    loads = [pltpu.make_async_copy(refs[k], inputs[k], lsem.at[16 + k]) for k in range(7)]
    for k in (0, 5, 6, 4, 3, 1, 2):
        loads[k].start()
    net = Net(send_sem, recv_sem)
    x, s = net.x, net.s
    own_left = pl.ds(pl.multiple_of(s * LROWS, 16), LROWS)
    lanes = lambda c: pl.ds(pl.multiple_of(c * (D // 2), 128), D // 2)
    locals_used = [0]

    def begin(*gathers):
        for g in gathers:
            g.start()
            g.local(lsem.at[locals_used[0]])
            locals_used[0] += 1

    def swap(ref):
        mine = ref.at[:, lanes(net.c)]
        return net.send(mine, mine, ref.at[:, lanes(1 - net.c)], "c")

    loads[5].wait()
    b["lq"][...] = (basis_l[...] * (1.0 / math.sqrt(D))).astype(BF)
    loads[6].wait()
    b["rq"][...] = (basis_r[...] * (1.0 / math.sqrt(FF))).astype(BF)
    for k in (0, 4, 3, 1, 2):
        loads[k].wait()
    net.barrier(NBR)

    g_grad = ShardGather(net, grad, b["gcols"])
    g_left = ShardGather(net, b["lq"].at[:, lanes(net.c)], b["lall"].at[:, lanes(net.c)])
    g_right = ShardGather(net, b["rq"], b["qcols"])
    begin(g_grad)
    g_grad.step1()
    begin(g_left)
    g_grad.step2()
    g_left.step1()
    begin(g_right)
    g_grad.step3()
    g_grad.finish()
    cast = LineBroadcast(net, b["gs_own"], b["gs"], lsem.at[locals_used[0]])
    locals_used[0] += 1
    pick = lax.broadcasted_iota(jnp.int32, (COLS, ROWS), 0) == lax.broadcasted_iota(
        jnp.int32, (COLS, ROWS), 1
    ) + ROWS * (x % 2)
    gcols = b["gcols"]
    b["gs_own"][...] = dot(gcols[...], jnp.where(pick, 1.0, 0.0).astype(BF)).astype(BF)
    cast.start()
    b["lterms"][...] = dot_nt(grad[...], gcols[...]).astype(BF)
    t_lterms = TensorGather(net, b["lterms"], b["lparts"], wide=False)
    begin(t_lterms)
    g_left.step2()
    g_right.step1()
    cast.middle()
    g_left.step3()
    cast.finish()

    new_sr[...] = beta * stat_r[...] + ((1.0 - beta) / D) * dot_tn(b["gs"][...], gcols[...])
    b["s_b"][...] = new_sr[...].astype(BF)
    t_stat = TensorGather(net, b["s_b"], b["s_rows"])
    begin(t_stat)
    g_left.finish()
    left_swap = swap(b["lall"])
    g_right.step2()
    t_stat.step1()
    t_lterms.step1()
    left_swap.recv()
    b["half_all"][...] = dot_tn(b["lall"][...], gcols[...]).astype(BF)
    t_half = TensorGather(net, b["half_all"].at[own_left, :], b["half_rows"])
    begin(t_half)
    g_right.step3()
    t_stat.step2()
    t_lterms.step2()
    t_half.step1()
    g_right.finish()
    t_stat.finish()
    b["p"][...] = dot(b["s_rows"][...], b["qcols"][...])
    b["p_b"][...] = b["p"][...].astype(BF)
    t_power = TensorGather(net, b["p_b"], b["p_rows"])
    begin(t_power)

    t_half.step2()
    t_lterms.finish()
    gram = b["lparts"][pl.ds(0, LROWS), :].astype(F32)
    for j in range(1, 8):
        gram += b["lparts"][pl.ds(j * LROWS, LROWS), :].astype(F32)
    new_sl[...] = beta * stat_l[...] + ((1.0 - beta) / FF) * gram
    b["pl_own"][...] = dot(new_sl[...].astype(BF), b["lall"][...])
    b["pl_b"][...] = b["pl_own"][...].astype(BF)
    t_half.finish()
    rot = dot(b["half_rows"][...], b["qcols"][...])
    first = beta * m1[...] + (1.0 - beta) * rot
    second = beta * m2[...] + (1.0 - beta) * (rot * rot)
    new_m1[...] = first
    new_m2[...] = second
    b["dir_b"][...] = ((first / correction) / (jnp.sqrt(second / correction) + adam_eps)).astype(BF)
    g_dir = ShardGather(net, b["dir_b"], b["dir_cols"])
    begin(g_dir)
    g_pl = ShardGather(net, b["pl_b"].at[:, lanes(net.c)], b["pl_all"].at[:, lanes(net.c)])
    begin(g_pl)
    t_power.step1()
    g_dir.step1()
    g_pl.step1()
    t_power.step2()
    g_dir.step2()
    g_pl.step2()
    t_power.finish()

    def term(rel):
        zt = (net.z + rel) % 4
        v = dot_tn(b["p_rows"][:, pl.ds(pl.multiple_of(zt * D, 128), D)], b["p_b"][...]).astype(BF)
        b["part"][zt] = v.reshape(4, ROWS, COLS)

    scatter = plane_scatter(net, b["part"], b["a"], b["f1"], b["f2"], b["fq"], b["fg1"], b["fg2"])
    term(2)
    next(scatter)
    for rel in (1, 3, 0):
        term(rel)
    next(scatter)
    g_dir.step3()
    g_pl.step3()

    def squares(j, total):
        v = b["p_rows"][pl.ds(pl.multiple_of(j * 16, 16), 16), :].astype(F32)
        return total + jnp.sum(v * v, axis=0, keepdims=True)

    total = lax.fori_loop(0, ROWS // 16, squares, jnp.zeros((1, FF), F32))
    b["tile"][...] = jnp.broadcast_to(jnp.sum(total, keepdims=True), (8, 128))
    g_tile = ShardGather(net, b["tile"], b["tiles"])
    begin(g_tile)
    next(scatter)
    g_tile.step1()
    next(scatter)
    g_tile.step2()
    next(scatter)
    g_tile.step3()
    for _ in scatter:
        pass
    g_tile.finish()
    norm = jnp.sum(b["tiles"][...], keepdims=True) / 1024.0
    scale = math.sqrt(FF) / (4.0 * jnp.sqrt(norm))
    b["a_b"][...] = (b["a"][...] * (scale * scale)).astype(BF)
    g_a = ShardGather(net, b["a_b"], b["a_cols"])
    begin(g_a)

    g_dir.finish()
    g_pl.finish()
    pl_swap = swap(b["pl_all"])
    back = dot(b["lq"][...], b["dir_cols"][...]).astype(BF)
    for j in range(8):
        b["upart"][j % 2, j // 2] = dot_nt(back, b["qcols"][pl.ds(j * COLS, COLS), :]).astype(BF)
    to_update = line_scatter(net, b["upart"], update, b["u0"], b["uq"], b["u1"], b["u2"])
    next(to_update)
    g_a.step1()
    next(to_update)

    pl_swap.recv()

    def left_squares(j, total):
        v = b["pl_all"][pl.ds(pl.multiple_of(j * 16, 16), 16), :].astype(F32)
        return total + jnp.sum(v * v, axis=0, keepdims=True)

    left_total = lax.fori_loop(0, D // 16, left_squares, jnp.zeros((1, D), F32))
    left_scale = math.sqrt(D) / (4.0 * jnp.sqrt(jnp.sum(left_total, keepdims=True)))

    def left_gram(ref, factor, lo, hi):
        for j in range(lo, hi):
            cut = pl.ds(j * 128, 128)
            b["gl"][cut, :] = (dot_tn(ref[:, cut], ref[...]) * factor).astype(BF)

    left_gram(b["pl_all"], left_scale * left_scale, 0, 6)
    g_a.step2()
    next(to_update)
    g_a.step3()
    g_a.finish()

    def mix(rows, factor, add, out, all_rows):
        v = dot(b[rows][...], b["a_cols"][...])
        b[out][...] = ((factor * v if factor != 1.0 else v) + add * b["p"][...]).astype(BF)
        g = TensorGather(net, b[out], b[all_rows])
        begin(g)
        return g

    t_y = mix("p_rows", 0.0625, -0.5625, "y1_b", "y1_rows")
    for _ in to_update:
        pass
    t_y.step1()
    for j in range(3):
        cut = pl.ds(j * 256, 256)
        v = b["pl_all"][cut, :]
        b["wl"][cut, :] = (left_scale * (1.5 * v.astype(F32) - 0.5 * dot(v, b["gl"][...]))).astype(BF)
    mine = left_scale * (1.5 * b["pl_own"][...] - 0.5 * dot(b["pl_b"][...], b["gl"][...]))
    b["pl_own"][...] = mine
    t_y.step2()
    t_y.finish()
    t_y = mix("y1_rows", 1.0, 1.6875, "y2_b", "y2_rows")
    left_gram(b["wl"], 1.0, 0, 3)
    t_y.step1()
    left_gram(b["wl"], 1.0, 3, 6)
    t_y.step2()
    t_y.finish()
    t_y = mix("y2_rows", 1.0, -2.4375, "y3_b", "y3_rows")
    mine = b["pl_own"][...]
    new_bl[...] = math.sqrt(D) * (1.5 * mine - 0.5 * dot(mine.astype(BF), b["gl"][...]))
    t_y.step1()
    t_y.step2()
    t_y.finish()
    v = dot(b["y3_rows"][...], b["a_cols"][...])
    new_br[...] = (math.sqrt(FF) * scale) * (2.25 * b["p"][...] + v)
    assert net.count <= SEMS and locals_used[0] <= 16
    cast.drain()
    net.drain()


def emit(*refs):
    for a, o in zip(refs[:7], refs[7:]):
        o[...] = a[...]


def local(gradient, moment_one, moment_two, stat_left, stat_right, basis_left, basis_right):
    args = (gradient, moment_one, moment_two, stat_left, stat_right, basis_left, basis_right)
    vm = pl.BlockSpec(memory_space=pltpu.VMEM)
    out = pl.pallas_call(
        kernel,
        out_shape=[jax.ShapeDtypeStruct(a.shape, a.dtype) for a in args],
        in_specs=[pl.BlockSpec(memory_space=pl.ANY)] * 7,
        out_specs=[vm] * 7,
        scratch_shapes=[pltpu.VMEM(shape, dtype) for shape, dtype in BUFFERS.values()]
        + [
            pltpu.SemaphoreType.DMA((SEMS,)),
            pltpu.SemaphoreType.DMA((SEMS,)),
            pltpu.SemaphoreType.DMA((23,)),
        ]
        + [pltpu.VMEM(a.shape, a.dtype) for a in args],
        compiler_params=pltpu.CompilerParams(
            collective_id=0, has_side_effects=True, vmem_limit_bytes=63 * 2**20
        ),
        name="step",
    )(*args)
    return pl.pallas_call(
        emit,
        out_shape=[jax.ShapeDtypeStruct(a.shape, a.dtype) for a in args],
        in_specs=[vm] * 7,
        out_specs=[vm] * 7,
        compiler_params=pltpu.CompilerParams(vmem_limit_bytes=63 * 2**20),
        name="emit",
    )(*out)


def solution(mesh):
    both, row = P("shard", "tensor"), P("shard", None)
    return jax.shard_map(
        local,
        mesh=mesh,
        in_specs=(both, both, both, row, both, row, both),
        out_specs=(both, both, both, row, both, row, both),
        check_vma=False,
    )
```

```python
import functools
import math

import jax
import jax.numpy as jnp
from jax import lax
from jax.experimental import pallas as pl
from jax.experimental.pallas import tpu as pltpu
from jax.sharding import PartitionSpec as P

D = 768
FF = 3072
BF = jnp.bfloat16
F32 = jnp.float32
MESH = pl.DeviceIdType.MESH

beta = 0.95
correction = 1.0 - 0.95**10
adam_eps = 1e-08


class Move:
    def __init__(self, landing):
        self.landing = landing

    def recv(self):
        self.landing.wait_recv()


class Slots:
    def __init__(self, first, count):
        self.first, self.count, self.used = first, count, 0

    def next(self):
        self.used += 1
        assert self.used <= self.count
        return self.first + self.used - 1

    def again(self):
        return Slots(self.first, self.count)


class Net:
    def __init__(self, send_sem, recv_sem):
        self.send_sem, self.recv_sem = send_sem, recv_sem
        self.count = 0
        self.taken = 0
        self.sent = {}
        s, t = lax.axis_index("shard"), lax.axis_index("tensor")
        self.s, self.t = s, t
        self.z, self.x = s // 4, s % 4
        self.y, self.c = t // 2, t % 2

    def take(self, count):
        self.taken += count
        return Slots(self.taken - count, count)

    def nbr(self, d):
        s, t = self.s, self.t
        z, x, y, c = self.z, self.x, self.y, self.c
        if d == "c":
            return (s, y * 2 + 1 - c)
        step = {"+": 1, "2": 2, "-": 3}[d[0]]
        if d[1] == "x":
            return (z * 4 + (x + step) % 4, t)
        if d[1] == "z":
            return (((z + step) % 4) * 4 + x, t)
        return (s, ((y + step) % 4) * 2 + c)

    def greet(self, dirs):
        sem = pltpu.get_barrier_semaphore()
        for d in dirs:
            pl.semaphore_signal(sem, inc=1, device_id=self.nbr(d), device_id_type=MESH)

    def meet(self, dirs):
        pl.semaphore_wait(pltpu.get_barrier_semaphore(), len(dirs))

    def send(self, src, dst, landing, d, slots):
        k, r = self.count % POOL, slots.next()
        self.count += 1
        if k in self.sent:
            self.sent[k].wait_send()
        mk = lambda a, b: pltpu.make_async_remote_copy(
            src_ref=a,
            dst_ref=b,
            send_sem=self.send_sem.at[k],
            recv_sem=self.recv_sem.at[r],
            device_id=self.nbr(d),
            device_id_type=MESH,
        )
        self.sent[k] = mk(src, dst)
        self.sent[k].start()
        return Move(mk(landing, landing))

    def drain(self):
        for copy in self.sent.values():
            copy.wait_send()
        self.sent = {}


def cuts(rows):
    if rows % 64 == 0:
        q = rows // 4
        return ((0, q, 2 * q), (2 * q, 3 * q, 4 * q))
    if rows == 48:
        return ((0, 16, 32), (32, 48, 48))
    return ((0, rows, rows), None)


class ShardGather:
    def __init__(self, net, src, buf, direct=False, slots=None):
        self.net, self.src, self.buf, self.direct = net, src, buf, direct
        self.flows = [(i, f) for i, f in enumerate(cuts(src.shape[0])) if f is not None]
        self.m = {}
        self.slots = slots or net.take(40 if self.flows[-1][0] else 20)

    def view(self, blk, lo, hi):
        n, rows = self.net, self.src.shape[0]
        slot = (n.z + blk[0]) % 4 * 4 + (n.x + blk[1]) % 4
        return self.buf.at[pl.ds(pl.multiple_of(slot * rows + lo, 8), hi - lo), :]

    def axes(self, i):
        return ("x", "z") if i == 0 else ("z", "x")

    def rel(self, i, first, second):
        return (second, first) if i == 0 else (first, second)

    def go(self, i, stage, sgn, first, second, lo, hi, key, own=False):
        if hi == lo:
            return
        axis = self.axes(i)[stage]
        d = ("+" if sgn > 0 else "-") + axis
        blk = self.rel(i, first, second)
        lf, ls = (first - sgn, second) if stage == 0 else (first, second - sgn)
        src = self.src.at[pl.ds(lo, hi - lo), :] if own else self.view(blk, lo, hi)
        self.m[key] = self.net.send(src, self.view(blk, lo, hi), self.view(self.rel(i, lf, ls), lo, hi), d, self.slots)

    def wait(self, *key):
        if key in self.m:
            self.m[key].recv()

    def start(self):
        n = self.net
        for i, (lo, mid, hi) in self.flows:
            for sgn in (1, -1):
                self.go(i, 0, sgn, 0, 0, lo, hi, (i, "a", sgn), own=True)
            if self.direct:
                src = self.src.at[pl.ds(lo, hi - lo), :]
                landing = self.view(self.rel(i, 2, 0), lo, hi)
                self.m[i, "aa", 1] = n.send(src, self.view((0, 0), lo, hi), landing, "2" + self.axes(i)[0], self.slots)
        for i, (lo, mid, hi) in self.flows:
            for sgn in (1, -1):
                self.go(i, 1, sgn, 0, 0, lo, hi, (i, "b", 0, sgn), own=True)

    def local(self, sem):
        n = self.net
        self.mine = pltpu.make_async_copy(self.src, self.view((0, 0), 0, self.src.shape[0]), sem)
        self.mine.start()

    def second(self, i, first, lo, hi):
        for sgn in (1, -1):
            self.go(i, 1, sgn, first, 0, lo, hi, (i, "b", first, sgn))

    def relay(self, i, first, lo, mid, hi):
        for sgn in (1, -1):
            self.wait(i, "b", first, sgn)
            a, b = (lo, mid) if sgn > 0 else (mid, hi)
            self.go(i, 1, sgn, first, -sgn, a, b, (i, "bb", first, sgn))

    def step1(self):
        for i, (lo, mid, hi) in self.flows:
            for sgn in (1, -1):
                self.wait(i, "a", sgn)
                a, b = (lo, mid) if sgn > 0 else (mid, hi)
                if not self.direct:
                    self.go(i, 0, sgn, -sgn, 0, a, b, (i, "aa", sgn))
                self.second(i, -sgn, lo, hi)

    def step2(self):
        for i, (lo, mid, hi) in self.flows:
            self.relay(i, 0, lo, mid, hi)
        for i, (lo, mid, hi) in self.flows:
            self.wait(i, "aa", 1)
            self.wait(i, "aa", -1)
            self.second(i, 2, lo, hi)

    def step3(self):
        for i, (lo, mid, hi) in self.flows:
            for first in (1, -1, 2):
                self.relay(i, first, lo, mid, hi)

    def finish(self):
        for i, _ in self.flows:
            for first in (0, 1, -1, 2):
                for sgn in (1, -1):
                    self.wait(i, "bb", first, sgn)
        self.mine.wait()


class TensorGather:
    def __init__(self, net, src, buf, wide=True, slots=None):
        self.net, self.src, self.buf, self.wide = net, src, buf, wide
        self.slots = slots or net.take(11)
        rows = src.shape[0]
        self.cut = (0, rows // 32 * 16, rows)

    def view(self, dy, other, lo, hi):
        n, (rows, cols) = self.net, self.src.shape
        slot = (n.y + dy) % 4 * 2 + ((1 - n.c) if other else n.c)
        if self.wide:
            return self.buf.at[pl.ds(lo, hi - lo), pl.ds(pl.multiple_of(slot * cols, 128), cols)]
        return self.buf.at[pl.ds(pl.multiple_of(slot * rows + lo, 16), hi - lo), :]

    def start(self):
        n = self.net
        lo, mid, hi = self.cut
        own = lambda a, b: self.src.at[pl.ds(a, b - a), :]
        put = lambda a, b, sgn: n.send(
            own(a, b), self.view(0, 0, a, b), self.view(-sgn, 0, a, b), "+y" if sgn > 0 else "-y", self.slots
        )
        self.a = {1: put(lo, mid, 1), -1: put(mid, hi, -1)}
        self.rest = {1: put(mid, hi, 1), -1: put(lo, mid, -1)}
        self.sib = [n.send(self.src, self.view(0, 0, lo, hi), self.view(0, 1, lo, hi), "c", self.slots)]

    def local(self, sem):
        self.mine = pltpu.make_async_copy(self.src, self.view(0, 0, 0, self.src.shape[0]), sem)
        self.mine.start()

    def pair(self, dy, lo, hi):
        n = self.net
        self.sib.append(n.send(self.view(dy, 0, lo, hi), self.view(dy, 0, lo, hi), self.view(dy, 1, lo, hi), "c", self.slots))

    def step1(self):
        n = self.net
        lo, mid, hi = self.cut
        self.aa = []
        for sgn in (1, -1):
            self.a[sgn].recv()
            a, b = (lo, mid) if sgn > 0 else (mid, hi)
            v = self.view(-sgn, 0, a, b)
            self.aa.append(n.send(v, v, self.view(2, 0, a, b), "+y" if sgn > 0 else "-y", self.slots))

    def step2(self):
        lo, mid, hi = self.cut
        for sgn in (1, -1):
            self.rest[sgn].recv()
            self.pair(-sgn, lo, hi)
        for m, (a, b) in zip(self.aa, ((lo, mid), (mid, hi))):
            m.recv()
            self.pair(2, a, b)

    def finish(self):
        for m in self.sib:
            m.recv()
        self.mine.wait()


def add_into(a, b):
    a[...] = (a[...].astype(F32) + b[...].astype(F32)).astype(a.dtype)


class RingScatter:
    def __init__(self, net, axis, pick, half, first, second):
        self.net, self.axis, self.pick, self.half = net, axis, pick, half
        self.first, self.second = first, second
        self.slots = net.take(6)

    def start(self):
        n = self.net
        way = lambda h: ("+", "-")[h] + self.axis
        self.one = [n.send(self.half(self.pick(2), h), self.first[h], self.first[h], way(h), self.slots) for h in (0, 1)]

    def near(self):
        n = self.net
        way = lambda h: ("+", "-")[h] + self.axis
        self.two = []
        for h, rel in ((0, 1), (1, -1)):
            dst = self.half(self.second[h], 1 - h)
            self.two.append(n.send(self.half(self.pick(rel), 1 - h), dst, dst, way(h), self.slots))

    def middle(self):
        n = self.net
        for h, rel in ((0, 1), (1, -1)):
            self.one[h].recv()
            add_into(self.half(self.pick(rel), h), self.first[h])
            dst = self.half(self.second[h], h)
            self.two.append(n.send(self.half(self.pick(rel), h), dst, dst, ("+", "-")[h] + self.axis, self.slots))

    def total(self):
        for m in self.two:
            m.recv()
        own = self.pick(0)
        return own[...].astype(F32) + self.second[0][...].astype(F32) + self.second[1][...].astype(F32)


class LineBroadcast:
    def __init__(self, net, src, dst, lsem):
        self.net, self.src, self.dst, self.lsem = net, src, dst, lsem
        self.slots = net.take(8)
        self.dy = (net.y - net.z + 4) % 4
        self.main = net.c == net.x // 2
        h = src.shape[0] // 2
        lo, hi = pl.ds(0, h), pl.ds(h, h)
        self.kinds = [(lo, "+y"), (hi, "+y"), (hi, "-y"), (lo, "-y"), (lo, "+y"), (hi, "-y"), (lo, "c"), (hi, "c")]

    def msg(self, j, a=None):
        n = self.net
        cut, d = self.kinds[j]
        a = self.dst if a is None else a
        return pltpu.make_async_remote_copy(
            src_ref=a.at[cut, :],
            dst_ref=self.dst.at[cut, :],
            send_sem=n.send_sem.at[POOL + j],
            recv_sem=n.recv_sem.at[self.slots.first + j],
            device_id=n.nbr(d),
            device_id_type=MESH,
        )

    def at(self, dy):
        return pl.when(jnp.logical_and(self.main, self.dy == dy))

    def start(self):
        @self.at(0)
        def _():
            for j in (0, 2, 1, 3, 6, 7):
                self.msg(j, self.src).start()
            pltpu.make_async_copy(self.src, self.dst, self.lsem).start()

    def middle(self):
        for dy, j, onward, half in ((1, 0, 4, 6), (3, 2, 5, 7)):

            @self.at(dy)
            def _(j=j, onward=onward, half=half):
                self.msg(j).wait_recv()
                self.msg(onward).start()
                self.msg(half).start()

    def finish(self):
        for dy, j, half in ((1, 1, 7), (3, 3, 6)):

            @self.at(dy)
            def _(j=j, half=half):
                self.msg(j).wait_recv()
                self.msg(half).start()

        @self.at(2)
        def _():
            for j, half in ((4, 6), (5, 7)):
                self.msg(j).wait_recv()
                self.msg(half).start()

        @pl.when(jnp.logical_not(self.main))
        def _():
            self.msg(6).wait_recv()
            self.msg(7).wait_recv()

        @self.at(0)
        def _():
            pltpu.make_async_copy(self.src, self.dst, self.lsem).wait()

    def drain(self):
        @self.at(0)
        def _():
            for j in range(4):
                self.msg(j, self.src).wait_send()

        for dy, onward in ((1, 4), (3, 5)):

            @self.at(dy)
            def _(onward=onward):
                self.msg(onward).wait_send()

        @pl.when(self.main)
        def _():
            self.msg(6).wait_send()
            self.msg(7).wait_send()


def plane_scatter(net, part, out, f1, f2, q, g1, g2):
    z, x = net.z, net.x
    h = part.shape[2] // 2
    zx = (z, x)
    stages = []
    for i in (0, 1):
        lo = i * h

        def pick(rel, i=i, lo=lo):
            if i == 0:
                return part.at[(z + rel) % 4, :, pl.ds(lo, h), :]
            return part.at[:, (x + rel) % 4, pl.ds(lo, h), :]

        def half(view, k):
            return view.at[pl.ds(2 * k, 2)]

        stages.append(RingScatter(net, "zx"[i], pick, half, [f1.at[i, 0], f1.at[i, 1]], [f2.at[i, 0], f2.at[i, 1]]))
    stages[0].start()
    yield
    stages[0].near()
    yield
    stages[1].start()
    stages[1].near()
    yield
    for r in stages:
        r.middle()
    yield
    later = []
    for i, r in enumerate(stages):
        q[i] = r.total().astype(q.dtype)

        def pick(rel, i=i):
            return q.at[i, (zx[1 - i] + rel) % 4]

        def half(view, k):
            return view.at[pl.ds(k * (h // 2), h // 2), :]

        later.append(RingScatter(net, "xz"[i], pick, half, [g1.at[i, 0], g1.at[i, 1]], [g2.at[i, 0], g2.at[i, 1]]))
        later[-1].start()
        later[-1].near()
    yield
    for r in later:
        r.middle()
    yield
    for i, r in enumerate(later):
        out[pl.ds(i * h, h), :] = r.total()


def line_scatter(net, part, out, g0, q, g1, g2):
    y, c = net.y, net.c
    rows = part.shape[2]
    m = net.send(part.at[1 - c], g0, g0, "c", net.take(1))
    yield
    m.recv()
    q[...] = (part[c].astype(F32) + g0[...].astype(F32)).astype(q.dtype)
    cut = rows // 32 * 16

    def pick(rel):
        return q.at[(y + rel) % 4]

    def half(view, k):
        return view.at[pl.ds(0, cut), :] if k == 0 else view.at[pl.ds(cut, rows - cut), :]

    ring = RingScatter(net, "y", pick, half, [g1.at[pl.ds(0, cut)], g1.at[pl.ds(cut, rows - cut)]], [g2.at[0], g2.at[1]])
    ring.start()
    ring.near()
    yield
    ring.middle()
    yield
    out[...] = ring.total().astype(out.dtype)


def dot(a, b):
    return jnp.dot(a, b, preferred_element_type=F32)


def dot_tn(a, b):
    return lax.dot_general(a, b, (((0,), (0,)), ((), ())), preferred_element_type=F32)


def dot_nt(a, b):
    return lax.dot_general(a, b, (((1,), (1,)), ((), ())), preferred_element_type=F32)


SEMS, POOL = 268, 72
ROWS, COLS, LROWS = FF // 16, FF // 8, D // 16
BUFFERS = dict(
    lq=((LROWS, D), BF),
    rq=((ROWS, COLS), BF),
    gcols=((D, COLS), BF),
    lall=((D, D), BF),
    qcols=((FF, COLS), BF),
    gs_own=((D, ROWS), BF),
    gs=((D, ROWS), BF),
    lterms=((LROWS, D), BF),
    lparts=((8 * LROWS, D), BF),
    half_all=((D, COLS), BF),
    half_rows=((LROWS, FF), BF),
    s_b=((ROWS, COLS), BF),
    s_rows=((ROWS, FF), BF),
    p=((ROWS, COLS), F32),
    p_b=((ROWS, COLS), BF),
    p_rows=((ROWS, FF), BF),
    dir_b=((LROWS, COLS), BF),
    dir_cols=((D, COLS), BF),
    pl_own=((LROWS, D), F32),
    pl_b=((LROWS, D), BF),
    pl_all=((D, D), BF),
    gl=((D, D), BF),
    wl=((D, D), BF),
    tile=((8, 128), F32),
    tiles=((128, 128), F32),
    part=((4, 4, ROWS, COLS), BF),
    f1=((2, 2, 2, ROWS // 2, COLS), BF),
    f2=((2, 2, 4, ROWS // 2, COLS), BF),
    fq=((2, 4, ROWS // 2, COLS), BF),
    fg1=((2, 2, ROWS // 4, COLS), BF),
    fg2=((2, 2, ROWS // 2, COLS), BF),
    a=((ROWS, COLS), F32),
    a_b=((ROWS, COLS), BF),
    a_cols=((FF, COLS), BF),
    y1_b=((ROWS, COLS), BF),
    y1_rows=((ROWS, FF), BF),
    y2_b=((ROWS, COLS), BF),
    y2_rows=((ROWS, FF), BF),
    y3_b=((ROWS, COLS), BF),
    y3_rows=((ROWS, FF), BF),
    upart=((2, 4, LROWS, COLS), BF),
    u0=((4, LROWS, COLS), BF),
    uq=((4, LROWS, COLS), BF),
    u1=((LROWS, COLS), BF),
    u2=((2, LROWS, COLS), BF),
)
NBR = ("+x", "-x", "2x", "+z", "-z", "2z", "+y", "-y", "c")


def kernel(*refs):
    b = dict(zip(BUFFERS, refs[14 : 14 + len(BUFFERS)]))
    send_sem, recv_sem, lsem = refs[14 + len(BUFFERS) : 17 + len(BUFFERS)]
    inputs, outputs = refs[17 + len(BUFFERS) : 24 + len(BUFFERS)], refs[24 + len(BUFFERS) :]
    update, new_m1, new_m2, new_sl, new_sr, new_bl, new_br = outputs
    stores = [pltpu.make_async_copy(outputs[k], refs[7 + k], lsem.at[23 + k]) for k in range(7)]
    grad, m1, m2, stat_l, stat_r, basis_l, basis_r = inputs
    loads = [pltpu.make_async_copy(refs[k], inputs[k], lsem.at[16 + k]) for k in range(7)]
    for k in (0, 5, 6, 4, 3, 1, 2):
        loads[k].start()
    net = Net(send_sem, recv_sem)
    x, s = net.x, net.s
    own_left = pl.ds(pl.multiple_of(s * LROWS, 16), LROWS)
    lanes = lambda c: pl.ds(pl.multiple_of(c * (D // 2), 128), D // 2)
    locals_used = [0]

    def begin(*gathers):
        for g in gathers:
            g.start()
            g.local(lsem.at[locals_used[0]])
            locals_used[0] += 1

    def swap(ref):
        mine = ref.at[:, lanes(net.c)]
        return net.send(mine, mine, ref.at[:, lanes(1 - net.c)], "c", net.take(1))

    net.greet(NBR)
    loads[0].wait()
    net.meet(NBR)

    g_grad = ShardGather(net, grad, b["gcols"], direct=True)
    begin(g_grad)
    loads[5].wait()
    b["lq"][...] = (basis_l[...] * (1.0 / math.sqrt(D))).astype(BF)
    loads[6].wait()
    b["rq"][...] = (basis_r[...] * (1.0 / math.sqrt(FF))).astype(BF)
    for k in (4, 3, 1, 2):
        loads[k].wait()
    g_left = ShardGather(net, b["lq"].at[:, lanes(net.c)], b["lall"].at[:, lanes(net.c)])
    g_right = ShardGather(net, b["rq"], b["qcols"])
    g_grad.step1()
    begin(g_left)
    g_grad.step2()
    g_left.step1()
    g_grad.step3()
    begin(g_right)
    g_left.step2()
    g_grad.finish()
    cast = LineBroadcast(net, b["gs_own"], b["gs"], lsem.at[locals_used[0]])
    locals_used[0] += 1
    pick = lax.broadcasted_iota(jnp.int32, (COLS, ROWS), 0) == lax.broadcasted_iota(
        jnp.int32, (COLS, ROWS), 1
    ) + ROWS * (x % 2)
    gcols = b["gcols"]
    b["gs_own"][...] = dot(gcols[...], jnp.where(pick, 1.0, 0.0).astype(BF)).astype(BF)
    cast.start()
    b["lterms"][...] = dot_nt(grad[...], gcols[...]).astype(BF)
    t_lterms = TensorGather(net, b["lterms"], b["lparts"], wide=False)
    begin(t_lterms)
    g_right.step1()
    cast.middle()
    g_left.step3()
    t_lterms.step1()
    g_right.step2()
    cast.finish()

    new_sr[...] = beta * stat_r[...] + ((1.0 - beta) / D) * dot_tn(b["gs"][...], gcols[...])
    b["s_b"][...] = new_sr[...].astype(BF)
    t_stat = TensorGather(net, b["s_b"], b["s_rows"])
    begin(t_stat)
    stores[4].start()
    g_left.finish()
    left_swap = swap(b["lall"])
    t_lterms.step2()
    g_right.step3()
    t_stat.step1()
    left_swap.recv()
    t_lterms.finish()
    gram = b["lparts"][pl.ds(0, LROWS), :].astype(F32)
    for j in range(1, 8):
        gram += b["lparts"][pl.ds(j * LROWS, LROWS), :].astype(F32)
    new_sl[...] = beta * stat_l[...] + ((1.0 - beta) / FF) * gram
    b["pl_own"][...] = dot(new_sl[...].astype(BF), b["lall"][...])
    b["pl_b"][...] = b["pl_own"][...].astype(BF)
    g_pl = ShardGather(net, b["pl_b"].at[:, lanes(net.c)], b["pl_all"].at[:, lanes(net.c)])
    begin(g_pl)
    stores[3].start()
    b["half_all"][...] = dot_tn(b["lall"][...], gcols[...]).astype(BF)
    t_half = TensorGather(net, b["half_all"].at[own_left, :], b["half_rows"])
    t_stat.step2()
    begin(t_half)
    g_right.finish()
    t_stat.finish()
    b["p"][...] = dot(b["s_rows"][...], b["qcols"][...])
    b["p_b"][...] = b["p"][...].astype(BF)
    t_power = TensorGather(net, b["p_b"], b["p_rows"])
    begin(t_power)
    g_pl.step1()
    t_half.step1()
    t_power.step1()
    g_pl.step2()
    t_half.step2()
    t_power.step2()
    g_pl.step3()
    t_power.finish()

    def term(rel):
        zt = (net.z + rel) % 4
        v = dot_tn(b["p_rows"][:, pl.ds(pl.multiple_of(zt * D, 128), D)], b["p_b"][...]).astype(BF)
        b["part"][zt] = v.reshape(4, ROWS, COLS)

    scatter = plane_scatter(net, b["part"], b["a"], b["f1"], b["f2"], b["fq"], b["fg1"], b["fg2"])
    term(2)
    next(scatter)
    term(1)
    term(3)
    next(scatter)
    term(0)
    next(scatter)

    def squares(j, total):
        v = b["p_rows"][pl.ds(pl.multiple_of(j * 16, 16), 16), :].astype(F32)
        return total + jnp.sum(v * v, axis=0, keepdims=True)

    total = lax.fori_loop(0, ROWS // 16, squares, jnp.zeros((1, FF), F32))
    b["tile"][...] = jnp.broadcast_to(jnp.sum(total, keepdims=True), (8, 128))
    g_tile = ShardGather(net, b["tile"], b["tiles"])
    begin(g_tile)
    t_half.finish()
    rot = dot(b["half_rows"][...], b["qcols"][...])
    first = beta * m1[...] + (1.0 - beta) * rot
    second = beta * m2[...] + (1.0 - beta) * (rot * rot)
    new_m1[...] = first
    new_m2[...] = second
    stores[1].start()
    stores[2].start()
    b["dir_b"][...] = ((first / correction) / (jnp.sqrt(second / correction) + adam_eps)).astype(BF)
    next(scatter)
    g_pl.finish()
    pl_swap = swap(b["pl_all"])
    pl_swap.recv()

    def left_squares(j, total):
        v = b["pl_all"][pl.ds(pl.multiple_of(j * 16, 16), 16), :].astype(F32)
        return total + jnp.sum(v * v, axis=0, keepdims=True)

    def left_gram(ref, factor, lo, hi):
        for j in range(lo, hi):
            cut = pl.ds(j * 128, 128)
            b["gl"][cut, :] = (dot_tn(ref[:, cut], ref[...]) * factor).astype(BF)

    left_total = lax.fori_loop(0, D // 16, left_squares, jnp.zeros((1, D), F32))
    left_scale = math.sqrt(D) / (4.0 * jnp.sqrt(jnp.sum(left_total, keepdims=True)))
    left_gram(b["pl_all"], left_scale * left_scale, 0, 4)
    g_tile.step1()
    next(scatter)
    g_tile.step2()
    left_gram(b["pl_all"], left_scale * left_scale, 4, 5)
    next(scatter)
    g_tile.step3()
    left_gram(b["pl_all"], left_scale * left_scale, 5, 6)
    for _ in scatter:
        pass
    g_tile.finish()
    norm = jnp.sum(b["tiles"][...], keepdims=True) / 1024.0
    scale = math.sqrt(FF) / (4.0 * jnp.sqrt(norm))
    b["a_b"][...] = (b["a"][...] * (scale * scale)).astype(BF)
    g_a = ShardGather(net, b["a_b"], b["a_cols"], slots=g_right.slots.again())
    begin(g_a)
    for j in range(3):
        cut = pl.ds(j * 256, 256)
        v = b["pl_all"][cut, :]
        b["wl"][cut, :] = (left_scale * (1.5 * v.astype(F32) - 0.5 * dot(v, b["gl"][...]))).astype(BF)
    mine = left_scale * (1.5 * b["pl_own"][...] - 0.5 * dot(b["pl_b"][...], b["gl"][...]))
    g_a.step1()
    left_gram(b["wl"], 1.0, 0, 5)
    g_a.step2()
    left_gram(b["wl"], 1.0, 5, 6)
    new_bl[...] = math.sqrt(D) * (1.5 * mine - 0.5 * dot(mine.astype(BF), b["gl"][...]))
    stores[5].start()
    g_a.step3()
    g_dir = ShardGather(net, b["dir_b"], b["dir_cols"], slots=g_left.slots.again())
    begin(g_dir)
    g_a.finish()

    def mix(rows, factor, add, out, all_rows, before):
        v = dot(b[rows][...], b["a_cols"][...])
        b[out][...] = ((factor * v if factor != 1.0 else v) + add * b["p"][...]).astype(BF)
        g = TensorGather(net, b[out], b[all_rows], slots=before.slots.again())
        begin(g)
        return g

    t_y = mix("p_rows", 0.0625, -0.5625, "y1_b", "y1_rows", t_stat)
    g_dir.step1()
    t_y.step1()
    g_dir.step2()
    t_y.step2()
    g_dir.step3()
    t_y.finish()
    t_y = mix("y1_rows", 1.0, 1.6875, "y2_b", "y2_rows", t_power)
    t_y.step1()
    g_dir.finish()
    back = dot(b["lq"][...], b["dir_cols"][...]).astype(BF)
    for j in range(8):
        b["upart"][j % 2, j // 2] = dot_nt(back, b["qcols"][pl.ds(j * COLS, COLS), :]).astype(BF)
    to_update = line_scatter(net, b["upart"], update, b["u0"], b["uq"], b["u1"], b["u2"])
    next(to_update)
    t_y.step2()
    t_y.finish()
    t_y = mix("y2_rows", 1.0, -2.4375, "y3_b", "y3_rows", t_stat)
    next(to_update)
    t_y.step1()
    next(to_update)
    t_y.step2()
    t_y.finish()
    v = dot(b["y3_rows"][...], b["a_cols"][...])
    new_br[...] = (math.sqrt(FF) * scale) * (2.25 * b["p"][...] + v)
    stores[6].start()
    for _ in to_update:
        pass
    stores[0].start()
    assert net.taken <= SEMS and locals_used[0] <= 16
    cast.drain()
    net.drain()
    for store in stores:
        store.wait()


def emit(*refs):
    held, sem = refs[14:21], refs[21]
    into = [pltpu.make_async_copy(refs[k], held[k], sem.at[0, k]) for k in range(7)]
    onto = [pltpu.make_async_copy(held[k], refs[7 + k], sem.at[1, k]) for k in range(7)]
    for copy in into:
        copy.start()
    for copy, store in zip(into, onto):
        copy.wait()
        store.start()
    for store in onto:
        store.wait()


def local(gradient, moment_one, moment_two, stat_left, stat_right, basis_left, basis_right):
    args = (gradient, moment_one, moment_two, stat_left, stat_right, basis_left, basis_right)
    out = pl.pallas_call(
        kernel,
        out_shape=[jax.ShapeDtypeStruct(a.shape, a.dtype) for a in args],
        in_specs=[pl.BlockSpec(memory_space=pl.ANY)] * 7,
        out_specs=[pl.BlockSpec(memory_space=pl.ANY)] * 7,
        scratch_shapes=[pltpu.VMEM(shape, dtype) for shape, dtype in BUFFERS.values()]
        + [
            pltpu.SemaphoreType.DMA((POOL + 8,)),
            pltpu.SemaphoreType.DMA((SEMS,)),
            pltpu.SemaphoreType.DMA((30,)),
        ]
        + [pltpu.VMEM(a.shape, a.dtype) for a in args * 2],
        compiler_params=pltpu.CompilerParams(
            collective_id=0, has_side_effects=True, vmem_limit_bytes=63 * 2**20
        ),
        name="step",
    )(*args)
    hbm = pl.BlockSpec(memory_space=pl.ANY)
    return pl.pallas_call(
        emit,
        out_shape=[jax.ShapeDtypeStruct(a.shape, a.dtype) for a in args],
        in_specs=[hbm] * 7,
        out_specs=[hbm] * 7,
        scratch_shapes=[pltpu.VMEM(a.shape, a.dtype) for a in args] + [pltpu.SemaphoreType.DMA((2, 7))],
        compiler_params=pltpu.CompilerParams(vmem_limit_bytes=63 * 2**20),
        name="emit",
    )(*out)


def solution(mesh):
    both, row = P("shard", "tensor"), P("shard", None)
    return jax.shard_map(
        local,
        mesh=mesh,
        in_specs=(both, both, both, row, both, row, both),
        out_specs=(both, both, both, row, both, row, both),
        check_vma=False,
    )
```

```python
import functools
import math

import jax
import jax.numpy as jnp
from jax import lax
from jax.experimental import pallas as pl
from jax.experimental.pallas import tpu as pltpu
from jax.sharding import PartitionSpec as P

D = 768
FF = 3072
BF = jnp.bfloat16
F32 = jnp.float32
MESH = pl.DeviceIdType.MESH

beta = 0.95
correction = 1.0 - 0.95**10
adam_eps = 1e-08


class Move:
    def __init__(self, landing):
        self.landing = landing

    def recv(self):
        self.landing.wait_recv()


class Slots:
    def __init__(self, first, count):
        self.first, self.count, self.used = first, count, 0

    def next(self):
        self.used += 1
        assert self.used <= self.count
        return self.first + self.used - 1

    def again(self):
        return Slots(self.first, self.count)


class Net:
    def __init__(self, send_sem, recv_sem):
        self.send_sem, self.recv_sem = send_sem, recv_sem
        self.count = 0
        self.taken = 0
        self.sent = {}
        s, t = lax.axis_index("shard"), lax.axis_index("tensor")
        self.s, self.t = s, t
        self.z, self.x = s // 4, s % 4
        self.y, self.c = t // 2, t % 2

    def take(self, count):
        self.taken += count
        return Slots(self.taken - count, count)

    def nbr(self, d):
        s, t = self.s, self.t
        z, x, y, c = self.z, self.x, self.y, self.c
        if d == "c":
            return (s, y * 2 + 1 - c)
        step = {"+": 1, "2": 2, "-": 3}[d[0]]
        if d[1] == "x":
            return (z * 4 + (x + step) % 4, t)
        if d[1] == "z":
            return (((z + step) % 4) * 4 + x, t)
        return (s, ((y + step) % 4) * 2 + c)

    def greet(self, dirs):
        sem = pltpu.get_barrier_semaphore()
        for d in dirs:
            pl.semaphore_signal(sem, inc=1, device_id=self.nbr(d), device_id_type=MESH)

    def meet(self, dirs):
        pl.semaphore_wait(pltpu.get_barrier_semaphore(), len(dirs))

    def send(self, src, dst, landing, d, slots):
        k, r = self.count % POOL, slots.next()
        self.count += 1
        if k in self.sent:
            self.sent[k].wait_send()
        mk = lambda a, b: pltpu.make_async_remote_copy(
            src_ref=a,
            dst_ref=b,
            send_sem=self.send_sem.at[k],
            recv_sem=self.recv_sem.at[r],
            device_id=self.nbr(d),
            device_id_type=MESH,
        )
        self.sent[k] = mk(src, dst)
        self.sent[k].start()
        return Move(mk(landing, landing))

    def drain(self):
        for copy in self.sent.values():
            copy.wait_send()
        self.sent = {}


def cuts(rows):
    if rows % 64 == 0:
        q = rows // 4
        return ((0, q, 2 * q), (2 * q, 3 * q, 4 * q))
    if rows == 48:
        return ((0, 16, 32), (32, 48, 48))
    return ((0, rows, rows), None)


class ShardGather:
    def __init__(self, net, src, buf, direct=False, slots=None):
        self.net, self.src, self.buf, self.direct = net, src, buf, direct
        self.flows = [(i, f) for i, f in enumerate(cuts(src.shape[0])) if f is not None]
        self.m = {}
        self.slots = slots or net.take(40 if self.flows[-1][0] else 20)

    def view(self, blk, lo, hi):
        n, rows = self.net, self.src.shape[0]
        slot = (n.z + blk[0]) % 4 * 4 + (n.x + blk[1]) % 4
        return self.buf.at[pl.ds(pl.multiple_of(slot * rows + lo, 8), hi - lo), :]

    def axes(self, i):
        return ("x", "z") if i == 0 else ("z", "x")

    def rel(self, i, first, second):
        return (second, first) if i == 0 else (first, second)

    def go(self, i, stage, sgn, first, second, lo, hi, key, own=False):
        if hi == lo:
            return
        axis = self.axes(i)[stage]
        d = ("+" if sgn > 0 else "-") + axis
        blk = self.rel(i, first, second)
        lf, ls = (first - sgn, second) if stage == 0 else (first, second - sgn)
        src = self.src.at[pl.ds(lo, hi - lo), :] if own else self.view(blk, lo, hi)
        self.m[key] = self.net.send(src, self.view(blk, lo, hi), self.view(self.rel(i, lf, ls), lo, hi), d, self.slots)

    def wait(self, *key):
        if key in self.m:
            self.m[key].recv()

    def start(self, only=(0, 1)):
        n = self.net
        flows = [f for f in self.flows if f[0] in only]
        for i, (lo, mid, hi) in flows:
            for sgn in (1, -1):
                self.go(i, 0, sgn, 0, 0, lo, hi, (i, "a", sgn), own=True)
            if self.direct:
                src = self.src.at[pl.ds(lo, hi - lo), :]
                landing = self.view(self.rel(i, 2, 0), lo, hi)
                self.m[i, "aa", 1] = n.send(src, self.view((0, 0), lo, hi), landing, "2" + self.axes(i)[0], self.slots)
        for i, (lo, mid, hi) in flows:
            for sgn in (1, -1):
                self.go(i, 1, sgn, 0, 0, lo, hi, (i, "b", 0, sgn), own=True)

    def local(self, sem):
        n = self.net
        self.mine = pltpu.make_async_copy(self.src, self.view((0, 0), 0, self.src.shape[0]), sem)
        self.mine.start()

    def second(self, i, first, lo, hi):
        for sgn in (1, -1):
            self.go(i, 1, sgn, first, 0, lo, hi, (i, "b", first, sgn))

    def relay(self, i, first, lo, mid, hi):
        for sgn in (1, -1):
            self.wait(i, "b", first, sgn)
            a, b = (lo, mid) if sgn > 0 else (mid, hi)
            self.go(i, 1, sgn, first, -sgn, a, b, (i, "bb", first, sgn))

    def step1(self):
        for i, (lo, mid, hi) in self.flows:
            for sgn in (1, -1):
                self.wait(i, "a", sgn)
                a, b = (lo, mid) if sgn > 0 else (mid, hi)
                if not self.direct:
                    self.go(i, 0, sgn, -sgn, 0, a, b, (i, "aa", sgn))
                self.second(i, -sgn, lo, hi)

    def step2(self):
        for i, (lo, mid, hi) in self.flows:
            self.relay(i, 0, lo, mid, hi)
        for i, (lo, mid, hi) in self.flows:
            self.wait(i, "aa", 1)
            self.wait(i, "aa", -1)
            self.second(i, 2, lo, hi)

    def step3(self):
        for i, (lo, mid, hi) in self.flows:
            for first in (1, -1, 2):
                self.relay(i, first, lo, mid, hi)

    def finish(self):
        for i, _ in self.flows:
            for first in (0, 1, -1, 2):
                for sgn in (1, -1):
                    self.wait(i, "bb", first, sgn)
        self.mine.wait()


class TensorGather:
    def __init__(self, net, src, buf, wide=True, slots=None):
        self.net, self.src, self.buf, self.wide = net, src, buf, wide
        self.slots = slots or net.take(11)
        rows = src.shape[0]
        self.cut = (0, rows // 32 * 16, rows)

    def view(self, dy, other, lo, hi):
        n, (rows, cols) = self.net, self.src.shape
        slot = (n.y + dy) % 4 * 2 + ((1 - n.c) if other else n.c)
        if self.wide:
            return self.buf.at[pl.ds(lo, hi - lo), pl.ds(pl.multiple_of(slot * cols, 128), cols)]
        return self.buf.at[pl.ds(pl.multiple_of(slot * rows + lo, 16), hi - lo), :]

    def start(self):
        n = self.net
        lo, mid, hi = self.cut
        own = lambda a, b: self.src.at[pl.ds(a, b - a), :]
        put = lambda a, b, sgn: n.send(
            own(a, b), self.view(0, 0, a, b), self.view(-sgn, 0, a, b), "+y" if sgn > 0 else "-y", self.slots
        )
        self.a = {1: put(lo, mid, 1), -1: put(mid, hi, -1)}
        self.rest = {1: put(mid, hi, 1), -1: put(lo, mid, -1)}
        self.sib = [n.send(self.src, self.view(0, 0, lo, hi), self.view(0, 1, lo, hi), "c", self.slots)]

    def local(self, sem):
        self.mine = pltpu.make_async_copy(self.src, self.view(0, 0, 0, self.src.shape[0]), sem)
        self.mine.start()

    def pair(self, dy, lo, hi):
        n = self.net
        self.sib.append(n.send(self.view(dy, 0, lo, hi), self.view(dy, 0, lo, hi), self.view(dy, 1, lo, hi), "c", self.slots))

    def step1(self):
        n = self.net
        lo, mid, hi = self.cut
        self.aa = []
        for sgn in (1, -1):
            self.a[sgn].recv()
            a, b = (lo, mid) if sgn > 0 else (mid, hi)
            v = self.view(-sgn, 0, a, b)
            self.aa.append(n.send(v, v, self.view(2, 0, a, b), "+y" if sgn > 0 else "-y", self.slots))

    def step2(self):
        lo, mid, hi = self.cut
        for sgn in (1, -1):
            self.rest[sgn].recv()
            self.pair(-sgn, lo, hi)
        for m, (a, b) in zip(self.aa, ((lo, mid), (mid, hi))):
            m.recv()
            self.pair(2, a, b)

    def finish(self):
        for m in self.sib:
            m.recv()
        self.mine.wait()


def add_into(a, b):
    a[...] = (a[...].astype(F32) + b[...].astype(F32)).astype(a.dtype)


class RingScatter:
    def __init__(self, net, axis, pick, half, first, second):
        self.net, self.axis, self.pick, self.half = net, axis, pick, half
        self.first, self.second = first, second
        self.slots = net.take(6)

    def start(self):
        n = self.net
        way = lambda h: ("+", "-")[h] + self.axis
        self.one = [n.send(self.half(self.pick(2), h), self.first[h], self.first[h], way(h), self.slots) for h in (0, 1)]

    def near(self):
        n = self.net
        way = lambda h: ("+", "-")[h] + self.axis
        self.two = []
        for h, rel in ((0, 1), (1, -1)):
            dst = self.half(self.second[h], 1 - h)
            self.two.append(n.send(self.half(self.pick(rel), 1 - h), dst, dst, way(h), self.slots))

    def middle(self):
        n = self.net
        for h, rel in ((0, 1), (1, -1)):
            self.one[h].recv()
            add_into(self.half(self.pick(rel), h), self.first[h])
            dst = self.half(self.second[h], h)
            self.two.append(n.send(self.half(self.pick(rel), h), dst, dst, ("+", "-")[h] + self.axis, self.slots))

    def total(self):
        for m in self.two:
            m.recv()
        own = self.pick(0)
        return own[...].astype(F32) + self.second[0][...].astype(F32) + self.second[1][...].astype(F32)


class LineBroadcast:
    def __init__(self, net, src, dst, lsem):
        self.net, self.src, self.dst, self.lsem = net, src, dst, lsem
        self.slots = net.take(8)
        self.dy = (net.y - net.z + 4) % 4
        self.main = net.c == net.x // 2
        h = src.shape[0] // 2
        lo, hi = pl.ds(0, h), pl.ds(h, h)
        self.kinds = [(lo, "+y"), (hi, "+y"), (hi, "-y"), (lo, "-y"), (lo, "+y"), (hi, "-y"), (lo, "c"), (hi, "c")]

    def msg(self, j, a=None):
        n = self.net
        cut, d = self.kinds[j]
        a = self.dst if a is None else a
        return pltpu.make_async_remote_copy(
            src_ref=a.at[cut, :],
            dst_ref=self.dst.at[cut, :],
            send_sem=n.send_sem.at[POOL + j],
            recv_sem=n.recv_sem.at[self.slots.first + j],
            device_id=n.nbr(d),
            device_id_type=MESH,
        )

    def at(self, dy):
        return pl.when(jnp.logical_and(self.main, self.dy == dy))

    def start(self):
        @self.at(0)
        def _():
            for j in (0, 2, 1, 3, 6, 7):
                self.msg(j, self.src).start()
            pltpu.make_async_copy(self.src, self.dst, self.lsem).start()

    def middle(self):
        for dy, j, onward, half in ((1, 0, 4, 6), (3, 2, 5, 7)):

            @self.at(dy)
            def _(j=j, onward=onward, half=half):
                self.msg(j).wait_recv()
                self.msg(onward).start()
                self.msg(half).start()

    def finish(self):
        for dy, j, half in ((1, 1, 7), (3, 3, 6)):

            @self.at(dy)
            def _(j=j, half=half):
                self.msg(j).wait_recv()
                self.msg(half).start()

        @self.at(2)
        def _():
            for j, half in ((4, 6), (5, 7)):
                self.msg(j).wait_recv()
                self.msg(half).start()

        @pl.when(jnp.logical_not(self.main))
        def _():
            self.msg(6).wait_recv()
            self.msg(7).wait_recv()

        @self.at(0)
        def _():
            pltpu.make_async_copy(self.src, self.dst, self.lsem).wait()

    def drain(self):
        @self.at(0)
        def _():
            for j in range(4):
                self.msg(j, self.src).wait_send()

        for dy, onward in ((1, 4), (3, 5)):

            @self.at(dy)
            def _(onward=onward):
                self.msg(onward).wait_send()

        @pl.when(self.main)
        def _():
            self.msg(6).wait_send()
            self.msg(7).wait_send()


def plane_scatter(net, part, out, f1, f2, q, g1, g2):
    z, x = net.z, net.x
    h = part.shape[2] // 2
    zx = (z, x)
    stages = []
    for i in (0, 1):
        lo = i * h

        def pick(rel, i=i, lo=lo):
            if i == 0:
                return part.at[(z + rel) % 4, :, pl.ds(lo, h), :]
            return part.at[:, (x + rel) % 4, pl.ds(lo, h), :]

        def half(view, k):
            return view.at[pl.ds(2 * k, 2)]

        stages.append(RingScatter(net, "zx"[i], pick, half, [f1.at[i, 0], f1.at[i, 1]], [f2.at[i, 0], f2.at[i, 1]]))
    stages[0].start()
    yield
    stages[0].near()
    yield
    stages[1].start()
    stages[1].near()
    yield
    for r in stages:
        r.middle()
    yield
    later = []
    for i, r in enumerate(stages):
        q[i] = r.total().astype(q.dtype)

        def pick(rel, i=i):
            return q.at[i, (zx[1 - i] + rel) % 4]

        def half(view, k):
            return view.at[pl.ds(k * (h // 2), h // 2), :]

        later.append(RingScatter(net, "xz"[i], pick, half, [g1.at[i, 0], g1.at[i, 1]], [g2.at[i, 0], g2.at[i, 1]]))
        later[-1].start()
        later[-1].near()
    yield
    for r in later:
        r.middle()
    yield
    for i, r in enumerate(later):
        out[pl.ds(i * h, h), :] = r.total().astype(out.dtype)
        yield


def line_scatter(net, part, out, g0, q, g1, g2):
    y, c = net.y, net.c
    rows = part.shape[2]
    m = net.send(part.at[1 - c], g0, g0, "c", net.take(1))
    yield
    m.recv()
    q[...] = (part[c].astype(F32) + g0[...].astype(F32)).astype(q.dtype)
    cut = rows // 32 * 16

    def pick(rel):
        return q.at[(y + rel) % 4]

    def half(view, k):
        return view.at[pl.ds(0, cut), :] if k == 0 else view.at[pl.ds(cut, rows - cut), :]

    ring = RingScatter(net, "y", pick, half, [g1.at[pl.ds(0, cut)], g1.at[pl.ds(cut, rows - cut)]], [g2.at[0], g2.at[1]])
    ring.start()
    ring.near()
    yield
    ring.middle()
    yield
    out[...] = ring.total().astype(out.dtype)


def dot(a, b):
    return jnp.dot(a, b, preferred_element_type=F32)


def dot_tn(a, b):
    return lax.dot_general(a, b, (((0,), (0,)), ((), ())), preferred_element_type=F32)


def dot_nt(a, b):
    return lax.dot_general(a, b, (((1,), (1,)), ((), ())), preferred_element_type=F32)


SEMS, POOL = 208, 56
ROWS, COLS, LROWS = FF // 16, FF // 8, D // 16
BUFFERS = dict(
    lq=((LROWS, D), BF),
    rq=((ROWS, COLS), BF),
    gcols=((D, COLS), BF),
    lall=((D, D), BF),
    qcols=((FF, COLS), BF),
    gs_own=((D, ROWS), BF),
    gs=((D, ROWS), BF),
    lterms=((LROWS, D), BF),
    lparts=((8 * LROWS, D), BF),
    half_all=((D, COLS), BF),
    half_rows=((LROWS, FF), BF),
    s_b=((ROWS, COLS), BF),
    s_rows=((ROWS, FF), BF),
    p=((ROWS, COLS), F32),
    p_b=((ROWS, COLS), BF),
    p_rows=((ROWS, FF), BF),
    dir_b=((LROWS, COLS), BF),
    dir_cols=((D, COLS), BF),
    pl_own=((LROWS, D), F32),
    pl_b=((LROWS, D), BF),
    pl_all=((D, D), BF),
    gl=((D, D), BF),
    wl=((D, D), BF),
    tile=((8, 128), F32),
    tiles=((128, 128), F32),
    part=((4, 4, ROWS, COLS), BF),
    f1=((2, 2, 2, ROWS // 2, COLS), BF),
    f2=((2, 2, 4, ROWS // 2, COLS), BF),
    fq=((2, 4, ROWS // 2, COLS), BF),
    fg1=((2, 2, ROWS // 4, COLS), BF),
    fg2=((2, 2, ROWS // 2, COLS), BF),
    a_b=((ROWS, COLS), BF),
    a_cols=((FF, COLS), BF),
    y1_b=((ROWS, COLS), BF),
    y1_rows=((ROWS, FF), BF),
    y2_b=((ROWS, COLS), BF),
    y2_rows=((ROWS, FF), BF),
    y3_b=((ROWS, COLS), BF),
    y3_rows=((ROWS, FF), BF),
    upart=((2, 4, LROWS, COLS), BF),
    u0=((4, LROWS, COLS), BF),
    uq=((4, LROWS, COLS), BF),
    u1=((LROWS, COLS), BF),
    u2=((2, LROWS, COLS), BF),
)
NBR = ("+x", "-x", "2x", "+z", "-z", "2z", "+y", "-y", "c")


def kernel(*refs):
    b = dict(zip(BUFFERS, refs[14 : 14 + len(BUFFERS)]))
    send_sem, recv_sem, lsem = refs[14 + len(BUFFERS) : 17 + len(BUFFERS)]
    inputs, outputs = refs[17 + len(BUFFERS) : 24 + len(BUFFERS)], refs[24 + len(BUFFERS) :]
    update, new_m1, new_m2, new_sl, new_sr, new_bl, new_br = outputs
    stores = [pltpu.make_async_copy(outputs[k], refs[7 + k], lsem.at[23 + k]) for k in range(7)]
    grad, m1, m2, stat_l, stat_r, basis_l, basis_r = inputs
    loads = [pltpu.make_async_copy(refs[k], inputs[k], lsem.at[16 + k]) for k in range(7)]
    for k in (0, 5, 6, 4, 3, 1, 2):
        loads[k].start()
    net = Net(send_sem, recv_sem)
    x, s = net.x, net.s
    own_left = pl.ds(pl.multiple_of(s * LROWS, 16), LROWS)
    lanes = lambda c: pl.ds(pl.multiple_of(c * (D // 2), 128), D // 2)
    locals_used = [0]

    def begin(*gathers):
        for g in gathers:
            g.start()
            g.local(lsem.at[locals_used[0]])
            locals_used[0] += 1

    def swap(ref):
        mine = ref.at[:, lanes(net.c)]
        return net.send(mine, mine, ref.at[:, lanes(1 - net.c)], "c", net.take(1))

    net.greet(NBR)
    loads[0].wait()
    net.meet(NBR)

    g_grad = ShardGather(net, grad, b["gcols"], direct=True)
    begin(g_grad)
    loads[5].wait()
    b["lq"][...] = (basis_l[...] * (1.0 / math.sqrt(D))).astype(BF)
    loads[6].wait()
    b["rq"][...] = (basis_r[...] * (1.0 / math.sqrt(FF))).astype(BF)
    for k in (4, 3, 1, 2):
        loads[k].wait()
    g_left = ShardGather(net, b["lq"].at[:, lanes(net.c)], b["lall"].at[:, lanes(net.c)])
    g_right = ShardGather(net, b["rq"], b["qcols"])
    g_grad.step1()
    begin(g_left)
    g_grad.step2()
    g_left.step1()
    g_grad.step3()
    begin(g_right)
    g_left.step2()
    g_grad.finish()
    cast = LineBroadcast(net, b["gs_own"], b["gs"], lsem.at[locals_used[0]])
    locals_used[0] += 1
    pick = lax.broadcasted_iota(jnp.int32, (COLS, ROWS), 0) == lax.broadcasted_iota(
        jnp.int32, (COLS, ROWS), 1
    ) + ROWS * (x % 2)
    gcols = b["gcols"]
    b["gs_own"][...] = dot(gcols[...], jnp.where(pick, 1.0, 0.0).astype(BF)).astype(BF)
    cast.start()
    b["lterms"][...] = dot_nt(grad[...], gcols[...]).astype(BF)
    t_lterms = TensorGather(net, b["lterms"], b["lparts"], wide=False)
    begin(t_lterms)
    g_right.step1()
    cast.middle()
    g_right.step2()
    g_left.step3()
    t_lterms.step1()
    cast.finish()

    new_sr[...] = beta * stat_r[...] + ((1.0 - beta) / D) * dot_tn(b["gs"][...], gcols[...])
    b["s_b"][...] = new_sr[...].astype(BF)
    t_stat = TensorGather(net, b["s_b"], b["s_rows"])
    begin(t_stat)
    stores[4].start()
    t_lterms.step2()
    g_right.step3()
    t_stat.step1()
    g_left.finish()
    left_swap = swap(b["lall"])
    left_swap.recv()
    t_lterms.finish()
    gram = b["lparts"][pl.ds(0, LROWS), :].astype(F32)
    for j in range(1, 8):
        gram += b["lparts"][pl.ds(j * LROWS, LROWS), :].astype(F32)
    new_sl[...] = beta * stat_l[...] + ((1.0 - beta) / FF) * gram
    b["pl_own"][...] = dot(new_sl[...].astype(BF), b["lall"][...])
    b["pl_b"][...] = b["pl_own"][...].astype(BF)
    g_pl = ShardGather(
        net, b["pl_b"].at[:, lanes(net.c)], b["pl_all"].at[:, lanes(net.c)], slots=g_grad.slots.again()
    )
    begin(g_pl)
    stores[3].start()
    b["half_all"][...] = dot_tn(b["lall"][...], gcols[...]).astype(BF)
    t_half = TensorGather(net, b["half_all"].at[own_left, :], b["half_rows"])
    t_stat.step2()
    begin(t_half)
    g_right.finish()
    t_stat.finish()
    b["p"][...] = dot(b["s_rows"][...], b["qcols"][...])
    b["p_b"][...] = b["p"][...].astype(BF)
    t_power = TensorGather(net, b["p_b"], b["p_rows"])
    begin(t_power)
    g_pl.step1()
    t_half.step1()
    t_power.step1()
    g_pl.step2()
    t_half.step2()
    t_power.step2()
    g_pl.step3()
    t_power.finish()

    def term(rel):
        zt = (net.z + rel) % 4
        v = dot_tn(b["p_rows"][:, pl.ds(pl.multiple_of(zt * D, 128), D)], b["p_b"][...]).astype(BF)
        b["part"][zt] = v.reshape(4, ROWS, COLS)

    scatter = plane_scatter(net, b["part"], b["a_b"], b["f1"], b["f2"], b["fq"], b["fg1"], b["fg2"])
    term(2)
    next(scatter)
    term(1)
    term(3)
    next(scatter)
    term(0)
    next(scatter)

    def squares(j, total):
        v = b["p_rows"][pl.ds(pl.multiple_of(j * 16, 16), 16), :].astype(F32)
        return total + jnp.sum(v * v, axis=0, keepdims=True)

    total = lax.fori_loop(0, ROWS // 16, squares, jnp.zeros((1, FF), F32))
    b["tile"][...] = jnp.broadcast_to(jnp.sum(total, keepdims=True), (8, 128))
    g_tile = ShardGather(net, b["tile"], b["tiles"], slots=g_left.slots.again())
    begin(g_tile)
    t_half.finish()
    rot = dot(b["half_rows"][...], b["qcols"][...])
    first = beta * m1[...] + (1.0 - beta) * rot
    second = beta * m2[...] + (1.0 - beta) * (rot * rot)
    new_m1[...] = first
    new_m2[...] = second
    stores[1].start()
    stores[2].start()
    b["dir_b"][...] = ((first / correction) / (jnp.sqrt(second / correction) + adam_eps)).astype(BF)
    next(scatter)
    g_pl.finish()
    pl_swap = swap(b["pl_all"])
    pl_swap.recv()

    def left_squares(j, total):
        v = b["pl_all"][pl.ds(pl.multiple_of(j * 16, 16), 16), :].astype(F32)
        return total + jnp.sum(v * v, axis=0, keepdims=True)

    def left_gram(ref, factor, lo, hi):
        for j in range(lo, hi):
            cut = pl.ds(j * 128, 128)
            b["gl"][cut, :] = (dot_tn(ref[:, cut], ref[...]) * factor).astype(BF)

    left_total = lax.fori_loop(0, D // 16, left_squares, jnp.zeros((1, D), F32))
    left_scale = math.sqrt(D) / (4.0 * jnp.sqrt(jnp.sum(left_total, keepdims=True)))
    left_gram(b["pl_all"], left_scale * left_scale, 0, 4)
    g_tile.step1()
    next(scatter)
    g_tile.step2()
    left_gram(b["pl_all"], left_scale * left_scale, 4, 5)
    next(scatter)
    g_tile.step3()
    left_gram(b["pl_all"], left_scale * left_scale, 5, 6)
    g_a = ShardGather(net, b["a_b"], b["a_cols"], slots=g_right.slots.again())
    next(scatter)
    g_a.start((0,))
    next(scatter)
    g_a.start((1,))
    g_a.local(lsem.at[locals_used[0]])
    locals_used[0] += 1
    for j in range(3):
        cut = pl.ds(j * 256, 256)
        v = b["pl_all"][cut, :]
        b["wl"][cut, :] = (left_scale * (1.5 * v.astype(F32) - 0.5 * dot(v, b["gl"][...]))).astype(BF)
    mine = left_scale * (1.5 * b["pl_own"][...] - 0.5 * dot(b["pl_b"][...], b["gl"][...]))
    g_a.step1()
    left_gram(b["wl"], 1.0, 0, 5)
    g_a.step2()
    left_gram(b["wl"], 1.0, 5, 6)
    new_bl[...] = math.sqrt(D) * (1.5 * mine - 0.5 * dot(mine.astype(BF), b["gl"][...]))
    stores[5].start()
    g_a.step3()
    g_dir = ShardGather(net, b["dir_b"], b["dir_cols"], slots=g_grad.slots.again())
    begin(g_dir)
    g_tile.finish()
    norm = jnp.sum(b["tiles"][...], keepdims=True) / 1024.0
    scale = math.sqrt(FF) / (4.0 * jnp.sqrt(norm))
    square = scale * scale
    g_a.finish()

    def mix(rows, factor, add, out, all_rows, before):
        v = dot(b[rows][...], b["a_cols"][...])
        b[out][...] = (factor * v + add * b["p"][...]).astype(BF)
        g = TensorGather(net, b[out], b[all_rows], slots=before.slots.again())
        begin(g)
        return g

    t_y = mix("p_rows", 0.0625 * square, -0.5625, "y1_b", "y1_rows", t_stat)
    g_dir.step1()
    t_y.step1()
    g_dir.step2()
    t_y.step2()
    g_dir.step3()
    t_y.finish()
    t_y = mix("y1_rows", square, 1.6875, "y2_b", "y2_rows", t_power)
    t_y.step1()
    g_dir.finish()
    back = dot(b["lq"][...], b["dir_cols"][...]).astype(BF)
    for j in range(8):
        b["upart"][j % 2, j // 2] = dot_nt(back, b["qcols"][pl.ds(j * COLS, COLS), :]).astype(BF)
    to_update = line_scatter(net, b["upart"], update, b["u0"], b["uq"], b["u1"], b["u2"])
    next(to_update)
    t_y.step2()
    t_y.finish()
    t_y = mix("y2_rows", square, -2.4375, "y3_b", "y3_rows", t_stat)
    next(to_update)
    t_y.step1()
    next(to_update)
    t_y.step2()
    t_y.finish()
    v = dot(b["y3_rows"][...], b["a_cols"][...])
    new_br[...] = (math.sqrt(FF) * scale) * (2.25 * b["p"][...] + square * v)
    stores[6].start()
    for _ in to_update:
        pass
    stores[0].start()
    assert net.taken <= SEMS and locals_used[0] <= 16
    cast.drain()
    net.drain()
    for store in stores:
        store.wait()


def emit(*refs):
    held, sem = refs[14:21], refs[21]
    into = [pltpu.make_async_copy(refs[k], held[k], sem.at[0, k]) for k in range(7)]
    onto = [pltpu.make_async_copy(held[k], refs[7 + k], sem.at[1, k]) for k in range(7)]
    for copy in into:
        copy.start()
    for copy, store in zip(into, onto):
        copy.wait()
        store.start()
    for store in onto:
        store.wait()


def local(gradient, moment_one, moment_two, stat_left, stat_right, basis_left, basis_right):
    args = (gradient, moment_one, moment_two, stat_left, stat_right, basis_left, basis_right)
    out = pl.pallas_call(
        kernel,
        out_shape=[jax.ShapeDtypeStruct(a.shape, a.dtype) for a in args],
        in_specs=[pl.BlockSpec(memory_space=pl.ANY)] * 7,
        out_specs=[pl.BlockSpec(memory_space=pl.ANY)] * 7,
        scratch_shapes=[pltpu.VMEM(shape, dtype) for shape, dtype in BUFFERS.values()]
        + [
            pltpu.SemaphoreType.DMA((POOL + 8,)),
            pltpu.SemaphoreType.DMA((SEMS,)),
            pltpu.SemaphoreType.DMA((30,)),
        ]
        + [pltpu.VMEM(a.shape, a.dtype) for a in args * 2],
        compiler_params=pltpu.CompilerParams(
            collective_id=0, has_side_effects=True, vmem_limit_bytes=63 * 2**20
        ),
        name="step",
    )(*args)
    hbm = pl.BlockSpec(memory_space=pl.ANY)
    return pl.pallas_call(
        emit,
        out_shape=[jax.ShapeDtypeStruct(a.shape, a.dtype) for a in args],
        in_specs=[hbm] * 7,
        out_specs=[hbm] * 7,
        scratch_shapes=[pltpu.VMEM(a.shape, a.dtype) for a in args] + [pltpu.SemaphoreType.DMA((2, 7))],
        compiler_params=pltpu.CompilerParams(vmem_limit_bytes=63 * 2**20),
        name="emit",
    )(*out)


def solution(mesh):
    both, row = P("shard", "tensor"), P("shard", None)
    return jax.shard_map(
        local,
        mesh=mesh,
        in_specs=(both, both, both, row, both, row, both),
        out_specs=(both, both, both, row, both, row, both),
        check_vma=False,
    )
```

```python
import functools
import math

import jax
import jax.numpy as jnp
from jax import lax
from jax.experimental import pallas as pl
from jax.experimental.pallas import tpu as pltpu
from jax.sharding import PartitionSpec as P

D = 768
FF = 3072
BF = jnp.bfloat16
F32 = jnp.float32
MESH = pl.DeviceIdType.MESH

beta = 0.95
correction = 1.0 - 0.95**10
adam_eps = 1e-08


class Move:
    def __init__(self, landing):
        self.landing = landing

    def recv(self):
        self.landing.wait_recv()


class Slots:
    def __init__(self, first, count):
        self.first, self.count, self.used = first, count, 0

    def next(self):
        self.used += 1
        assert self.used <= self.count
        return self.first + self.used - 1

    def again(self):
        return Slots(self.first, self.count)


class Net:
    def __init__(self, send_sem, recv_sem):
        self.send_sem, self.recv_sem = send_sem, recv_sem
        self.count = 0
        self.taken = 0
        self.sent = {}
        s, t = lax.axis_index("shard"), lax.axis_index("tensor")
        self.s, self.t = s, t
        self.z, self.x = s // 4, s % 4
        self.y, self.c = t // 2, t % 2

    def take(self, count):
        self.taken += count
        return Slots(self.taken - count, count)

    def nbr(self, d):
        s, t = self.s, self.t
        z, x, y, c = self.z, self.x, self.y, self.c
        if d == "c":
            return (s, y * 2 + 1 - c)
        step = {"+": 1, "2": 2, "-": 3}[d[0]]
        if d[1] == "x":
            return (z * 4 + (x + step) % 4, t)
        if d[1] == "z":
            return (((z + step) % 4) * 4 + x, t)
        return (s, ((y + step) % 4) * 2 + c)

    def greet(self, dirs):
        sem = pltpu.get_barrier_semaphore()
        for d in dirs:
            pl.semaphore_signal(sem, inc=1, device_id=self.nbr(d), device_id_type=MESH)

    def meet(self, dirs):
        pl.semaphore_wait(pltpu.get_barrier_semaphore(), len(dirs))

    def send(self, src, dst, landing, d, slots):
        k, r = self.count % POOL, slots.next()
        self.count += 1
        if k in self.sent:
            self.sent[k].wait_send()
        mk = lambda a, b: pltpu.make_async_remote_copy(
            src_ref=a,
            dst_ref=b,
            send_sem=self.send_sem.at[k],
            recv_sem=self.recv_sem.at[r],
            device_id=self.nbr(d),
            device_id_type=MESH,
        )
        self.sent[k] = mk(src, dst)
        self.sent[k].start()
        return Move(mk(landing, landing))

    def drain(self):
        for copy in self.sent.values():
            copy.wait_send()
        self.sent = {}


def cuts(rows):
    if rows % 64 == 0:
        q = rows // 4
        return ((0, q, 2 * q), (2 * q, 3 * q, 4 * q))
    if rows == 48:
        return ((0, 16, 32), (32, 48, 48))
    return ((0, rows, rows), None)


class ShardGather:
    def __init__(self, net, src, buf, direct=False, slots=None):
        self.net, self.src, self.buf, self.direct = net, src, buf, direct
        self.flows = [(i, f) for i, f in enumerate(cuts(src.shape[0])) if f is not None]
        self.m = {}
        self.slots = slots or net.take(40 if self.flows[-1][0] else 20)

    def view(self, blk, lo, hi):
        n, rows = self.net, self.src.shape[0]
        slot = (n.z + blk[0]) % 4 * 4 + (n.x + blk[1]) % 4
        return self.buf.at[pl.ds(pl.multiple_of(slot * rows + lo, 8), hi - lo), :]

    def axes(self, i):
        return ("x", "z") if i == 0 else ("z", "x")

    def rel(self, i, first, second):
        return (second, first) if i == 0 else (first, second)

    def go(self, i, stage, sgn, first, second, lo, hi, key, own=False):
        if hi == lo:
            return
        axis = self.axes(i)[stage]
        d = ("+" if sgn > 0 else "-") + axis
        blk = self.rel(i, first, second)
        lf, ls = (first - sgn, second) if stage == 0 else (first, second - sgn)
        src = self.src.at[pl.ds(lo, hi - lo), :] if own else self.view(blk, lo, hi)
        self.m[key] = self.net.send(src, self.view(blk, lo, hi), self.view(self.rel(i, lf, ls), lo, hi), d, self.slots)

    def wait(self, *key):
        if key in self.m:
            self.m[key].recv()

    def start(self, only=(0, 1)):
        n = self.net
        flows = [f for f in self.flows if f[0] in only]
        for i, (lo, mid, hi) in flows:
            for sgn in (1, -1):
                self.go(i, 0, sgn, 0, 0, lo, hi, (i, "a", sgn), own=True)
            if self.direct:
                src = self.src.at[pl.ds(lo, hi - lo), :]
                landing = self.view(self.rel(i, 2, 0), lo, hi)
                self.m[i, "aa", 1] = n.send(src, self.view((0, 0), lo, hi), landing, "2" + self.axes(i)[0], self.slots)
        for i, (lo, mid, hi) in flows:
            for sgn in (1, -1):
                self.go(i, 1, sgn, 0, 0, lo, hi, (i, "b", 0, sgn), own=True)

    def local(self, sem):
        n = self.net
        self.mine = pltpu.make_async_copy(self.src, self.view((0, 0), 0, self.src.shape[0]), sem)
        self.mine.start()

    def second(self, i, first, lo, hi):
        for sgn in (1, -1):
            self.go(i, 1, sgn, first, 0, lo, hi, (i, "b", first, sgn))

    def relay(self, i, first, lo, mid, hi):
        for sgn in (1, -1):
            self.wait(i, "b", first, sgn)
            a, b = (lo, mid) if sgn > 0 else (mid, hi)
            self.go(i, 1, sgn, first, -sgn, a, b, (i, "bb", first, sgn))

    def step1(self):
        for i, (lo, mid, hi) in self.flows:
            for sgn in (1, -1):
                self.wait(i, "a", sgn)
                a, b = (lo, mid) if sgn > 0 else (mid, hi)
                if not self.direct:
                    self.go(i, 0, sgn, -sgn, 0, a, b, (i, "aa", sgn))
                self.second(i, -sgn, lo, hi)

    def step2(self):
        for i, (lo, mid, hi) in self.flows:
            self.relay(i, 0, lo, mid, hi)
        for i, (lo, mid, hi) in self.flows:
            self.wait(i, "aa", 1)
            self.wait(i, "aa", -1)
            self.second(i, 2, lo, hi)

    def step3(self):
        for i, (lo, mid, hi) in self.flows:
            for first in (1, -1, 2):
                self.relay(i, first, lo, mid, hi)

    def finish(self):
        for i, _ in self.flows:
            for first in (0, 1, -1, 2):
                for sgn in (1, -1):
                    self.wait(i, "bb", first, sgn)
        self.mine.wait()


class TensorGather:
    def __init__(self, net, src, buf, wide=True, slots=None):
        self.net, self.src, self.buf, self.wide = net, src, buf, wide
        self.slots = slots or net.take(11)
        rows = src.shape[0]
        self.cut = (0, rows // 32 * 16, rows)

    def view(self, dy, other, lo, hi):
        n, (rows, cols) = self.net, self.src.shape
        slot = (n.y + dy) % 4 * 2 + ((1 - n.c) if other else n.c)
        if self.wide:
            return self.buf.at[pl.ds(lo, hi - lo), pl.ds(pl.multiple_of(slot * cols, 128), cols)]
        return self.buf.at[pl.ds(pl.multiple_of(slot * rows + lo, 16), hi - lo), :]

    def start(self):
        n = self.net
        lo, mid, hi = self.cut
        own = lambda a, b: self.src.at[pl.ds(a, b - a), :]
        put = lambda a, b, sgn: n.send(
            own(a, b), self.view(0, 0, a, b), self.view(-sgn, 0, a, b), "+y" if sgn > 0 else "-y", self.slots
        )
        self.a = {1: put(lo, mid, 1), -1: put(mid, hi, -1)}
        self.rest = {1: put(mid, hi, 1), -1: put(lo, mid, -1)}
        self.sib = [n.send(self.src, self.view(0, 0, lo, hi), self.view(0, 1, lo, hi), "c", self.slots)]

    def local(self, sem):
        self.mine = pltpu.make_async_copy(self.src, self.view(0, 0, 0, self.src.shape[0]), sem)
        self.mine.start()

    def pair(self, dy, lo, hi):
        n = self.net
        self.sib.append(n.send(self.view(dy, 0, lo, hi), self.view(dy, 0, lo, hi), self.view(dy, 1, lo, hi), "c", self.slots))

    def step1(self):
        n = self.net
        lo, mid, hi = self.cut
        self.aa = []
        for sgn in (1, -1):
            self.a[sgn].recv()
            a, b = (lo, mid) if sgn > 0 else (mid, hi)
            v = self.view(-sgn, 0, a, b)
            self.aa.append(n.send(v, v, self.view(2, 0, a, b), "+y" if sgn > 0 else "-y", self.slots))

    def step2(self):
        lo, mid, hi = self.cut
        for sgn in (1, -1):
            self.rest[sgn].recv()
            self.pair(-sgn, lo, hi)
        for m, (a, b) in zip(self.aa, ((lo, mid), (mid, hi))):
            m.recv()
            self.pair(2, a, b)

    def finish(self):
        for m in self.sib:
            m.recv()
        self.mine.wait()


def add_into(a, b):
    a[...] = (a[...].astype(F32) + b[...].astype(F32)).astype(a.dtype)


class RingScatter:
    def __init__(self, net, axis, pick, half, first, second):
        self.net, self.axis, self.pick, self.half = net, axis, pick, half
        self.first, self.second = first, second
        self.slots = net.take(6)

    def start(self):
        n = self.net
        way = lambda h: ("+", "-")[h] + self.axis
        self.one = [n.send(self.half(self.pick(2), h), self.first[h], self.first[h], way(h), self.slots) for h in (0, 1)]

    def near(self):
        n = self.net
        way = lambda h: ("+", "-")[h] + self.axis
        self.two = []
        for h, rel in ((0, 1), (1, -1)):
            dst = self.half(self.second[h], 1 - h)
            self.two.append(n.send(self.half(self.pick(rel), 1 - h), dst, dst, way(h), self.slots))

    def middle(self):
        n = self.net
        for h, rel in ((0, 1), (1, -1)):
            self.one[h].recv()
            add_into(self.half(self.pick(rel), h), self.first[h])
            dst = self.half(self.second[h], h)
            self.two.append(n.send(self.half(self.pick(rel), h), dst, dst, ("+", "-")[h] + self.axis, self.slots))

    def total(self):
        for m in self.two:
            m.recv()
        own = self.pick(0)
        return own[...].astype(F32) + self.second[0][...].astype(F32) + self.second[1][...].astype(F32)


class LineBroadcast:
    def __init__(self, net, src, dst, lsem):
        self.net, self.src, self.dst, self.lsem = net, src, dst, lsem
        self.slots = net.take(8)
        self.dy = (net.y - net.z + 4) % 4
        self.main = net.c == net.x // 2
        h = src.shape[0] // 2
        lo, hi = pl.ds(0, h), pl.ds(h, h)
        self.kinds = [(lo, "+y"), (hi, "+y"), (hi, "-y"), (lo, "-y"), (lo, "+y"), (hi, "-y"), (lo, "c"), (hi, "c")]

    def msg(self, j, a=None):
        n = self.net
        cut, d = self.kinds[j]
        a = self.dst if a is None else a
        return pltpu.make_async_remote_copy(
            src_ref=a.at[cut, :],
            dst_ref=self.dst.at[cut, :],
            send_sem=n.send_sem.at[POOL + j],
            recv_sem=n.recv_sem.at[self.slots.first + j],
            device_id=n.nbr(d),
            device_id_type=MESH,
        )

    def at(self, dy):
        return pl.when(jnp.logical_and(self.main, self.dy == dy))

    def start(self):
        @self.at(0)
        def _():
            for j in (0, 2, 1, 3, 6, 7):
                self.msg(j, self.src).start()
            pltpu.make_async_copy(self.src, self.dst, self.lsem).start()

    def middle(self):
        for dy, j, onward, half in ((1, 0, 4, 6), (3, 2, 5, 7)):

            @self.at(dy)
            def _(j=j, onward=onward, half=half):
                self.msg(j).wait_recv()
                self.msg(onward).start()
                self.msg(half).start()

    def finish(self):
        for dy, j, half in ((1, 1, 7), (3, 3, 6)):

            @self.at(dy)
            def _(j=j, half=half):
                self.msg(j).wait_recv()
                self.msg(half).start()

        @self.at(2)
        def _():
            for j, half in ((4, 6), (5, 7)):
                self.msg(j).wait_recv()
                self.msg(half).start()

        @pl.when(jnp.logical_not(self.main))
        def _():
            self.msg(6).wait_recv()
            self.msg(7).wait_recv()

        @self.at(0)
        def _():
            pltpu.make_async_copy(self.src, self.dst, self.lsem).wait()

    def drain(self):
        @self.at(0)
        def _():
            for j in range(4):
                self.msg(j, self.src).wait_send()

        for dy, onward in ((1, 4), (3, 5)):

            @self.at(dy)
            def _(onward=onward):
                self.msg(onward).wait_send()

        @pl.when(self.main)
        def _():
            self.msg(6).wait_send()
            self.msg(7).wait_send()


def plane_scatter(net, part, out, f1, f2, q, g1, g2):
    z, x = net.z, net.x
    h = part.shape[2] // 2
    zx = (z, x)
    stages = []
    for i in (0, 1):
        lo = i * h

        def pick(rel, i=i, lo=lo):
            if i == 0:
                return part.at[(z + rel) % 4, :, pl.ds(lo, h), :]
            return part.at[:, (x + rel) % 4, pl.ds(lo, h), :]

        def half(view, k):
            return view.at[pl.ds(2 * k, 2)]

        stages.append(RingScatter(net, "zx"[i], pick, half, [f1.at[i, 0], f1.at[i, 1]], [f2.at[i, 0], f2.at[i, 1]]))
    stages[0].start()
    yield
    stages[0].near()
    yield
    stages[1].start()
    stages[1].near()
    yield
    for r in stages:
        r.middle()
    yield
    later = []
    for i, r in enumerate(stages):
        q[i] = r.total().astype(q.dtype)

        def pick(rel, i=i):
            return q.at[i, (zx[1 - i] + rel) % 4]

        def half(view, k):
            return view.at[pl.ds(k * (h // 2), h // 2), :]

        later.append(RingScatter(net, "xz"[i], pick, half, [g1.at[i, 0], g1.at[i, 1]], [g2.at[i, 0], g2.at[i, 1]]))
        later[-1].start()
        later[-1].near()
    yield
    for r in later:
        r.middle()
    yield
    for i, r in enumerate(later):
        out[pl.ds(i * h, h), :] = r.total().astype(out.dtype)
        yield


def line_scatter(net, part, out, g0, q, g1, g2):
    y, c = net.y, net.c
    rows = part.shape[2]
    m = net.send(part.at[1 - c], g0, g0, "c", net.take(1))
    yield
    m.recv()
    q[...] = (part[c].astype(F32) + g0[...].astype(F32)).astype(q.dtype)
    cut = rows // 32 * 16

    def pick(rel):
        return q.at[(y + rel) % 4]

    def half(view, k):
        return view.at[pl.ds(0, cut), :] if k == 0 else view.at[pl.ds(cut, rows - cut), :]

    ring = RingScatter(net, "y", pick, half, [g1.at[pl.ds(0, cut)], g1.at[pl.ds(cut, rows - cut)]], [g2.at[0], g2.at[1]])
    ring.start()
    ring.near()
    yield
    ring.middle()
    yield
    out[...] = ring.total().astype(out.dtype)


def dot(a, b):
    return jnp.dot(a, b, preferred_element_type=F32)


def dot_tn(a, b):
    return lax.dot_general(a, b, (((0,), (0,)), ((), ())), preferred_element_type=F32)


def dot_nt(a, b):
    return lax.dot_general(a, b, (((1,), (1,)), ((), ())), preferred_element_type=F32)


SEMS, POOL = 208, 56
ROWS, COLS, LROWS = FF // 16, FF // 8, D // 16
BUFFERS = dict(
    lq=((LROWS, D), BF),
    rq=((ROWS, COLS), BF),
    gcols=((D, COLS), BF),
    lall=((D, D), BF),
    qcols=((FF, COLS), BF),
    gs_own=((D, ROWS), BF),
    gs=((D, ROWS), BF),
    lterms=((LROWS, D), BF),
    lparts=((8 * LROWS, D), BF),
    half_all=((D, COLS), BF),
    half_rows=((LROWS, FF), BF),
    s_b=((ROWS, COLS), BF),
    s_rows=((ROWS, FF), BF),
    p=((ROWS, COLS), F32),
    p_b=((ROWS, COLS), BF),
    p_rows=((ROWS, FF), BF),
    dir_b=((LROWS, COLS), BF),
    dir_cols=((D, COLS), BF),
    pl_own=((LROWS, D), F32),
    pl_b=((LROWS, D), BF),
    pl_all=((D, D), BF),
    gl=((D, D), BF),
    wl=((D, D), BF),
    tile=((8, 128), F32),
    tiles=((128, 128), F32),
    part=((4, 4, ROWS, COLS), BF),
    f1=((2, 2, 2, ROWS // 2, COLS), BF),
    f2=((2, 2, 4, ROWS // 2, COLS), BF),
    fq=((2, 4, ROWS // 2, COLS), BF),
    fg1=((2, 2, ROWS // 4, COLS), BF),
    fg2=((2, 2, ROWS // 2, COLS), BF),
    a_b=((ROWS, COLS), BF),
    a_cols=((FF, COLS), BF),
    y1_b=((ROWS, COLS), BF),
    y1_rows=((ROWS, FF), BF),
    y2_b=((ROWS, COLS), BF),
    y2_rows=((ROWS, FF), BF),
    y3_b=((ROWS, COLS), BF),
    y3_rows=((ROWS, FF), BF),
    upart=((2, 4, LROWS, COLS), BF),
    u0=((4, LROWS, COLS), BF),
    uq=((4, LROWS, COLS), BF),
    u1=((LROWS, COLS), BF),
    u2=((2, LROWS, COLS), BF),
)
NBR = ("+x", "-x", "2x", "+z", "-z", "2z", "+y", "-y", "c")


def kernel(*refs):
    b = dict(zip(BUFFERS, refs[14 : 14 + len(BUFFERS)]))
    send_sem, recv_sem, lsem = refs[14 + len(BUFFERS) : 17 + len(BUFFERS)]
    inputs, outputs = refs[17 + len(BUFFERS) : 24 + len(BUFFERS)], refs[24 + len(BUFFERS) :]
    update, new_m1, new_m2, new_sl, new_sr, new_bl, new_br = outputs
    stores = [pltpu.make_async_copy(outputs[k], refs[7 + k], lsem.at[23 + k]) for k in range(7)]
    grad, m1, m2, stat_l, stat_r, basis_l, basis_r = inputs
    loads = [pltpu.make_async_copy(refs[k], inputs[k], lsem.at[16 + k]) for k in range(7)]
    for k in (0, 5, 6, 4, 3, 1, 2):
        loads[k].start()
    net = Net(send_sem, recv_sem)
    x, s = net.x, net.s
    own_left = pl.ds(pl.multiple_of(s * LROWS, 16), LROWS)
    lanes = lambda c: pl.ds(pl.multiple_of(c * (D // 2), 128), D // 2)
    locals_used = [0]

    def begin(*gathers):
        for g in gathers:
            g.start()
            g.local(lsem.at[locals_used[0]])
            locals_used[0] += 1

    def swap(ref):
        mine = ref.at[:, lanes(net.c)]
        return net.send(mine, mine, ref.at[:, lanes(1 - net.c)], "c", net.take(1))

    net.greet(NBR)
    loads[0].wait()
    net.meet(NBR)

    g_grad = ShardGather(net, grad, b["gcols"], direct=True)
    begin(g_grad)
    loads[5].wait()
    b["lq"][...] = (basis_l[...] * (1.0 / math.sqrt(D))).astype(BF)
    loads[6].wait()
    b["rq"][...] = (basis_r[...] * (1.0 / math.sqrt(FF))).astype(BF)
    for k in (4, 3, 1, 2):
        loads[k].wait()
    g_left = ShardGather(net, b["lq"].at[:, lanes(net.c)], b["lall"].at[:, lanes(net.c)])
    g_right = ShardGather(net, b["rq"], b["qcols"])
    g_grad.step1()
    begin(g_left)
    g_grad.step2()
    g_left.step1()
    g_grad.step3()
    begin(g_right)
    g_left.step2()
    g_grad.finish()
    cast = LineBroadcast(net, b["gs_own"], b["gs"], lsem.at[locals_used[0]])
    locals_used[0] += 1
    pick = lax.broadcasted_iota(jnp.int32, (COLS, ROWS), 0) == lax.broadcasted_iota(
        jnp.int32, (COLS, ROWS), 1
    ) + ROWS * (x % 2)
    gcols = b["gcols"]
    b["gs_own"][...] = dot(gcols[...], jnp.where(pick, 1.0, 0.0).astype(BF)).astype(BF)
    cast.start()
    b["lterms"][...] = dot_nt(grad[...], gcols[...]).astype(BF)
    t_lterms = TensorGather(net, b["lterms"], b["lparts"], wide=False)
    begin(t_lterms)
    g_right.step1()
    cast.middle()
    g_right.step2()
    g_left.step3()
    t_lterms.step1()
    cast.finish()

    new_sr[...] = beta * stat_r[...] + ((1.0 - beta) / D) * dot_tn(b["gs"][...], gcols[...])
    b["s_b"][...] = new_sr[...].astype(BF)
    t_stat = TensorGather(net, b["s_b"], b["s_rows"])
    begin(t_stat)
    stores[4].start()
    t_lterms.step2()
    g_right.step3()
    t_stat.step1()
    g_left.finish()
    left_swap = swap(b["lall"])
    left_swap.recv()
    t_lterms.finish()
    gram = b["lparts"][pl.ds(0, LROWS), :].astype(F32)
    for j in range(1, 8):
        gram += b["lparts"][pl.ds(j * LROWS, LROWS), :].astype(F32)
    new_sl[...] = beta * stat_l[...] + ((1.0 - beta) / FF) * gram
    b["pl_own"][...] = dot(new_sl[...].astype(BF), b["lall"][...])
    b["pl_b"][...] = b["pl_own"][...].astype(BF)
    g_pl = ShardGather(
        net, b["pl_b"].at[:, lanes(net.c)], b["pl_all"].at[:, lanes(net.c)], slots=g_grad.slots.again()
    )
    begin(g_pl)
    stores[3].start()
    b["half_all"][...] = dot_tn(b["lall"][...], gcols[...]).astype(BF)
    t_half = TensorGather(net, b["half_all"].at[own_left, :], b["half_rows"])
    t_stat.step2()
    begin(t_half)
    g_right.finish()
    t_stat.finish()
    b["p"][...] = dot(b["s_rows"][...], b["qcols"][...])
    b["p_b"][...] = b["p"][...].astype(BF)
    t_power = TensorGather(net, b["p_b"], b["p_rows"])
    begin(t_power)
    g_pl.step1()
    t_half.step1()
    t_power.step1()
    g_pl.step2()
    t_half.step2()
    t_power.step2()
    g_pl.step3()
    t_power.finish()

    def term(rel):
        zt = (net.z + rel) % 4
        v = dot_tn(b["p_rows"][:, pl.ds(pl.multiple_of(zt * D, 128), D)], b["p_b"][...]).astype(BF)
        b["part"][zt] = v.reshape(4, ROWS, COLS)

    scatter = plane_scatter(net, b["part"], b["a_b"], b["f1"], b["f2"], b["fq"], b["fg1"], b["fg2"])
    term(2)
    next(scatter)
    term(1)
    term(3)
    next(scatter)
    term(0)
    next(scatter)

    def squares(j, total):
        v = b["p_rows"][pl.ds(pl.multiple_of(j * 16, 16), 16), :].astype(F32)
        return total + jnp.sum(v * v, axis=0, keepdims=True)

    total = lax.fori_loop(0, ROWS // 16, squares, jnp.zeros((1, FF), F32))
    b["tile"][...] = jnp.broadcast_to(jnp.sum(total, keepdims=True), (8, 128))
    g_tile = ShardGather(net, b["tile"], b["tiles"], slots=g_left.slots.again())
    begin(g_tile)
    t_half.finish()
    rot = dot(b["half_rows"][...], b["qcols"][...])
    first = beta * m1[...] + (1.0 - beta) * rot
    second = beta * m2[...] + (1.0 - beta) * (rot * rot)
    new_m1[...] = first
    new_m2[...] = second
    stores[1].start()
    stores[2].start()
    b["dir_b"][...] = ((first / correction) / (jnp.sqrt(second / correction) + adam_eps)).astype(BF)
    next(scatter)
    g_pl.finish()
    pl_swap = swap(b["pl_all"])
    pl_swap.recv()

    def left_squares(j, total):
        v = b["pl_all"][pl.ds(pl.multiple_of(j * 16, 16), 16), :].astype(F32)
        return total + jnp.sum(v * v, axis=0, keepdims=True)

    def left_gram(ref, factor, lo, hi):
        for j in range(lo, hi):
            cut = pl.ds(j * 128, 128)
            b["gl"][cut, :] = (dot_tn(ref[:, cut], ref[...]) * factor).astype(BF)

    left_total = lax.fori_loop(0, D // 16, left_squares, jnp.zeros((1, D), F32))
    left_scale = math.sqrt(D) / (4.0 * jnp.sqrt(jnp.sum(left_total, keepdims=True)))
    left_gram(b["pl_all"], left_scale * left_scale, 0, 4)
    g_tile.step1()
    next(scatter)
    g_tile.step2()
    left_gram(b["pl_all"], left_scale * left_scale, 4, 5)
    next(scatter)
    g_tile.step3()
    left_gram(b["pl_all"], left_scale * left_scale, 5, 6)
    g_a = ShardGather(net, b["a_b"], b["a_cols"], slots=g_right.slots.again())
    next(scatter)
    g_a.start((0,))
    next(scatter)
    g_a.start((1,))
    g_a.local(lsem.at[locals_used[0]])
    locals_used[0] += 1
    for j in range(3):
        cut = pl.ds(j * 256, 256)
        v = b["pl_all"][cut, :]
        b["wl"][cut, :] = (left_scale * (1.5 * v.astype(F32) - 0.5 * dot(v, b["gl"][...]))).astype(BF)
    mine = left_scale * (1.5 * b["pl_own"][...] - 0.5 * dot(b["pl_b"][...], b["gl"][...]))
    g_a.step1()
    left_gram(b["wl"], 1.0, 0, 5)
    g_a.step2()
    left_gram(b["wl"], 1.0, 5, 6)
    new_bl[...] = math.sqrt(D) * (1.5 * mine - 0.5 * dot(mine.astype(BF), b["gl"][...]))
    stores[5].start()
    g_a.step3()
    g_dir = ShardGather(net, b["dir_b"], b["dir_cols"], slots=g_grad.slots.again())
    g_tile.finish()
    norm = jnp.sum(b["tiles"][...], keepdims=True) / 1024.0
    scale = math.sqrt(FF) / (4.0 * jnp.sqrt(norm))
    square = scale * scale
    g_a.finish()

    def mix(rows, factor, add, out, all_rows, before):
        v = dot(b[rows][...], b["a_cols"][...])
        b[out][...] = (factor * v + add * b["p"][...]).astype(BF)
        g = TensorGather(net, b[out], b[all_rows], slots=before.slots.again())
        begin(g)
        return g

    t_y = mix("p_rows", 0.0625 * square, -0.5625, "y1_b", "y1_rows", t_stat)
    begin(g_dir)
    t_y.step1()
    g_dir.step1()
    t_y.step2()
    g_dir.step2()
    t_y.finish()
    t_y = mix("y1_rows", square, 1.6875, "y2_b", "y2_rows", t_power)
    g_dir.step3()
    t_y.step1()
    g_dir.finish()
    back = dot(b["lq"][...], b["dir_cols"][...]).astype(BF)
    for j in range(8):
        b["upart"][j % 2, j // 2] = dot_nt(back, b["qcols"][pl.ds(j * COLS, COLS), :]).astype(BF)
    to_update = line_scatter(net, b["upart"], update, b["u0"], b["uq"], b["u1"], b["u2"])
    next(to_update)
    t_y.step2()
    t_y.finish()
    t_y = mix("y2_rows", square, -2.4375, "y3_b", "y3_rows", t_stat)
    next(to_update)
    t_y.step1()
    next(to_update)
    t_y.step2()
    t_y.finish()
    v = dot(b["y3_rows"][...], b["a_cols"][...])
    new_br[...] = (math.sqrt(FF) * scale) * (2.25 * b["p"][...] + square * v)
    stores[6].start()
    for _ in to_update:
        pass
    stores[0].start()
    assert net.taken <= SEMS and locals_used[0] <= 16
    cast.drain()
    net.drain()
    for store in stores:
        store.wait()


def emit(*refs):
    held, sem = refs[14:21], refs[21]
    into = [pltpu.make_async_copy(refs[k], held[k], sem.at[0, k]) for k in range(7)]
    onto = [pltpu.make_async_copy(held[k], refs[7 + k], sem.at[1, k]) for k in range(7)]
    for copy in into:
        copy.start()
    for copy, store in zip(into, onto):
        copy.wait()
        store.start()
    for store in onto:
        store.wait()


def local(gradient, moment_one, moment_two, stat_left, stat_right, basis_left, basis_right):
    args = (gradient, moment_one, moment_two, stat_left, stat_right, basis_left, basis_right)
    out = pl.pallas_call(
        kernel,
        out_shape=[jax.ShapeDtypeStruct(a.shape, a.dtype) for a in args],
        in_specs=[pl.BlockSpec(memory_space=pl.ANY)] * 7,
        out_specs=[pl.BlockSpec(memory_space=pl.ANY)] * 7,
        scratch_shapes=[pltpu.VMEM(shape, dtype) for shape, dtype in BUFFERS.values()]
        + [
            pltpu.SemaphoreType.DMA((POOL + 8,)),
            pltpu.SemaphoreType.DMA((SEMS,)),
            pltpu.SemaphoreType.DMA((30,)),
        ]
        + [pltpu.VMEM(a.shape, a.dtype) for a in args * 2],
        compiler_params=pltpu.CompilerParams(
            collective_id=0, has_side_effects=True, vmem_limit_bytes=63 * 2**20
        ),
        name="step",
    )(*args)
    hbm = pl.BlockSpec(memory_space=pl.ANY)
    return pl.pallas_call(
        emit,
        out_shape=[jax.ShapeDtypeStruct(a.shape, a.dtype) for a in args],
        in_specs=[hbm] * 7,
        out_specs=[hbm] * 7,
        scratch_shapes=[pltpu.VMEM(a.shape, a.dtype) for a in args] + [pltpu.SemaphoreType.DMA((2, 7))],
        compiler_params=pltpu.CompilerParams(vmem_limit_bytes=63 * 2**20),
        name="emit",
    )(*out)


def solution(mesh):
    both, row = P("shard", "tensor"), P("shard", None)
    return jax.shard_map(
        local,
        mesh=mesh,
        in_specs=(both, both, both, row, both, row, both),
        out_specs=(both, both, both, row, both, row, both),
        check_vma=False,
    )
```

```python
import functools
import math

import jax
import jax.numpy as jnp
from jax import lax
from jax.experimental import pallas as pl
from jax.experimental.pallas import tpu as pltpu
from jax.sharding import PartitionSpec as P

D = 768
FF = 3072
BF = jnp.bfloat16
F32 = jnp.float32
MESH = pl.DeviceIdType.MESH

beta = 0.95
correction = 1.0 - 0.95**10
adam_eps = 1e-08


class Move:
    def __init__(self, landing):
        self.landing = landing

    def recv(self):
        self.landing.wait_recv()


class Slots:
    def __init__(self, first, count):
        self.first, self.count, self.used = first, count, 0

    def next(self):
        self.used += 1
        assert self.used <= self.count
        return self.first + self.used - 1

    def again(self):
        return Slots(self.first, self.count)


class Net:
    def __init__(self, send_sem, recv_sem):
        self.send_sem, self.recv_sem = send_sem, recv_sem
        self.count = 0
        self.taken = 0
        self.sent = {}
        s, t = lax.axis_index("shard"), lax.axis_index("tensor")
        self.s, self.t = s, t
        self.z, self.x = s // 4, s % 4
        self.y, self.c = t // 2, t % 2

    def take(self, count):
        self.taken += count
        return Slots(self.taken - count, count)

    def nbr(self, d):
        s, t = self.s, self.t
        z, x, y, c = self.z, self.x, self.y, self.c
        if d == "c":
            return (s, y * 2 + 1 - c)
        step = {"+": 1, "2": 2, "-": 3}[d[0]]
        if d[1] == "x":
            return (z * 4 + (x + step) % 4, t)
        if d[1] == "z":
            return (((z + step) % 4) * 4 + x, t)
        return (s, ((y + step) % 4) * 2 + c)

    def greet(self, dirs):
        sem = pltpu.get_barrier_semaphore()
        for d in dirs:
            pl.semaphore_signal(sem, inc=1, device_id=self.nbr(d), device_id_type=MESH)

    def meet(self, dirs):
        pl.semaphore_wait(pltpu.get_barrier_semaphore(), len(dirs))

    def send(self, src, dst, landing, d, slots):
        k, r = self.count % POOL, slots.next()
        self.count += 1
        if k in self.sent:
            self.sent[k].wait_send()
        mk = lambda a, b: pltpu.make_async_remote_copy(
            src_ref=a,
            dst_ref=b,
            send_sem=self.send_sem.at[k],
            recv_sem=self.recv_sem.at[r],
            device_id=self.nbr(d),
            device_id_type=MESH,
        )
        self.sent[k] = mk(src, dst)
        self.sent[k].start()
        return Move(mk(landing, landing))

    def drain(self):
        for copy in self.sent.values():
            copy.wait_send()
        self.sent = {}


def cuts(rows):
    if rows % 64 == 0:
        q = rows // 4
        return ((0, q, 2 * q), (2 * q, 3 * q, 4 * q))
    if rows == 48:
        return ((0, 16, 32), (32, 48, 48))
    return ((0, rows, rows), None)


class ShardGather:
    def __init__(self, net, src, buf, direct=False, slots=None):
        self.net, self.src, self.buf, self.direct = net, src, buf, direct
        self.flows = [(i, f) for i, f in enumerate(cuts(src.shape[0])) if f is not None]
        self.m = {}
        self.slots = slots or net.take(40 if self.flows[-1][0] else 20)

    def view(self, blk, lo, hi):
        n, rows = self.net, self.src.shape[0]
        slot = (n.z + blk[0]) % 4 * 4 + (n.x + blk[1]) % 4
        return self.buf.at[pl.ds(pl.multiple_of(slot * rows + lo, 8), hi - lo), :]

    def axes(self, i):
        return ("x", "z") if i == 0 else ("z", "x")

    def rel(self, i, first, second):
        return (second, first) if i == 0 else (first, second)

    def go(self, i, stage, sgn, first, second, lo, hi, key, own=False):
        if hi == lo:
            return
        axis = self.axes(i)[stage]
        d = ("+" if sgn > 0 else "-") + axis
        blk = self.rel(i, first, second)
        lf, ls = (first - sgn, second) if stage == 0 else (first, second - sgn)
        src = self.src.at[pl.ds(lo, hi - lo), :] if own else self.view(blk, lo, hi)
        self.m[key] = self.net.send(src, self.view(blk, lo, hi), self.view(self.rel(i, lf, ls), lo, hi), d, self.slots)

    def wait(self, *key):
        if key in self.m:
            self.m[key].recv()

    def start(self, only=(0, 1)):
        n = self.net
        flows = [f for f in self.flows if f[0] in only]
        for i, (lo, mid, hi) in flows:
            for sgn in (1, -1):
                self.go(i, 0, sgn, 0, 0, lo, hi, (i, "a", sgn), own=True)
            if self.direct:
                src = self.src.at[pl.ds(lo, hi - lo), :]
                landing = self.view(self.rel(i, 2, 0), lo, hi)
                self.m[i, "aa", 1] = n.send(src, self.view((0, 0), lo, hi), landing, "2" + self.axes(i)[0], self.slots)
        for i, (lo, mid, hi) in flows:
            for sgn in (1, -1):
                self.go(i, 1, sgn, 0, 0, lo, hi, (i, "b", 0, sgn), own=True)

    def local(self, sem):
        n = self.net
        self.mine = pltpu.make_async_copy(self.src, self.view((0, 0), 0, self.src.shape[0]), sem)
        self.mine.start()

    def second(self, i, first, lo, hi):
        for sgn in (1, -1):
            self.go(i, 1, sgn, first, 0, lo, hi, (i, "b", first, sgn))

    def relay(self, i, first, lo, mid, hi):
        for sgn in (1, -1):
            self.wait(i, "b", first, sgn)
            a, b = (lo, mid) if sgn > 0 else (mid, hi)
            self.go(i, 1, sgn, first, -sgn, a, b, (i, "bb", first, sgn))

    def step1(self):
        for i, (lo, mid, hi) in self.flows:
            for sgn in (1, -1):
                self.wait(i, "a", sgn)
                a, b = (lo, mid) if sgn > 0 else (mid, hi)
                if not self.direct:
                    self.go(i, 0, sgn, -sgn, 0, a, b, (i, "aa", sgn))
                self.second(i, -sgn, lo, hi)

    def step2(self):
        for i, (lo, mid, hi) in self.flows:
            self.relay(i, 0, lo, mid, hi)
        for i, (lo, mid, hi) in self.flows:
            self.wait(i, "aa", 1)
            self.wait(i, "aa", -1)
            self.second(i, 2, lo, hi)

    def step3(self):
        for i, (lo, mid, hi) in self.flows:
            for first in (1, -1, 2):
                self.relay(i, first, lo, mid, hi)

    def finish(self):
        for i, _ in self.flows:
            for first in (0, 1, -1, 2):
                for sgn in (1, -1):
                    self.wait(i, "bb", first, sgn)
        self.mine.wait()


class TensorGather:
    def __init__(self, net, src, buf, wide=True, slots=None):
        self.net, self.src, self.buf, self.wide = net, src, buf, wide
        self.slots = slots or net.take(11)
        rows = src.shape[0]
        self.cut = (0, rows // 32 * 16, rows)

    def view(self, dy, other, lo, hi):
        n, (rows, cols) = self.net, self.src.shape
        slot = (n.y + dy) % 4 * 2 + ((1 - n.c) if other else n.c)
        if self.wide:
            return self.buf.at[pl.ds(lo, hi - lo), pl.ds(pl.multiple_of(slot * cols, 128), cols)]
        return self.buf.at[pl.ds(pl.multiple_of(slot * rows + lo, 16), hi - lo), :]

    def start(self):
        n = self.net
        lo, mid, hi = self.cut
        own = lambda a, b: self.src.at[pl.ds(a, b - a), :]
        put = lambda a, b, sgn: n.send(
            own(a, b), self.view(0, 0, a, b), self.view(-sgn, 0, a, b), "+y" if sgn > 0 else "-y", self.slots
        )
        self.a = {1: put(lo, mid, 1), -1: put(mid, hi, -1)}
        self.rest = {1: put(mid, hi, 1), -1: put(lo, mid, -1)}
        self.sib = [n.send(self.src, self.view(0, 0, lo, hi), self.view(0, 1, lo, hi), "c", self.slots)]

    def local(self, sem):
        self.mine = pltpu.make_async_copy(self.src, self.view(0, 0, 0, self.src.shape[0]), sem)
        self.mine.start()

    def pair(self, dy, lo, hi):
        n = self.net
        self.sib.append(n.send(self.view(dy, 0, lo, hi), self.view(dy, 0, lo, hi), self.view(dy, 1, lo, hi), "c", self.slots))

    def step1(self):
        n = self.net
        lo, mid, hi = self.cut
        self.aa = []
        for sgn in (1, -1):
            self.a[sgn].recv()
            a, b = (lo, mid) if sgn > 0 else (mid, hi)
            v = self.view(-sgn, 0, a, b)
            self.aa.append(n.send(v, v, self.view(2, 0, a, b), "+y" if sgn > 0 else "-y", self.slots))

    def step2(self):
        lo, mid, hi = self.cut
        for sgn in (1, -1):
            self.rest[sgn].recv()
            self.pair(-sgn, lo, hi)
        for m, (a, b) in zip(self.aa, ((lo, mid), (mid, hi))):
            m.recv()
            self.pair(2, a, b)

    def finish(self):
        for m in self.sib:
            m.recv()
        self.mine.wait()


def add_into(a, b):
    a[...] = (a[...].astype(F32) + b[...].astype(F32)).astype(a.dtype)


class RingScatter:
    def __init__(self, net, axis, pick, half, first, second):
        self.net, self.axis, self.pick, self.half = net, axis, pick, half
        self.first, self.second = first, second
        self.slots = net.take(6)

    def start(self):
        n = self.net
        way = lambda h: ("+", "-")[h] + self.axis
        self.one = [n.send(self.half(self.pick(2), h), self.first[h], self.first[h], way(h), self.slots) for h in (0, 1)]

    def near(self):
        n = self.net
        way = lambda h: ("+", "-")[h] + self.axis
        self.two = []
        for h, rel in ((0, 1), (1, -1)):
            dst = self.half(self.second[h], 1 - h)
            self.two.append(n.send(self.half(self.pick(rel), 1 - h), dst, dst, way(h), self.slots))

    def middle(self):
        n = self.net
        for h, rel in ((0, 1), (1, -1)):
            self.one[h].recv()
            add_into(self.half(self.pick(rel), h), self.first[h])
            dst = self.half(self.second[h], h)
            self.two.append(n.send(self.half(self.pick(rel), h), dst, dst, ("+", "-")[h] + self.axis, self.slots))

    def total(self):
        for m in self.two:
            m.recv()
        own = self.pick(0)
        return own[...].astype(F32) + self.second[0][...].astype(F32) + self.second[1][...].astype(F32)


class LineBroadcast:
    def __init__(self, net, src, dst, lsem):
        self.net, self.src, self.dst, self.lsem = net, src, dst, lsem
        self.slots = net.take(8)
        self.dy = (net.y - net.z + 4) % 4
        self.main = net.c == net.x // 2
        h = src.shape[0] // 2
        lo, hi = pl.ds(0, h), pl.ds(h, h)
        self.kinds = [(lo, "+y"), (hi, "+y"), (hi, "-y"), (lo, "-y"), (lo, "+y"), (hi, "-y"), (lo, "c"), (hi, "c")]

    def msg(self, j, a=None):
        n = self.net
        cut, d = self.kinds[j]
        a = self.dst if a is None else a
        return pltpu.make_async_remote_copy(
            src_ref=a.at[cut, :],
            dst_ref=self.dst.at[cut, :],
            send_sem=n.send_sem.at[POOL + j],
            recv_sem=n.recv_sem.at[self.slots.first + j],
            device_id=n.nbr(d),
            device_id_type=MESH,
        )

    def at(self, dy):
        return pl.when(jnp.logical_and(self.main, self.dy == dy))

    def start(self):
        @self.at(0)
        def _():
            for j in (0, 2, 1, 3, 6, 7):
                self.msg(j, self.src).start()
            pltpu.make_async_copy(self.src, self.dst, self.lsem).start()

    def middle(self):
        for dy, j, onward, half in ((1, 0, 4, 6), (3, 2, 5, 7)):

            @self.at(dy)
            def _(j=j, onward=onward, half=half):
                self.msg(j).wait_recv()
                self.msg(onward).start()
                self.msg(half).start()

    def finish(self):
        for dy, j, half in ((1, 1, 7), (3, 3, 6)):

            @self.at(dy)
            def _(j=j, half=half):
                self.msg(j).wait_recv()
                self.msg(half).start()

        @self.at(2)
        def _():
            for j, half in ((4, 6), (5, 7)):
                self.msg(j).wait_recv()
                self.msg(half).start()

        @pl.when(jnp.logical_not(self.main))
        def _():
            self.msg(6).wait_recv()
            self.msg(7).wait_recv()

        @self.at(0)
        def _():
            pltpu.make_async_copy(self.src, self.dst, self.lsem).wait()

    def drain(self):
        @self.at(0)
        def _():
            for j in range(4):
                self.msg(j, self.src).wait_send()

        for dy, onward in ((1, 4), (3, 5)):

            @self.at(dy)
            def _(onward=onward):
                self.msg(onward).wait_send()

        @pl.when(self.main)
        def _():
            self.msg(6).wait_send()
            self.msg(7).wait_send()


def plane_scatter(net, part, out, f1, f2, q, g1, g2):
    z, x = net.z, net.x
    h = part.shape[2] // 2
    zx = (z, x)
    stages = []
    for i in (0, 1):
        lo = i * h

        def pick(rel, i=i, lo=lo):
            if i == 0:
                return part.at[(z + rel) % 4, :, pl.ds(lo, h), :]
            return part.at[:, (x + rel) % 4, pl.ds(lo, h), :]

        def half(view, k):
            return view.at[pl.ds(2 * k, 2)]

        stages.append(RingScatter(net, "zx"[i], pick, half, [f1.at[i, 0], f1.at[i, 1]], [f2.at[i, 0], f2.at[i, 1]]))
    stages[0].start()
    yield
    stages[0].near()
    yield
    stages[1].start()
    stages[1].near()
    yield
    for r in stages:
        r.middle()
    yield
    later = []
    for i, r in enumerate(stages):
        q[i] = r.total().astype(q.dtype)

        def pick(rel, i=i):
            return q.at[i, (zx[1 - i] + rel) % 4]

        def half(view, k):
            return view.at[pl.ds(k * (h // 2), h // 2), :]

        later.append(RingScatter(net, "xz"[i], pick, half, [g1.at[i, 0], g1.at[i, 1]], [g2.at[i, 0], g2.at[i, 1]]))
        later[-1].start()
        later[-1].near()
    yield
    for r in later:
        r.middle()
    yield
    for i, r in enumerate(later):
        out[pl.ds(i * h, h), :] = r.total().astype(out.dtype)
        yield


def line_scatter(net, part, out, g0, q, g1, g2):
    y, c = net.y, net.c
    rows = part.shape[2]
    m = net.send(part.at[1 - c], g0, g0, "c", net.take(1))
    yield
    m.recv()
    q[...] = (part[c].astype(F32) + g0[...].astype(F32)).astype(q.dtype)
    cut = rows // 32 * 16

    def pick(rel):
        return q.at[(y + rel) % 4]

    def half(view, k):
        return view.at[pl.ds(0, cut), :] if k == 0 else view.at[pl.ds(cut, rows - cut), :]

    ring = RingScatter(net, "y", pick, half, [g1.at[pl.ds(0, cut)], g1.at[pl.ds(cut, rows - cut)]], [g2.at[0], g2.at[1]])
    ring.start()
    ring.near()
    yield
    ring.middle()
    yield
    out[...] = ring.total().astype(out.dtype)


def dot(a, b):
    return jnp.dot(a, b, preferred_element_type=F32)


def dot_tn(a, b):
    return lax.dot_general(a, b, (((0,), (0,)), ((), ())), preferred_element_type=F32)


def dot_nt(a, b):
    return lax.dot_general(a, b, (((1,), (1,)), ((), ())), preferred_element_type=F32)


SEMS, POOL = 208, 40
ROWS, COLS, LROWS = FF // 16, FF // 8, D // 16
BUFFERS = dict(
    lq=((LROWS, D), BF),
    rq=((ROWS, COLS), BF),
    gcols=((D, COLS), BF),
    lall=((D, D), BF),
    qcols=((FF, COLS), BF),
    gs_own=((D, ROWS), BF),
    gs=((D, ROWS), BF),
    lterms=((LROWS, D), BF),
    lparts=((8 * LROWS, D), BF),
    half_all=((D, COLS), BF),
    half_rows=((LROWS, FF), BF),
    s_b=((ROWS, COLS), BF),
    s_rows=((ROWS, FF), BF),
    p=((ROWS, COLS), F32),
    p_b=((ROWS, COLS), BF),
    p_rows=((ROWS, FF), BF),
    dir_b=((LROWS, COLS), BF),
    dir_cols=((D, COLS), BF),
    pl_own=((LROWS, D), F32),
    pl_b=((LROWS, D), BF),
    pl_all=((D, D), BF),
    gl=((D, D), BF),
    wl=((D, D), BF),
    tile=((8, 128), F32),
    tiles=((128, 128), F32),
    part=((4, 4, ROWS, COLS), BF),
    f1=((2, 2, 2, ROWS // 2, COLS), BF),
    f2=((2, 2, 4, ROWS // 2, COLS), BF),
    fq=((2, 4, ROWS // 2, COLS), BF),
    fg1=((2, 2, ROWS // 4, COLS), BF),
    fg2=((2, 2, ROWS // 2, COLS), BF),
    a_b=((ROWS, COLS), BF),
    a_cols=((FF, COLS), BF),
    y1_b=((ROWS, COLS), BF),
    y1_rows=((ROWS, FF), BF),
    y2_b=((ROWS, COLS), BF),
    y2_rows=((ROWS, FF), BF),
    y3_b=((ROWS, COLS), BF),
    y3_rows=((ROWS, FF), BF),
    upart=((2, 4, LROWS, COLS), BF),
    u0=((4, LROWS, COLS), BF),
    uq=((4, LROWS, COLS), BF),
    u1=((LROWS, COLS), BF),
    u2=((2, LROWS, COLS), BF),
)
NBR = ("+x", "-x", "2x", "+z", "-z", "2z", "+y", "-y", "c")


def kernel(*refs):
    b = dict(zip(BUFFERS, refs[14 : 14 + len(BUFFERS)]))
    send_sem, recv_sem, lsem = refs[14 + len(BUFFERS) : 17 + len(BUFFERS)]
    inputs, outputs = refs[17 + len(BUFFERS) : 24 + len(BUFFERS)], refs[24 + len(BUFFERS) :]
    update, new_m1, new_m2, new_sl, new_sr, new_bl, new_br = outputs
    stores = [pltpu.make_async_copy(outputs[k], refs[7 + k], lsem.at[23 + k]) for k in range(7)]
    grad, m1, m2, stat_l, stat_r, basis_l, basis_r = inputs
    loads = [pltpu.make_async_copy(refs[k], inputs[k], lsem.at[16 + k]) for k in range(7)]
    for k in (0, 5, 6, 4, 3, 1, 2):
        loads[k].start()
    net = Net(send_sem, recv_sem)
    x, s = net.x, net.s
    own_left = pl.ds(pl.multiple_of(s * LROWS, 16), LROWS)
    lanes = lambda c: pl.ds(pl.multiple_of(c * (D // 2), 128), D // 2)
    locals_used = [0]

    def begin(*gathers):
        for g in gathers:
            g.start()
            g.local(lsem.at[locals_used[0]])
            locals_used[0] += 1

    def swap(ref):
        mine = ref.at[:, lanes(net.c)]
        return net.send(mine, mine, ref.at[:, lanes(1 - net.c)], "c", net.take(1))

    net.greet(NBR)
    loads[0].wait()
    net.meet(NBR)

    g_grad = ShardGather(net, grad, b["gcols"], direct=True)
    begin(g_grad)
    loads[5].wait()
    b["lq"][...] = (basis_l[...] * (1.0 / math.sqrt(D))).astype(BF)
    loads[6].wait()
    b["rq"][...] = (basis_r[...] * (1.0 / math.sqrt(FF))).astype(BF)
    for k in (4, 3, 1, 2):
        loads[k].wait()
    g_left = ShardGather(net, b["lq"].at[:, lanes(net.c)], b["lall"].at[:, lanes(net.c)])
    g_right = ShardGather(net, b["rq"], b["qcols"])
    g_grad.step1()
    begin(g_left)
    g_grad.step2()
    g_left.step1()
    g_grad.step3()
    begin(g_right)
    g_left.step2()
    g_grad.finish()
    cast = LineBroadcast(net, b["gs_own"], b["gs"], lsem.at[locals_used[0]])
    locals_used[0] += 1
    pick = lax.broadcasted_iota(jnp.int32, (COLS, ROWS), 0) == lax.broadcasted_iota(
        jnp.int32, (COLS, ROWS), 1
    ) + ROWS * (x % 2)
    gcols = b["gcols"]
    b["gs_own"][...] = dot(gcols[...], jnp.where(pick, 1.0, 0.0).astype(BF)).astype(BF)
    cast.start()
    b["lterms"][...] = dot_nt(grad[...], gcols[...]).astype(BF)
    t_lterms = TensorGather(net, b["lterms"], b["lparts"], wide=False)
    begin(t_lterms)
    g_right.step1()
    cast.middle()
    g_right.step2()
    g_left.step3()
    t_lterms.step1()
    cast.finish()

    new_sr[...] = beta * stat_r[...] + ((1.0 - beta) / D) * dot_tn(b["gs"][...], gcols[...])
    b["s_b"][...] = new_sr[...].astype(BF)
    t_stat = TensorGather(net, b["s_b"], b["s_rows"])
    begin(t_stat)
    stores[4].start()
    t_lterms.step2()
    g_right.step3()
    t_stat.step1()
    g_left.finish()
    left_swap = swap(b["lall"])
    left_swap.recv()
    t_lterms.finish()
    gram = b["lparts"][pl.ds(0, LROWS), :].astype(F32)
    for j in range(1, 8):
        gram += b["lparts"][pl.ds(j * LROWS, LROWS), :].astype(F32)
    new_sl[...] = beta * stat_l[...] + ((1.0 - beta) / FF) * gram
    b["pl_own"][...] = dot(new_sl[...].astype(BF), b["lall"][...])
    b["pl_b"][...] = b["pl_own"][...].astype(BF)
    g_pl = ShardGather(
        net, b["pl_b"].at[:, lanes(net.c)], b["pl_all"].at[:, lanes(net.c)], slots=g_grad.slots.again()
    )
    begin(g_pl)
    stores[3].start()
    b["half_all"][...] = dot_tn(b["lall"][...], gcols[...]).astype(BF)
    t_half = TensorGather(net, b["half_all"].at[own_left, :], b["half_rows"])
    t_stat.step2()
    begin(t_half)
    g_right.finish()
    t_stat.finish()
    b["p"][...] = dot(b["s_rows"][...], b["qcols"][...])
    b["p_b"][...] = b["p"][...].astype(BF)
    t_power = TensorGather(net, b["p_b"], b["p_rows"])
    begin(t_power)
    g_pl.step1()
    t_half.step1()
    t_power.step1()
    g_pl.step2()
    t_half.step2()
    t_power.step2()
    g_pl.step3()
    t_power.finish()

    def term(rel):
        zt = (net.z + rel) % 4
        v = dot_tn(b["p_rows"][:, pl.ds(pl.multiple_of(zt * D, 128), D)], b["p_b"][...]).astype(BF)
        b["part"][zt] = v.reshape(4, ROWS, COLS)

    scatter = plane_scatter(net, b["part"], b["a_b"], b["f1"], b["f2"], b["fq"], b["fg1"], b["fg2"])
    term(2)
    next(scatter)
    term(1)
    term(3)
    next(scatter)
    term(0)
    next(scatter)

    def squares(j, total):
        v = b["p_rows"][pl.ds(pl.multiple_of(j * 16, 16), 16), :].astype(F32)
        return total + jnp.sum(v * v, axis=0, keepdims=True)

    total = lax.fori_loop(0, ROWS // 16, squares, jnp.zeros((1, FF), F32))
    b["tile"][...] = jnp.broadcast_to(jnp.sum(total, keepdims=True), (8, 128))
    g_tile = ShardGather(net, b["tile"], b["tiles"], slots=g_left.slots.again())
    begin(g_tile)
    t_half.finish()
    rot = dot(b["half_rows"][...], b["qcols"][...])
    first = beta * m1[...] + (1.0 - beta) * rot
    second = beta * m2[...] + (1.0 - beta) * (rot * rot)
    new_m1[...] = first
    new_m2[...] = second
    stores[1].start()
    stores[2].start()
    b["dir_b"][...] = ((first / correction) / (jnp.sqrt(second / correction) + adam_eps)).astype(BF)
    next(scatter)
    g_pl.finish()
    pl_swap = swap(b["pl_all"])
    pl_swap.recv()

    def left_squares(j, total):
        v = b["pl_all"][pl.ds(pl.multiple_of(j * 16, 16), 16), :].astype(F32)
        return total + jnp.sum(v * v, axis=0, keepdims=True)

    def left_gram(ref, factor, lo, hi):
        for j in range(lo, hi):
            cut = pl.ds(j * 128, 128)
            b["gl"][cut, :] = (dot_tn(ref[:, cut], ref[...]) * factor).astype(BF)

    left_total = lax.fori_loop(0, D // 16, left_squares, jnp.zeros((1, D), F32))
    left_scale = math.sqrt(D) / (4.0 * jnp.sqrt(jnp.sum(left_total, keepdims=True)))
    left_gram(b["pl_all"], left_scale * left_scale, 0, 4)
    g_tile.step1()
    next(scatter)
    g_tile.step2()
    left_gram(b["pl_all"], left_scale * left_scale, 4, 5)
    next(scatter)
    g_tile.step3()
    left_gram(b["pl_all"], left_scale * left_scale, 5, 6)
    g_a = ShardGather(net, b["a_b"], b["a_cols"], slots=g_right.slots.again())
    next(scatter)
    g_a.start((0,))
    next(scatter)
    g_a.start((1,))
    g_a.local(lsem.at[locals_used[0]])
    locals_used[0] += 1
    for j in range(3):
        cut = pl.ds(j * 256, 256)
        v = b["pl_all"][cut, :]
        b["wl"][cut, :] = (left_scale * (1.5 * v.astype(F32) - 0.5 * dot(v, b["gl"][...]))).astype(BF)
    mine = left_scale * (1.5 * b["pl_own"][...] - 0.5 * dot(b["pl_b"][...], b["gl"][...]))
    g_a.step1()
    left_gram(b["wl"], 1.0, 0, 5)
    g_a.step2()
    left_gram(b["wl"], 1.0, 5, 6)
    new_bl[...] = math.sqrt(D) * (1.5 * mine - 0.5 * dot(mine.astype(BF), b["gl"][...]))
    stores[5].start()
    g_a.step3()
    g_dir = ShardGather(net, b["dir_b"], b["dir_cols"], slots=g_grad.slots.again())
    g_tile.finish()
    norm = jnp.sum(b["tiles"][...], keepdims=True) / 1024.0
    scale = math.sqrt(FF) / (4.0 * jnp.sqrt(norm))
    square = scale * scale
    g_a.finish()

    def mix(rows, factor, add, out, all_rows, before):
        v = dot(b[rows][...], b["a_cols"][...])
        b[out][...] = (factor * v + add * b["p"][...]).astype(BF)
        g = TensorGather(net, b[out], b[all_rows], slots=before.slots.again())
        begin(g)
        return g

    t_y = mix("p_rows", 0.0625 * square, -0.5625, "y1_b", "y1_rows", t_stat)
    begin(g_dir)
    t_y.step1()
    g_dir.step1()
    t_y.step2()
    g_dir.step2()
    t_y.finish()
    t_y = mix("y1_rows", square, 1.6875, "y2_b", "y2_rows", t_power)
    g_dir.step3()
    t_y.step1()
    g_dir.finish()
    back = dot(b["lq"][...], b["dir_cols"][...]).astype(BF)
    for j in range(8):
        b["upart"][j % 2, j // 2] = dot_nt(back, b["qcols"][pl.ds(j * COLS, COLS), :]).astype(BF)
    to_update = line_scatter(net, b["upart"], update, b["u0"], b["uq"], b["u1"], b["u2"])
    next(to_update)
    t_y.step2()
    t_y.finish()
    t_y = mix("y2_rows", square, -2.4375, "y3_b", "y3_rows", t_stat)
    next(to_update)
    t_y.step1()
    next(to_update)
    t_y.step2()
    t_y.finish()
    v = dot(b["y3_rows"][...], b["a_cols"][...])
    new_br[...] = (math.sqrt(FF) * scale) * (2.25 * b["p"][...] + square * v)
    stores[6].start()
    for _ in to_update:
        pass
    stores[0].start()
    assert net.taken <= SEMS and locals_used[0] <= 16
    cast.drain()
    net.drain()
    for store in stores:
        store.wait()


def emit(*refs):
    held, sem = refs[14:21], refs[21]
    into = [pltpu.make_async_copy(refs[k], held[k], sem.at[0, k]) for k in range(7)]
    onto = [pltpu.make_async_copy(held[k], refs[7 + k], sem.at[1, k]) for k in range(7)]
    for copy in into:
        copy.start()
    for copy, store in zip(into, onto):
        copy.wait()
        store.start()
    for store in onto:
        store.wait()


def local(gradient, moment_one, moment_two, stat_left, stat_right, basis_left, basis_right):
    args = (gradient, moment_one, moment_two, stat_left, stat_right, basis_left, basis_right)
    out = pl.pallas_call(
        kernel,
        out_shape=[jax.ShapeDtypeStruct(a.shape, a.dtype) for a in args],
        in_specs=[pl.BlockSpec(memory_space=pl.ANY)] * 7,
        out_specs=[pl.BlockSpec(memory_space=pl.ANY)] * 7,
        scratch_shapes=[pltpu.VMEM(shape, dtype) for shape, dtype in BUFFERS.values()]
        + [
            pltpu.SemaphoreType.DMA((POOL + 8,)),
            pltpu.SemaphoreType.DMA((SEMS,)),
            pltpu.SemaphoreType.DMA((30,)),
        ]
        + [pltpu.VMEM(a.shape, a.dtype) for a in args * 2],
        compiler_params=pltpu.CompilerParams(
            collective_id=0, has_side_effects=True, vmem_limit_bytes=63 * 2**20
        ),
        name="step",
    )(*args)
    hbm = pl.BlockSpec(memory_space=pl.ANY)
    return pl.pallas_call(
        emit,
        out_shape=[jax.ShapeDtypeStruct(a.shape, a.dtype) for a in args],
        in_specs=[hbm] * 7,
        out_specs=[hbm] * 7,
        scratch_shapes=[pltpu.VMEM(a.shape, a.dtype) for a in args] + [pltpu.SemaphoreType.DMA((2, 7))],
        compiler_params=pltpu.CompilerParams(vmem_limit_bytes=63 * 2**20),
        name="emit",
    )(*out)


def solution(mesh):
    both, row = P("shard", "tensor"), P("shard", None)
    return jax.shard_map(
        local,
        mesh=mesh,
        in_specs=(both, both, both, row, both, row, both),
        out_specs=(both, both, both, row, both, row, both),
        check_vma=False,
    )
```
